32 devices in a mesh: dp: 8 (over y, x, core), tensor: 4 (over z).
Axes of the slice: x: 2, y: 2, z: 4, core: 2. Of those that a mesh axis runs over, the one named last changes fastest.
Arguments:
- layer_in: bfloat16 [64, 128, 1024], P('dp', 'tensor'), may hold values from -6 to 6
- cotangent: bfloat16 [64, 128, 1024], P('dp', 'tensor'), may hold values from -8 to 8
- row_counts: int32 [16], replicated, may hold values from 1 to 8, 64 in all
- tail_tokens: int32 [16], replicated, may hold values from 1 to 128
- row_order: int32 [64], replicated, may hold values from 0 to 63, each once
- gain_one: bfloat16 [1024], P('dp'), may hold values from 0.099609375 to 1.8984375
- w_in: bfloat16 [1024, 3, 1024], P('dp', None, 'tensor'), may hold values from -0.1875 to 0.1875
- kernel: bfloat16 [3, 1024], P(None, 'dp'), may hold values from -3.5 to 3.5
- w_out: bfloat16 [1024, 1024], P('tensor', 'dp'), may hold values from -0.1875 to 0.1875
- gain_two: bfloat16 [1024], P('dp'), may hold values from 0.099609375 to 1.8984375
- w_gu: bfloat16 [1024, 2, 4608], P('dp', None, 'tensor'), may hold values from -0.1875 to 0.1875
- w_down: bfloat16 [4608, 1024], P('tensor', 'dp'), may hold values from -0.125 to 0.125
Outputs:
- layer_out: bfloat16 [64, 128, 1024], P('dp', 'tensor')
- grad_in: bfloat16 [64, 128, 1024], P('dp', 'tensor')
- grad_gain_one: float32 [1024], P('dp')
- grad_w_in: float32 [1024, 3, 1024], P('dp', None, 'tensor')
- grad_kernel: float32 [3, 1024], P(None, 'dp')
- grad_w_out: float32 [1024, 1024], P('tensor', 'dp')
- grad_gain_two: float32 [1024], P('dp')
- grad_w_gu: float32 [1024, 2, 4608], P('dp', None, 'tensor')
- grad_w_down: float32 [4608, 1024], P('tensor', 'dp')
The draws below stay inside these ranges and needn't reach their ends.
Inputs may be any that keep to these rules, and one draw needn't show every extreme that they name: row_counts sum to 64; the longest sequence has exactly 8 rows. `row_order`: each given-order row stands in exactly one dealt slot.
All inputs are finite; a program needn't handle non-finite values.
Results may differ from the reference program's by a relative error of at most 0.025.
Values may be sent and summed in bfloat16 or wider, within the bound.
No kernel may reach another device: no remote copies, remote signals or barrier semaphores. Data moves between devices by JAX's collectives and lax.ppermute only.
A program may use at most 128 MiB of HBM per device.

```python
import math
from functools import partial
import jax
import jax.numpy as jnp
import numpy as np
from jax import lax

D = 1024
FF = 4608
K = 3
ROW_LEN = 128
MAXROWS = 8
ROWS = 64
NSEQ = 16
N_TENSOR = 4


def place_ends(array, rng, low, top_value):
    longest = array.shape.index(max(array.shape))
    spots = []
    for shift in (0, 1):
        where = [jax.random.randint(jax.random.fold_in(rng, axis), (), 0, length) for axis, length in enumerate(array.shape)]
        where[longest] = (where[longest] + shift) % array.shape[longest]
        spots.append(tuple(where))
    return array.at[spots[0]].set(low).at[spots[1]].set(top_value)


def spiked(values, stream_key, source, target, parts, factor):
    owner, partner = [(jnp.arange(values.shape[position]) // (values.shape[position] // parts)).reshape([-1 if axis == position else 1 for axis in range(values.ndim)]) for position in (source, target)]
    chosen = jax.random.permutation(stream_key, parts)[partner]
    strong = (owner == chosen) | (owner == (partner + parts // 2) % parts)
    return jnp.where(strong, factor * values, values)


def shard_levels(own_key, shape, split, least, top_value):
    level, own = 1.0, jax.random.fold_in(own_key, 6)
    for axis_at, parts in split:
        heights = jnp.exp(jax.random.uniform(jax.random.fold_in(own, axis_at), (parts,), jnp.float32, least / len(split), top_value / len(split)))
        level = level * jnp.repeat(heights, shape[axis_at] // parts).reshape([-1 if axis == axis_at else 1 for axis in range(len(shape))])
    return level


def profile(count, total, limit, skew):
    loads = [(1 << 20) // math.isqrt(standing ** skew) + 1 for standing in range(2, count + 1)]
    rest, counts = total - limit - (count - 1), [1] * (count - 1)
    while rest > 0:
        movable = [i for i in range(count - 1) if counts[i] < limit]
        whole, budget = sum([loads[i] for i in movable]), rest
        for i in movable:
            extra = min(limit - counts[i], max(1, budget * loads[i] // whole), rest)
            counts[i] = counts[i] + extra
            rest = rest - extra
    return np.array([limit] + counts)


def ragged_sizes(rng, count, total, limit, skew):
    if count == 2:
        one = jax.random.randint(rng, (), max(1, total - limit), min(limit, total - 1) + 1)
        return jnp.stack([one, total - one])
    tallies = jnp.asarray(profile(count, total, limit, skew), jnp.int32)
    couples = (count - 1) // 2
    donor, taker = tallies[1:1 + 2 * couples:2], tallies[2:2 + 2 * couples:2]
    slack = jnp.minimum(donor - 1, limit - taker)
    moved = jax.random.randint(jax.random.fold_in(rng, 1), (couples,), 0, 1 << 20) % (slack + 1)
    tallies = tallies.at[1:1 + 2 * couples:2].set(donor - moved).at[2:2 + 2 * couples:2].set(taker + moved)
    return tallies[jax.random.permutation(jax.random.fold_in(rng, 2), count)]


def normal_values(own_key, shape, scale, limit, split=(), held_as=jnp.bfloat16):
    values = jax.random.normal(own_key, shape, jnp.float32) * scale
    if len(split) > 0:
        values = shard_levels(own_key, shape, split, -0.22, 0.18) * values
    return jnp.clip(values, min=-limit, max=limit).astype(held_as)


def heavy_noise(rng, shape, scale, limit, shards, heavy, held_as=jnp.bfloat16):
    values = scale * jax.random.normal(rng, shape, jnp.float32)
    if shards:
        values = values * shard_levels(rng, shape, shards, -0.22, 0.18)
    return jnp.clip(spiked(values, jax.random.fold_in(rng, 3), *heavy), -limit, limit).astype(held_as)


def setup_inputs(seed: int = 0) -> dict:
    streams_of = jax.random.split(jax.random.key(seed), 13)
    return {
        "layer_in": normal_values(streams_of[0], (ROWS, ROW_LEN, D), 1.0, 6.0, ((0, 8), (1, 4))),
        "cotangent": heavy_noise(streams_of[1], (ROWS, ROW_LEN, D), 1.0, 8.0, ((0, 8), (1, 4)), (0, 2, 8, 2.0)),
        "row_counts": ragged_sizes(streams_of[2], NSEQ, ROWS, MAXROWS, 1).astype(jnp.int32),
        "tail_tokens": place_ends(jax.random.randint(streams_of[3], (NSEQ,), 1, ROW_LEN + 1), jax.random.fold_in(streams_of[3], 1), 1, ROW_LEN).astype(jnp.int32),
        "row_order": jax.random.permutation(streams_of[4], ROWS).astype(jnp.int32),
        "gain_one": jnp.clip(1.0 + 0.18 * jax.random.normal(streams_of[5], (D,), jnp.float32), 0.099609375, 1.8984375).astype(jnp.bfloat16),
        "w_in": normal_values(streams_of[6], (D, 3, D), D ** -0.5, 0.1875, ((0, 8), (2, 4))),
        "kernel": normal_values(streams_of[7], (K, D), K ** -0.5, 3.5, ((1, 8),)),
        "w_out": normal_values(streams_of[8], (D, D), D ** -0.5, 0.1875, ((0, 4), (1, 8))),
        "gain_two": jnp.clip(1.0 + 0.18 * jax.random.normal(streams_of[9], (D,), jnp.float32), 0.099609375, 1.8984375).astype(jnp.bfloat16),
        "w_gu": normal_values(streams_of[10], (D, 2, FF), D ** -0.5, 0.1875, ((0, 8), (2, 4))),
        "w_down": normal_values(streams_of[11], (FF, D), (FF // 2) ** -0.5, 0.125, ((0, 4), (1, 8))),
    }


EPS = 1e-05
HIGH = lax.Precision.HIGHEST

@jax.custom_vjp
def low(v):
    return lax.optimization_barrier(v.astype(jnp.bfloat16)).astype(jnp.float32)

@jax.custom_vjp
def low_back(v):
    return v

def low_keep(v):
    return (low(v), None)

def low_pass(kept, grad):
    return (grad,)

def back_keep(v):
    return (v, None)

def back_low(kept, grad):
    return (low(grad),)
low.defvjp(low_keep, low_pass)
low_back.defvjp(back_keep, back_low)

def rms_norm(value, gain):
    return value * lax.rsqrt(lax.optimization_barrier(jnp.mean(value * value, axis=-1, keepdims=True)) + EPS) * gain

def group_copies(value, groups):
    shape = value.shape
    return low_back(jnp.broadcast_to(value[:, :, None, :], (shape[0], shape[1], groups, shape[2])))

def block_step(weights, carry, block):
    gain_one, w_in, kernel, w_out, gain_two, w_gu, w_down = weights
    tokens, starting = block
    groups = N_TENSOR
    reach = kernel.shape[0] - 1
    rows = tokens.shape[0]
    length = tokens.shape[1]
    width = tokens.shape[2]
    hidden_width = w_down.shape[0]
    normed_one = low(rms_norm(tokens, gain_one))
    copies_one = group_copies(normed_one, groups)
    w_in_groups = w_in.reshape(width, 3, groups, width // groups)
    projected = low_back(jnp.einsum('rtgd,dkgc->rtkgc', copies_one, w_in_groups, precision=HIGH)).reshape(rows, length, 3, width)
    mixed = low(projected[:, :, 0] * projected[:, :, 2])
    earlier = jnp.concatenate([carry[None], mixed[:-1, length - reach:]], axis=0)
    earlier = earlier * (1.0 - starting)[:, None, None]
    padded = jnp.concatenate([earlier, mixed], axis=1)
    conv_out = jnp.zeros_like(mixed)
    for offset in range(reach + 1):
        conv_out = conv_out + kernel[offset] * padded[:, offset:offset + length]
    gated = low(projected[:, :, 1] * conv_out)
    gated_groups = gated.reshape(rows, length, groups, width // groups)
    mixer_parts = low(jnp.einsum('rtgc,gce->rtge', gated_groups, w_out.reshape(groups, width // groups, width), precision=HIGH))
    middle = tokens + low_back(lax.optimization_barrier(jnp.sum(mixer_parts, axis=2)))
    normed_two = low(rms_norm(middle, gain_two))
    copies_two = group_copies(normed_two, groups)
    w_gu_groups = w_gu.reshape(width, 2, groups, hidden_width // groups)
    gate_up = low_back(jnp.einsum('rtgd,dkgf->rtkgf', copies_two, w_gu_groups, precision=HIGH)).reshape(rows, length, 2, hidden_width)
    hidden = low(jax.nn.silu(gate_up[:, :, 0]) * gate_up[:, :, 1])
    hidden_groups = hidden.reshape(rows, length, groups, hidden_width // groups)
    ffn_parts = low(jnp.einsum('rtgf,gfe->rtge', hidden_groups, w_down.reshape(groups, hidden_width // groups, width), precision=HIGH))
    result = middle + low_back(lax.optimization_barrier(jnp.sum(ffn_parts, axis=2)))
    return (mixed[-1, length - reach:], result)

def reference(layer_in, cotangent, row_counts, tail_tokens, row_order, gain_one, w_in, kernel, w_out, gain_two, w_gu, w_down):
    starts = (jnp.cumsum(row_counts) - row_counts).astype(jnp.int32)
    ends = (starts + row_counts - 1).astype(jnp.int32)
    starting = jnp.zeros((ROWS,), jnp.float32).at[starts].set(1.0)
    opening = jnp.zeros((ROWS,), jnp.int32).at[starts].set(1)
    closing = jnp.zeros((ROWS,), jnp.int32).at[ends].set(1)
    sequence = (jnp.cumsum(opening) - 1).astype(jnp.int32)
    row_valid = jnp.where(closing == 1, tail_tokens[sequence], ROW_LEN)
    valid = (jnp.arange(ROW_LEN, dtype=jnp.int32)[None, :] < row_valid[:, None]).astype(jnp.float32)
    ordered_in = jnp.zeros((ROWS, ROW_LEN, D), jnp.float32).at[row_order].set(layer_in.astype(jnp.float32))
    ordered_cot = jnp.zeros((ROWS, ROW_LEN, D), jnp.float32).at[row_order].set(cotangent.astype(jnp.float32))
    ordered_cot = ordered_cot * valid[:, :, None]
    weights = tuple((weight_arg.astype(jnp.float32) for weight_arg in (gain_one, w_in, kernel, w_out, gain_two, w_gu, w_down)))
    group_rows = 16

    def forward(tokens, params):
        blocks = tokens.reshape(ROWS // group_rows, group_rows, ROW_LEN, D)
        flags = starting.reshape(ROWS // group_rows, group_rows)
        stepper = jax.checkpoint(partial(block_step, params))
        initial = jnp.zeros((K - 1, D), jnp.float32)
        unused, outputs = lax.scan(stepper, initial, (blocks, flags))
        return outputs.reshape(ROWS, ROW_LEN, D)
    result, pull = jax.vjp(forward, ordered_in, weights)
    d_tokens, d_params = pull(ordered_cot)
    layer_out = result[row_order].astype(jnp.bfloat16)
    grad_in = d_tokens[row_order].astype(jnp.bfloat16)
    return (layer_out, grad_in, d_params[0], d_params[1], d_params[2], d_params[3], d_params[4], d_params[5], d_params[6])
```

```python
import functools
import jax
import jax.numpy as jnp
from jax import lax
from jax.experimental import pallas as pl
from jax.experimental.pallas import tpu as pltpu
from jax.sharding import PartitionSpec as P

EPS = 1e-05
INNER = 8
BF = jnp.bfloat16
F32 = jnp.float32


def dp_swap(value, step):
    size = lax.axis_size("dp")
    hop = step * (size // INNER)
    return lax.ppermute(value, "dp", [(i, i ^ hop) for i in range(size)])


def z_shift(value, step):
    size = lax.axis_size("tensor")
    return lax.ppermute(value, "tensor", [(i, (i + step) % size) for i in range(size)])


def outer_groups():
    outer = lax.axis_size("dp") // INNER
    return [[i * outer + o for o in range(outer)] for i in range(INNER)]


def mm(a, b):
    return lax.dot_general(a, b, (((1,), (0,)), ((), ())), preferred_element_type=F32)


def mm_nt(a, b):
    return lax.dot_general(a, b, (((1,), (1,)), ((), ())), preferred_element_type=F32)


def mm_tn(a, b):
    return lax.dot_general(a, b, (((0,), (0,)), ((), ())), preferred_element_type=F32)


def plane_gather(local):
    own = [local] + [dp_swap(local, 2 * kq) for kq in (1, 2, 3)]
    other = [dp_swap(piece, 1) for piece in own]
    return [piece for pair in zip(own, other) for piece in pair]


def place_mixer_kernel(idx_ref, *refs):
    pieces, outs, small_ref = refs[:8], refs[8:12], refs[12]
    held, in_sems, out_sems, small_sems = refs[13:]
    me, z = idx_ref[0], idx_ref[1]
    n_z = outs[0].shape[1] // 256
    rows = outs[0].shape[0] // 8
    loads = [pltpu.make_async_copy(pieces[k], held.at[k], in_sems.at[k]) for k in range(8)]
    for load in loads:
        load.start()
    stores = []
    for k in range(8):
        loads[k].wait()
        at = jnp.bitwise_xor(me, k)
        for s in range(n_z):
            col = lax.rem(z + n_z - s, n_z) * 256
            for st in range(4):
                store = pltpu.make_async_copy(
                    held.at[k, pl.ds((s * 4 + st) * rows, rows)],
                    outs[st].at[
                        pl.ds(pl.multiple_of(at * rows, rows), rows),
                        pl.ds(pl.multiple_of(col, 256), 256),
                    ],
                    out_sems.at[k, s * 4 + st],
                )
                store.start()
                stores.append(store)
        store = pltpu.make_async_copy(
            held.at[k, pl.ds(n_z * 4 * rows, 16)], small_ref.at[at], small_sems.at[k]
        )
        store.start()
        stores.append(store)
    for store in stores:
        store.wait()


def place_mixer(index, pieces, n_z):
    width = n_z * 256
    depth = (pieces[0].shape[0] - 16) // (4 * n_z) * 8
    hbm = pl.BlockSpec(memory_space=pl.ANY)
    return pl.pallas_call(
        place_mixer_kernel,
        out_shape=[jax.ShapeDtypeStruct((depth, width), BF)] * 4
        + [jax.ShapeDtypeStruct((8, 16, 256), BF)],
        in_specs=[pl.BlockSpec(memory_space=pltpu.SMEM)] + [hbm] * 8,
        out_specs=[hbm] * 5,
        scratch_shapes=[
            pltpu.VMEM((8,) + pieces[0].shape, BF),
            pltpu.SemaphoreType.DMA((8,)),
            pltpu.SemaphoreType.DMA((8, 4 * n_z)),
            pltpu.SemaphoreType.DMA((8,)),
        ],
        cost_estimate=pl.CostEstimate(flops=0, bytes_accessed=17_000_000, transcendentals=0),
        name="place_mixer",
    )(index, *pieces)


def place_ffn_kernel(idx_ref, *refs):
    pieces, outs = refs[:8], refs[8:11]
    held, in_sems, out_sems = refs[11:]
    me = idx_ref[0]
    rows = outs[0].shape[0] // 8
    loads = [pltpu.make_async_copy(pieces[k], held.at[k], in_sems.at[k]) for k in range(8)]
    for load in loads:
        load.start()
    stores = []
    for k in range(8):
        loads[k].wait()
        at = jnp.bitwise_xor(me, k)
        for st in range(3):
            store = pltpu.make_async_copy(
                held.at[k, st],
                outs[st].at[pl.ds(pl.multiple_of(at * rows, rows), rows)],
                out_sems.at[k, st],
            )
            store.start()
            stores.append(store)
    for store in stores:
        store.wait()


def place_ffn(index, pieces):
    _, rows, hidden = pieces[0].shape
    hbm = pl.BlockSpec(memory_space=pl.ANY)
    return pl.pallas_call(
        place_ffn_kernel,
        out_shape=[jax.ShapeDtypeStruct((8 * rows, hidden), BF)] * 3,
        in_specs=[pl.BlockSpec(memory_space=pltpu.SMEM)] + [hbm] * 8,
        out_specs=[hbm] * 3,
        scratch_shapes=[
            pltpu.VMEM((8,) + pieces[0].shape, BF),
            pltpu.SemaphoreType.DMA((8,)),
            pltpu.SemaphoreType.DMA((8, 3)),
        ],
        cost_estimate=pl.CostEstimate(flops=0, bytes_accessed=14_000_000, transcendentals=0),
        name="place_ffn",
    )(index, *pieces)


def ffn_kernel(n_ref, d_ref, wg_ref, wu_ref, wd_ref, dn_ref, part_ref, hid_ref, dg_ref, du_ref, acc_n, acc_p):
    j = pl.program_id(0)
    normed, d_out = n_ref[...], d_ref[...]
    wg, wu, wd = wg_ref[...], wu_ref[...], wd_ref[...]
    gate, up = mm(normed, wg), mm(normed, wu)
    sig = jax.nn.sigmoid(gate)
    silu = gate * sig
    hidden = (silu * up).astype(BF)
    d_hidden = mm(d_out, wd)
    d_gate = (d_hidden * up * (sig * (1.0 + gate * (1.0 - sig)))).astype(BF)
    d_up = (d_hidden * silu).astype(BF)
    hid_ref[...] = hidden
    dg_ref[...] = d_gate
    du_ref[...] = d_up
    d_normed = mm_nt(d_gate, wg) + mm_nt(d_up, wu)
    part = mm_nt(hidden, wd)

    @pl.when(j == 0)
    def _():
        acc_n[...] = d_normed
        acc_p[...] = part

    @pl.when(j > 0)
    def _():
        acc_n[...] += d_normed
        acc_p[...] += part

    @pl.when(j == pl.num_programs(0) - 1)
    def _():
        dn_ref[...] = acc_n[...].astype(BF)
        part_ref[...] = acc_p[...].astype(BF)


def ffn_piece(normed, d_out, wg, wu, wd):
    tokens, width = normed.shape
    hidden = wg.shape[1]
    block = 384 if hidden % 384 == 0 else 128
    whole = pl.BlockSpec((tokens, width), lambda j: (0, 0))
    weight = pl.BlockSpec((width, block), lambda j: (0, j))
    act = pl.BlockSpec((tokens, block), lambda j: (0, j))
    return pl.pallas_call(
        ffn_kernel,
        grid=(hidden // block,),
        out_shape=[jax.ShapeDtypeStruct((tokens, width), BF)] * 2
        + [jax.ShapeDtypeStruct((tokens, hidden), BF)] * 3,
        in_specs=[whole, whole, weight, weight, weight],
        out_specs=[whole, whole, act, act, act],
        scratch_shapes=[pltpu.VMEM((tokens, width), F32)] * 2,
        cost_estimate=pl.CostEstimate(
            flops=12 * tokens * width * hidden,
            bytes_accessed=6 * width * hidden + 8 * tokens * width + 6 * tokens * hidden,
            transcendentals=tokens * hidden,
        ),
        name="ffn_piece",
    )(normed, d_out, wg, wu, wd)


def norm_scale(value):
    return lax.rsqrt(jnp.mean(value * value, axis=-1, keepdims=True) + EPS)


def norm_back(d_normed, value, scale, gain):
    weighted = d_normed * gain
    d_value = scale * weighted - value * (scale * scale * scale) * jnp.mean(
        weighted * value, axis=-1, keepdims=True
    )
    return d_value, jnp.sum(d_normed * value * scale, axis=0)


def plane_reduce(blocks, me_in):
    size = blocks.shape[0] // 8
    tail = blocks.shape[1:]
    view = blocks.reshape((4, 2, size) + tail)
    core = lax.rem(me_in, 2)
    quad = me_in // 2
    away = lax.dynamic_index_in_dim(view, 1 - core, 1, keepdims=False)
    home = lax.dynamic_index_in_dim(view, core, 1, keepdims=False)
    half = (home.astype(F32) + dp_swap(away, 1).astype(F32)).astype(BF)
    total = lax.dynamic_index_in_dim(half, quad, 0, keepdims=False).astype(F32)
    for kq in (1, 2, 3):
        piece = lax.dynamic_index_in_dim(half, jnp.bitwise_xor(quad, kq), 0, keepdims=False)
        total = total + dp_swap(piece, 2 * kq).astype(F32)
    return total


def body(
    layer_in,
    cotangent,
    row_counts,
    tail_tokens,
    row_order,
    gain_one,
    w_in,
    kernel,
    w_out,
    gain_two,
    w_gu,
    w_down,
):
    row_count, own_len, width = layer_in.shape
    n_dp, n_z = lax.axis_size("dp"), lax.axis_size("tensor")
    outer = n_dp // INNER
    me, z = lax.axis_index("dp"), lax.axis_index("tensor")
    me_in = me // outer
    row_len = own_len * n_z
    channels = w_in.shape[2]
    reach = kernel.shape[0] - 1
    tokens = row_count * own_len
    block = width // INNER
    index = jnp.stack([me_in, z]).astype(jnp.int32)

    given = lax.dynamic_slice_in_dim(row_order, me * row_count, row_count)
    starts = jnp.cumsum(row_counts) - row_counts
    ends = starts + row_counts - 1
    is_first = jnp.any(starts[None, :] == given[:, None], axis=1)
    at_end = ends[None, :] == given[:, None]
    row_valid = jnp.where(
        jnp.any(at_end, axis=1),
        jnp.sum(jnp.where(at_end, tail_tokens[None, :], 0), axis=1),
        row_len,
    )
    positions = z * own_len + jnp.arange(own_len, dtype=jnp.int32)
    valid = (positions[None, :] < row_valid[:, None]).astype(F32)

    small = jnp.concatenate([gain_one[None], gain_two[None], kernel], axis=0)
    w_in_t = w_in.transpose(1, 0, 2)
    w_out_t = w_out.T[None]
    mixer_own = jnp.concatenate([w_in_t, w_out_t], axis=0)
    ffn_own = jnp.concatenate([w_gu.transpose(1, 0, 2), w_down.T[None]], axis=0)
    if outer > 1:
        groups = outer_groups()
        mixer_own = lax.all_gather(mixer_own, "dp", axis=1, tiled=True, axis_index_groups=groups)
        ffn_own = lax.all_gather(ffn_own, "dp", axis=1, tiled=True, axis_index_groups=groups)
        small = lax.all_gather(small, "dp", axis=1, tiled=True, axis_index_groups=groups)
    n_small = small.shape[0]
    small_rows = jnp.pad(small, ((0, 16 - n_small), (0, 256 - block)))
    mixer_rows = mixer_own.reshape(4 * block, channels)
    shifted = [mixer_rows] + [z_shift(mixer_rows, s) for s in range(1, n_z)]
    mixer_pieces = plane_gather(jnp.concatenate(shifted + [small_rows], axis=0))
    w_b, w_c, w_u, w_o, small_all = place_mixer(index, mixer_pieces, n_z)
    ffn_pieces = plane_gather(ffn_own)
    w_g, w_p, w_d = place_ffn(index, ffn_pieces)
    small_full = small_all[:, :n_small, :block].transpose(1, 0, 2).reshape(n_small, width).astype(F32)
    gain_one_all, gain_two_all, taps = small_full[0], small_full[1], small_full[2:]

    tails = layer_in[:, own_len - reach :]
    before = z_shift(tails, 1)
    spread_in = before[None]
    if outer > 1:
        spread_in = lax.all_gather(before, "dp", axis=0, axis_index_groups=groups)
    every = spread_in[None]
    for step in (1, 2, 4):
        every = jnp.concatenate([every, dp_swap(every, step)], axis=0)
    slots = INNER * outer * row_count
    rel = jnp.bitwise_xor(me_in, jnp.arange(INNER, dtype=jnp.int32))
    slot_rows = row_order.reshape(INNER, outer * row_count)[rel].reshape(slots)
    before_mask = jnp.logical_and(
        slot_rows[None, :] == (given - 1)[:, None], jnp.logical_not(is_first)[:, None]
    )
    before_mask = jnp.logical_and(before_mask, z == 0).astype(BF)
    crossed = mm(before_mask, every.reshape(slots, reach * width)).reshape(row_count, reach, width)
    x_halo = jnp.where(z == 0, crossed, before.astype(F32)).reshape(row_count * reach, width)

    d_result = (cotangent.astype(F32) * valid[:, :, None]).reshape(tokens, width)
    d_ffn = d_result.astype(BF)
    d_ffn_set = [d_ffn] + [z_shift(d_ffn, s) for s in range(1, n_z)]

    x_own = layer_in.reshape(tokens, width).astype(F32)
    scale_one = norm_scale(x_own)
    n_one = (x_own * scale_one * gain_one_all).astype(BF)
    scale_halo = norm_scale(x_halo)
    n_halo = (x_halo * scale_halo * gain_one_all).astype(BF)
    total_ch = channels * n_z
    b_own, c_own, u_own = mm(n_one, w_b), mm(n_one, w_c), mm(n_one, w_u)
    b_halo, u_halo = mm(n_halo, w_b), mm(n_halo, w_u)
    mixed = (b_own * u_own).astype(BF).astype(F32).reshape(row_count, own_len, total_ch)
    mixed_halo = (b_halo * u_halo).astype(BF).astype(F32).reshape(row_count, reach, total_ch)
    padded = jnp.concatenate([mixed_halo, mixed], axis=1)
    conv = jnp.zeros((row_count, own_len, total_ch), F32)
    for k in range(reach + 1):
        conv = conv + taps[k] * padded[:, k : k + own_len]
    conv_flat = conv.reshape(tokens, total_ch)
    gated = (c_own * conv_flat).astype(BF)
    middle = x_own + mm_nt(gated, w_o)
    scale_two = norm_scale(middle)
    n_two = (middle * scale_two * gain_two_all).astype(BF)

    n_two_set = [n_two] + [z_shift(n_two, s) for s in range(1, n_z)]
    runs = [ffn_piece(n_two_set[s], d_ffn_set[s], w_g, w_p, w_d) for s in range(n_z)]
    d_normed_two = runs[0][0].astype(F32)
    for s in range(1, n_z):
        d_normed_two = d_normed_two + z_shift(runs[s][0], n_z - s).astype(F32)
    ffn_sum = runs[0][1].astype(F32)
    for s in range(1, n_z):
        ffn_sum = ffn_sum + z_shift(runs[s][1], n_z - s).astype(F32)
    layer_out = (middle + ffn_sum).astype(BF).reshape(row_count, own_len, width)

    n_two_cat = jnp.concatenate(n_two_set, axis=0)
    d_ffn_cat = jnp.concatenate(d_ffn_set, axis=0)
    hid_cat, dg_cat, du_cat = (jnp.concatenate([run[i] for run in runs], axis=0) for i in (2, 3, 4))
    hidden_units = hid_cat.shape[1]
    ffn_grads = jnp.stack(
        [
            mm_tn(n_two_cat, dg_cat).astype(BF).reshape(INNER, block, hidden_units),
            mm_tn(n_two_cat, du_cat).astype(BF).reshape(INNER, block, hidden_units),
            mm_tn(d_ffn_cat, hid_cat).astype(BF).reshape(INNER, block, hidden_units),
        ],
        axis=1,
    )
    ffn_total = plane_reduce(ffn_grads, me_in)[0]

    d_mid_norm, g_two = norm_back(d_normed_two, middle, scale_two, gain_two_all)
    d_middle = d_result + d_mid_norm
    d_mix = d_middle.astype(BF)
    d_gated = mm(d_mix, w_o)
    d_c = (d_gated * conv_flat).astype(BF)
    d_conv = (d_gated * c_own).reshape(row_count, own_len, total_ch)
    d_padded = jnp.zeros((row_count, own_len + reach, total_ch), F32)
    tap_grads = []
    for k in range(reach + 1):
        d_padded = d_padded + jnp.pad(taps[k] * d_conv, ((0, 0), (k, reach - k), (0, 0)))
        tap_grads.append(jnp.sum(d_conv * padded[:, k : k + own_len], axis=(0, 1)))
    d_mixed = d_padded[:, reach:].reshape(tokens, total_ch)
    d_mixed_halo = d_padded[:, :reach].reshape(row_count * reach, total_ch)
    d_b, d_u = (d_mixed * u_own).astype(BF), (d_mixed * b_own).astype(BF)
    d_b_halo, d_u_halo = (d_mixed_halo * u_halo).astype(BF), (d_mixed_halo * b_halo).astype(BF)
    d_n_one = mm_nt(d_b, w_b) + mm_nt(d_c, w_c) + mm_nt(d_u, w_u)
    d_n_halo = mm_nt(d_b_halo, w_b) + mm_nt(d_u_halo, w_u)
    d_x, g_one = norm_back(d_n_one, x_own, scale_one, gain_one_all)
    d_x_halo, g_one_halo = norm_back(d_n_halo, x_halo, scale_halo, gain_one_all)

    mixer_grads = jnp.stack(
        [
            (mm_tn(n_one, d_b) + mm_tn(n_halo, d_b_halo)).astype(BF),
            mm_tn(n_one, d_c).astype(BF),
            (mm_tn(n_one, d_u) + mm_tn(n_halo, d_u_halo)).astype(BF),
            mm_tn(d_mix, gated).astype(BF),
        ],
        axis=0,
    )
    mixer_grads = mixer_grads.reshape(4, INNER, block, n_z, channels).transpose(1, 3, 0, 2, 4)
    mixer_grads = mixer_grads.reshape(INNER, n_z, 4 * block, channels)
    small_grads = jnp.stack([g_one + g_one_halo, g_two] + tap_grads, axis=0)
    small_grads = small_grads.reshape(n_small, INNER, block).transpose(1, 0, 2).astype(BF)
    small_grads = jnp.pad(small_grads, ((0, 0), (0, 16 - n_small), (0, channels - block)))
    small_grads = jnp.broadcast_to(small_grads[:, None], (INNER, n_z, 16, channels))
    mixer_sum = plane_reduce(jnp.concatenate([mixer_grads, small_grads], axis=2), me_in)[0].astype(BF)
    mixer_total = lax.dynamic_index_in_dim(mixer_sum, z, 0, keepdims=False).astype(F32)
    for s in range(1, n_z):
        piece = lax.dynamic_index_in_dim(mixer_sum, lax.rem(z + s, n_z), 0, keepdims=False)
        mixer_total = mixer_total + z_shift(piece, s).astype(F32)

    back = d_x_halo.reshape(row_count, reach * width).astype(BF)
    spread = lax.dot_general(before_mask, back, (((0,), (0,)), ((), ())), preferred_element_type=F32)
    spread = spread.reshape(INNER, outer * row_count, reach * width)
    for step in (4, 2, 1):
        spread = spread[:step] + dp_swap(spread[step:].astype(BF), step).astype(F32)
    returned = spread[0]
    if outer > 1:
        returned = lax.psum_scatter(
            returned, "dp", scatter_dimension=0, tiled=True, axis_index_groups=groups
        )
    returned = jnp.where(z == 0, returned.astype(BF), back)
    returned = z_shift(returned, n_z - 1).astype(F32).reshape(row_count, reach, width)
    grad_in = (d_x + d_middle).reshape(row_count, own_len, width)
    grad_in = grad_in + jnp.pad(returned, ((0, 0), (own_len - reach, 0), (0, 0)))

    main = mixer_total[: 4 * block].reshape(4, block, channels)
    small_total = mixer_total[4 * block : 4 * block + n_small, :block]
    if outer > 1:
        main = lax.psum_scatter(main, "dp", scatter_dimension=1, tiled=True, axis_index_groups=groups)
        small_total = lax.psum_scatter(
            small_total, "dp", scatter_dimension=1, tiled=True, axis_index_groups=groups
        )
        ffn_total = lax.psum_scatter(
            ffn_total, "dp", scatter_dimension=1, tiled=True, axis_index_groups=groups
        )
    return (
        layer_out,
        grad_in.astype(BF),
        small_total[0],
        main[:3].transpose(1, 0, 2),
        small_total[2:],
        main[3].T,
        small_total[1],
        ffn_total[:2].transpose(1, 0, 2),
        ffn_total[2].T,
    )


def solution(mesh):
    in_specs = (
        P("dp", "tensor", None),
        P("dp", "tensor", None),
        P(),
        P(),
        P(),
        P("dp"),
        P("dp", None, "tensor"),
        P(None, "dp"),
        P("tensor", "dp"),
        P("dp"),
        P("dp", None, "tensor"),
        P("tensor", "dp"),
    )
    out_specs = (
        P("dp", "tensor", None),
        P("dp", "tensor", None),
        P("dp"),
        P("dp", None, "tensor"),
        P(None, "dp"),
        P("tensor", "dp"),
        P("dp"),
        P("dp", None, "tensor"),
        P("tensor", "dp"),
    )
    return jax.shard_map(body, mesh=mesh, in_specs=in_specs, out_specs=out_specs, check_vma=False)
```

```python
import functools
import jax
import jax.numpy as jnp
from jax import lax
from jax.experimental import pallas as pl
from jax.experimental.pallas import tpu as pltpu
from jax.sharding import PartitionSpec as P

EPS = 1e-05
INNER = 8
BF = jnp.bfloat16
F32 = jnp.float32
VMEM_LIMIT = 26 << 20


def dp_swap(value, step):
    size = lax.axis_size("dp")
    hop = step * (size // INNER)
    return lax.ppermute(value, "dp", [(i, i ^ hop) for i in range(size)])


def z_shift(value, step):
    size = lax.axis_size("tensor")
    return lax.ppermute(value, "tensor", [(i, (i + step) % size) for i in range(size)])


def after(value, *events):
    return lax.optimization_barrier((value,) + events)[0]


def mm(a, b):
    return lax.dot_general(a, b, (((1,), (0,)), ((), ())), preferred_element_type=F32)


def mm_nt(a, b):
    return lax.dot_general(a, b, (((1,), (1,)), ((), ())), preferred_element_type=F32)


def mm_tn(a, b):
    return lax.dot_general(a, b, (((0,), (0,)), ((), ())), preferred_element_type=F32)


def shape(*dims, dtype=BF):
    return jax.ShapeDtypeStruct(dims, dtype)


def whole_call(kernel, name, outs, args, scalars=0, hbm=0, scratch=(), flops=0, extra=0):
    specs = [pl.BlockSpec(memory_space=pltpu.SMEM)] * scalars
    specs += [pl.BlockSpec(memory_space=pl.ANY)] * hbm
    specs += [pl.BlockSpec(memory_space=pltpu.VMEM)] * (len(args) - scalars - hbm)
    moved = sum(a.size * a.dtype.itemsize for a in args) + sum(
        o.size * jnp.dtype(o.dtype).itemsize for o in outs
    )
    return pl.pallas_call(
        kernel,
        out_shape=outs,
        in_specs=specs,
        out_specs=[pl.BlockSpec(memory_space=pltpu.VMEM)] * len(outs),
        scratch_shapes=list(scratch),
        compiler_params=pltpu.CompilerParams(vmem_limit_bytes=VMEM_LIMIT),
        cost_estimate=pl.CostEstimate(flops=flops, bytes_accessed=moved, transcendentals=extra),
        name=name,
    )(*args)


def pair_up(own, other):
    return [piece for pair in zip(own, other) for piece in pair]


def plane_gather(local):
    own = [local] + [dp_swap(local, 2 * kq) for kq in (1, 2, 3)]
    return pair_up(own, [dp_swap(piece, 1) for piece in own])


def place_mixer_kernel(with_small, idx_ref, *refs):
    pieces, outs, sems = refs[:8], refs[8:-1], refs[-1]
    me, z = idx_ref[0], idx_ref[1]
    n_z = outs[0].shape[1] // 256
    rows = outs[0].shape[0] // 8
    copies = []
    for k in range(8):
        at = pl.multiple_of(jnp.bitwise_xor(me, k) * rows, rows)
        for s in range(n_z):
            col = pl.multiple_of(lax.rem(z + n_z - s, n_z) * 256, 256)
            for st in range(2):
                copies.append(
                    pltpu.make_async_copy(
                        pieces[k].at[pl.ds((s * 2 + st) * rows, rows)],
                        outs[st].at[pl.ds(at, rows), pl.ds(col, 256)],
                        sems.at[k, s * 2 + st],
                    )
                )
        if with_small:
            copies.append(
                pltpu.make_async_copy(
                    pieces[k].at[pl.ds(2 * n_z * rows, 16), pl.ds(0, rows)],
                    outs[2].at[:, pl.ds(at, rows)],
                    sems.at[k, 2 * n_z],
                )
            )
    for copy in copies:
        copy.start()
    for copy in copies:
        copy.wait()


def place_mixer(index, pieces, width, n_z, with_small):
    outs = [shape(width, n_z * 256)] * 2 + ([shape(16, width)] if with_small else [])
    return whole_call(
        functools.partial(place_mixer_kernel, with_small),
        "place_small" if with_small else "place_mixer",
        outs,
        (index, *pieces),
        scalars=1,
        hbm=8,
        scratch=[pltpu.SemaphoreType.DMA((8, 2 * n_z + 1))],
    )


def place_ffn_kernel(idx_ref, *refs):
    pieces, (gu_ref, down_ref), sems = refs[:8], refs[8:10], refs[10]
    me = idx_ref[0]
    rows = gu_ref.shape[0] // 8
    split = gu_ref.shape[1]
    copies = []
    for k in range(8):
        at = pl.ds(pl.multiple_of(jnp.bitwise_xor(me, k) * rows, rows), rows)
        copies.append(
            pltpu.make_async_copy(pieces[k].at[:, pl.ds(0, split)], gu_ref.at[at], sems.at[k, 0])
        )
        copies.append(
            pltpu.make_async_copy(
                pieces[k].at[:, pl.ds(split, split // 2)], down_ref.at[at], sems.at[k, 1]
            )
        )
    for copy in copies:
        copy.start()
    for copy in copies:
        copy.wait()


def place_ffn(index, pieces):
    rows, columns = pieces[0].shape
    return whole_call(
        place_ffn_kernel,
        "place_ffn",
        [shape(8 * rows, columns // 3 * 2), shape(8 * rows, columns // 3)],
        (index, *pieces),
        scalars=1,
        hbm=8,
        scratch=[pltpu.SemaphoreType.DMA((8, 2))],
    )


def ffn_kernel(n_ref, d_ref, gu_ref, down_ref, dn_ref, part_ref, hid_ref, dgu_ref):
    units = down_ref.shape[1]
    both = mm(n_ref[...], gu_ref[...])
    gate, up = both[:, :units], both[:, units:]
    sig = jax.nn.sigmoid(gate)
    silu = gate * sig
    hidden = (silu * up).astype(BF)
    hid_ref[...] = hidden
    d_hidden = mm(d_ref[...], down_ref[...])
    dgu_ref[:, :units] = (d_hidden * up * (sig * (1.0 + gate * (1.0 - sig)))).astype(BF)
    dgu_ref[:, units:] = (d_hidden * silu).astype(BF)
    dn_ref[...] = mm_nt(dgu_ref[...], gu_ref[...]).astype(BF)
    part_ref[...] = mm_nt(hidden, down_ref[...]).astype(BF)


def ffn_piece(normed, d_out, w_gu, w_down):
    tokens, width = normed.shape
    units = w_down.shape[1]
    return whole_call(
        ffn_kernel,
        "ffn_piece",
        [shape(tokens, width)] * 2 + [shape(tokens, units), shape(tokens, 2 * units)],
        (normed, d_out, w_gu, w_down),
        flops=12 * tokens * width * units,
        extra=tokens * units,
    )


def norm_scale(value):
    return lax.rsqrt(jnp.mean(value * value, axis=-1, keepdims=True) + EPS)


def norm_back(d_normed, value, scale, gain):
    weighted = d_normed * gain
    d_value = scale * weighted - value * (scale * scale * scale) * jnp.mean(
        weighted * value, axis=-1, keepdims=True
    )
    return d_value, jnp.sum(d_normed * value * scale, axis=0, keepdims=True)


def halo_picks(tokens, own_len, halo):
    token = lax.broadcasted_iota(jnp.int32, (tokens, halo), 0)
    slot = lax.broadcasted_iota(jnp.int32, (tokens, halo), 1)
    run, pos = token // own_len, token % own_len
    one = jnp.logical_and(pos == 0, slot == 2 * run + 1)
    two = jnp.logical_and(pos < 2, slot == 2 * run + pos)
    return one.astype(BF), two.astype(BF)


def earlier(mixed, mixed_halo, own_len):
    tokens = mixed.shape[0]
    pick_one, pick_two = halo_picks(tokens, own_len, mixed_halo.shape[0])
    pos = lax.broadcasted_iota(jnp.int32, mixed.shape, 0) % own_len
    one = jnp.where(pos == 0, mm(pick_one, mixed_halo), pltpu.roll(mixed, 1, axis=0))
    two = jnp.where(pos < 2, mm(pick_two, mixed_halo), pltpu.roll(mixed, 2, axis=0))
    return one, two


def mixer_in_kernel(
    own_len, x_ref, xh_ref, small_ref, wb_ref, wu_ref, n_ref, nh_ref, b_ref, u_ref, bh_ref, uh_ref, mix_ref, mixh_ref, conv_ref
):
    gain = small_ref[0:1].astype(F32)
    x, xh = x_ref[...].astype(F32), xh_ref[...].astype(F32)
    n_ref[...] = (x * norm_scale(x) * gain).astype(BF)
    nh_ref[...] = (xh * norm_scale(xh) * gain).astype(BF)
    b_ref[...] = mm(n_ref[...], wb_ref[...])
    u_ref[...] = mm(n_ref[...], wu_ref[...])
    bh_ref[...] = mm(nh_ref[...], wb_ref[...])
    uh_ref[...] = mm(nh_ref[...], wu_ref[...])
    mix_ref[...] = (b_ref[...] * u_ref[...]).astype(BF)
    mixh_ref[...] = (bh_ref[...] * uh_ref[...]).astype(BF)
    mixed = mix_ref[...].astype(F32)
    one, two = earlier(mixed, mixh_ref[...], own_len)
    taps = [small_ref[2 + k : 3 + k].astype(F32) for k in range(3)]
    conv_ref[...] = taps[0] * two + taps[1] * one + taps[2] * mixed


def mixer_in(own_len, x, x_halo, small, w_b, w_u):
    (tokens, width), halo, ch = x.shape, x_halo.shape[0], w_b.shape[1]
    return whole_call(
        functools.partial(mixer_in_kernel, own_len),
        "mixer_in",
        [
            shape(tokens, width),
            shape(halo, width),
            shape(tokens, ch, dtype=F32),
            shape(tokens, ch, dtype=F32),
            shape(halo, ch, dtype=F32),
            shape(halo, ch, dtype=F32),
            shape(tokens, ch),
            shape(halo, ch),
            shape(tokens, ch, dtype=F32),
        ],
        (x, x_halo, small, w_b, w_u),
        flops=4 * tokens * width * ch,
    )


def mixer_out_kernel(x_ref, n_ref, conv_ref, small_ref, wc_ref, wo_ref, c_ref, gated_ref, mid_ref, n2_ref):
    c_ref[...] = mm(n_ref[...], wc_ref[...])
    gated_ref[...] = (c_ref[...] * conv_ref[...]).astype(BF)
    mid = x_ref[...].astype(F32) + mm_nt(gated_ref[...], wo_ref[...])
    mid_ref[...] = mid
    n2_ref[...] = (mid * norm_scale(mid) * small_ref[1:2].astype(F32)).astype(BF)


def mixer_out(x, n_one, conv, small, w_c, w_o):
    (tokens, width), ch = x.shape, w_c.shape[1]
    return whole_call(
        mixer_out_kernel,
        "mixer_out",
        [
            shape(tokens, ch, dtype=F32),
            shape(tokens, ch),
            shape(tokens, width, dtype=F32),
            shape(tokens, width),
        ],
        (x, n_one, conv, small, w_c, w_o),
        flops=4 * tokens * width * ch,
    )


def mixer_back_kernel(own_len, n_parts, *refs):
    parts = refs[:n_parts]
    (mid_ref, dy_ref, x_ref, xh_ref, small_ref, b_ref, u_ref, c_ref, bh_ref, uh_ref, mix_ref, mixh_ref, conv_ref) = refs[
        n_parts : n_parts + 13
    ]
    wb_ref, wu_ref, wc_ref, wo_ref = refs[n_parts + 13 : n_parts + 17]
    dmix_ref, db_ref, du_ref, dc_ref, dbh_ref, duh_ref, gin_ref, dxh_ref, sg_ref = refs[n_parts + 17 :]
    gain_one, gain_two = small_ref[0:1].astype(F32), small_ref[1:2].astype(F32)
    taps = [small_ref[2 + k : 3 + k].astype(F32) for k in range(3)]
    d_n2 = parts[0][...].astype(F32)
    for part in parts[1:]:
        d_n2 = d_n2 + part[...].astype(F32)
    mid = mid_ref[...]
    d_mid, g_two = norm_back(d_n2, mid, norm_scale(mid), gain_two)
    d_mid = d_mid + dy_ref[...].astype(F32)
    dmix_ref[...] = d_mid.astype(BF)
    d_gated = mm(dmix_ref[...], wo_ref[...])
    dc_ref[...] = (d_gated * conv_ref[...]).astype(BF)
    d_conv = d_gated * c_ref[...]
    mixed = mix_ref[...].astype(F32)
    one, two = earlier(mixed, mixh_ref[...], own_len)
    tap_rows = [jnp.sum(d_conv * view, axis=0, keepdims=True) for view in (two, one, mixed)]
    tokens = mixed.shape[0]
    pos = lax.broadcasted_iota(jnp.int32, mixed.shape, 0) % own_len
    d_mixed = taps[2] * d_conv
    d_mixed = d_mixed + taps[1] * jnp.where(pos < own_len - 1, pltpu.roll(d_conv, tokens - 1, axis=0), 0.0)
    d_mixed = d_mixed + taps[0] * jnp.where(pos < own_len - 2, pltpu.roll(d_conv, tokens - 2, axis=0), 0.0)
    db_ref[...] = (d_mixed * u_ref[...]).astype(BF)
    du_ref[...] = (d_mixed * b_ref[...]).astype(BF)
    pick_one, pick_two = halo_picks(tokens, own_len, mixh_ref.shape[0])
    low = d_conv.astype(BF)
    d_halo = taps[1] * mm_tn(pick_one, low) + taps[0] * mm_tn(pick_two, low)
    dbh_ref[...] = (d_halo * uh_ref[...]).astype(BF)
    duh_ref[...] = (d_halo * bh_ref[...]).astype(BF)
    d_n1 = mm_nt(db_ref[...], wb_ref[...]) + mm_nt(du_ref[...], wu_ref[...]) + mm_nt(dc_ref[...], wc_ref[...])
    x, xh = x_ref[...].astype(F32), xh_ref[...].astype(F32)
    d_x, g_one = norm_back(d_n1, x, norm_scale(x), gain_one)
    gin_ref[...] = d_x + d_mid
    d_nh = mm_nt(dbh_ref[...], wb_ref[...]) + mm_nt(duh_ref[...], wu_ref[...])
    d_xh, g_halo = norm_back(d_nh, xh, norm_scale(xh), gain_one)
    dxh_ref[...] = d_xh.astype(BF)
    for row, value in enumerate([g_one + g_halo, g_two] + tap_rows):
        sg_ref[row : row + 1] = value
    sg_ref[5:8] = jnp.zeros((3, sg_ref.shape[1]), F32)


def mixer_back(own_len, parts, saved, weights):
    (tokens, width), ch = parts[0].shape, weights[0].shape[1]
    halo = saved[3].shape[0]
    return whole_call(
        functools.partial(mixer_back_kernel, own_len, len(parts)),
        "mixer_back",
        [shape(tokens, width)]
        + [shape(tokens, ch)] * 3
        + [shape(halo, ch)] * 2
        + [shape(tokens, width, dtype=F32), shape(halo, width), shape(8, width, dtype=F32)],
        (*parts, *saved, *weights),
        flops=8 * tokens * width * ch,
    )


def mixer_grad_kernel(with_halo, idx_ref, *refs):
    n_in = 7 if with_halo else 4
    ins, away_ref, home_ref = refs[:n_in], refs[n_in], refs[n_in + 1]
    me = idx_ref[0]
    quad, core = me // 2, lax.rem(me, 2)
    n_z, ch = away_ref.shape[1], away_ref.shape[3]
    rows = ins[0].shape[1] // 8

    @pl.loop(0, 4)
    def _(kq):
        chip = jnp.bitwise_xor(quad, kq) * 2
        away = pl.multiple_of((chip + 1 - core) * rows, rows)
        home = pl.multiple_of((chip + core) * rows, rows)
        for st in range(2):
            left_ref, right_ref = ins[2 * st], ins[2 * st + 1]
            left = jnp.concatenate([left_ref[:, pl.ds(away, rows)], left_ref[:, pl.ds(home, rows)]], axis=1)
            grad = mm_tn(left, right_ref[...])
            if with_halo:
                nh_ref = ins[4]
                left = jnp.concatenate([nh_ref[:, pl.ds(away, rows)], nh_ref[:, pl.ds(home, rows)]], axis=1)
                grad = grad + mm_tn(left, ins[5][:, st * n_z * ch : (st + 1) * n_z * ch])
            grad = grad.astype(BF)
            for z in range(n_z):
                cols = slice(z * ch, (z + 1) * ch)
                away_ref[kq, z, st * rows : (st + 1) * rows] = grad[:rows, cols]
                home_ref[kq, z, st * rows : (st + 1) * rows] = grad[rows:, cols]
        if with_halo:
            for ref, at in ((away_ref, away), (home_ref, home)):
                values = ins[6][:, pl.ds(at, rows)]
                values = jnp.concatenate([values, jnp.zeros_like(values)], axis=0)
                values = jnp.concatenate([values] + [jnp.zeros_like(values)] * (ch // rows - 1), axis=1)
                for z in range(n_z):
                    ref[kq, z, 2 * rows :] = values.astype(BF)


def mixer_grads(index, ins, n_z, rows, with_halo):
    ch = ins[1].shape[1] // n_z
    extra = 16 if with_halo else 0
    outs = [shape(4, n_z, 2 * rows + extra, ch)] * 2
    return whole_call(
        functools.partial(mixer_grad_kernel, with_halo),
        "grads_in" if with_halo else "grads_out",
        outs,
        (index, *ins),
        scalars=1,
        flops=4 * ins[0].size * ins[1].shape[1],
    )


def ffn_grad_kernel(first, count, idx_ref, n_ref, d_ref, hid_ref, dgu_ref, away_ref, home_ref):
    me = idx_ref[0]
    quad, core = me // 2, lax.rem(me, 2)
    rows = n_ref.shape[1] // 8
    split = dgu_ref.shape[1]

    @pl.loop(0, count)
    def _(i):
        chip = jnp.bitwise_xor(quad, first - i) * 2
        away = pl.multiple_of((chip + 1 - core) * rows, rows)
        home = pl.multiple_of((chip + core) * rows, rows)
        left = jnp.concatenate([n_ref[:, pl.ds(away, rows)], n_ref[:, pl.ds(home, rows)]], axis=1)
        grad = mm_tn(left, dgu_ref[...]).astype(BF)
        away_ref[i, :, :split] = grad[:rows]
        home_ref[i, :, :split] = grad[rows:]
        left = jnp.concatenate([d_ref[:, pl.ds(away, rows)], d_ref[:, pl.ds(home, rows)]], axis=1)
        grad = mm_tn(left, hid_ref[...]).astype(BF)
        away_ref[i, :, split:] = grad[:rows]
        home_ref[i, :, split:] = grad[rows:]


def ffn_grads(index, first, count, n_all, d_all, hid_all, dgu_all):
    rows = n_all.shape[1] // 8
    columns = hid_all.shape[1] + dgu_all.shape[1]
    return whole_call(
        functools.partial(ffn_grad_kernel, first, count),
        "ffn_grads",
        [shape(count, rows, columns)] * 2,
        (index, n_all, d_all, hid_all, dgu_all),
        scalars=1,
        flops=count * 4 * rows * n_all.shape[0] * columns,
    )


def plane_reduce(halves):
    arrived = {kq: dp_swap(halves[kq], 2 * kq) for kq in (3, 1, 2)}
    return halves[0].astype(F32) + arrived[1].astype(F32) + arrived[2].astype(F32) + arrived[3].astype(F32)


def body(
    layer_in,
    cotangent,
    row_counts,
    tail_tokens,
    row_order,
    gain_one,
    w_in,
    kernel,
    w_out,
    gain_two,
    w_gu,
    w_down,
):
    row_count, own_len, width = layer_in.shape
    n_dp, n_z = lax.axis_size("dp"), lax.axis_size("tensor")
    outer = n_dp // INNER
    me, z = lax.axis_index("dp"), lax.axis_index("tensor")
    me_in = me // outer
    row_len = own_len * n_z
    channels = w_in.shape[2]
    reach = kernel.shape[0] - 1
    tokens = row_count * own_len
    block = width // INNER
    units = w_down.shape[0]
    index = jnp.stack([me_in, z]).astype(jnp.int32)

    given = lax.dynamic_slice_in_dim(row_order, me * row_count, row_count)
    starts = jnp.cumsum(row_counts) - row_counts
    ends = starts + row_counts - 1
    is_first = jnp.any(starts[None, :] == given[:, None], axis=1)
    at_end = ends[None, :] == given[:, None]
    row_valid = jnp.where(
        jnp.any(at_end, axis=1),
        jnp.sum(jnp.where(at_end, tail_tokens[None, :], 0), axis=1),
        row_len,
    )
    positions = z * own_len + jnp.arange(own_len, dtype=jnp.int32)
    valid = positions[None, :] < row_valid[:, None]

    small = jnp.concatenate([gain_one[None], gain_two[None], kernel], axis=0)
    w_b, w_c, w_u = (w_in[:, st] for st in range(3))
    mix_bu = jnp.stack([w_b, w_u])
    mix_co = jnp.stack([w_c, w_out.T])
    ffn_own = jnp.concatenate([w_gu[:, 0], w_gu[:, 1], w_down.T], axis=1)
    groups = [[i * outer + o for o in range(outer)] for i in range(INNER)]
    if outer > 1:
        wide = functools.partial(lax.all_gather, axis_name="dp", tiled=True, axis_index_groups=groups)
        mix_bu, mix_co, ffn_own = wide(mix_bu, axis=1), wide(mix_co, axis=1), wide(ffn_own, axis=0)
        small = wide(small, axis=1)
    n_small = small.shape[0]
    small_rows = jnp.pad(small, ((0, 16 - n_small), (0, channels - block)))
    bu_rows, co_rows = (m.reshape(2 * block, channels) for m in (mix_bu, mix_co))

    bu_set = [bu_rows] + [z_shift(bu_rows, s) for s in range(1, n_z)]
    bu_pieces = plane_gather(jnp.concatenate(bu_set + [small_rows], axis=0))
    co_set = [co_rows] + [z_shift(co_rows, s) for s in range(1, n_z)]
    co_pieces = plane_gather(jnp.concatenate(co_set, axis=0))
    w_b, w_u, small_all = place_mixer(index, bu_pieces, width, n_z, True)
    w_c, w_o = place_mixer(index, co_pieces, width, n_z, False)
    w_gu_all, w_down_all = place_ffn(index, plane_gather(ffn_own))

    before = z_shift(layer_in[:, own_len - reach :].reshape(row_count, reach * width), 1)
    every = before[None]
    if outer > 1:
        every = lax.all_gather(before, "dp", axis=0, axis_index_groups=groups)
    every = every[None]
    for step in (1, 2, 4):
        every = jnp.concatenate([every, dp_swap(every, step)], axis=0)
    slots = INNER * outer * row_count
    rel = jnp.bitwise_xor(me_in, jnp.arange(INNER, dtype=jnp.int32))
    slot_rows = row_order.reshape(INNER, outer * row_count)[rel].reshape(slots)
    before_mask = jnp.logical_and(
        slot_rows[None, :] == (given - 1)[:, None], jnp.logical_not(is_first)[:, None]
    )
    before_mask = jnp.logical_and(before_mask, z == 0).astype(BF)
    crossed = mm(before_mask, every.reshape(slots, reach * width))
    x_halo = jnp.where(z == 0, crossed.astype(BF), before).reshape(row_count * reach, width)

    d_ffn = jnp.where(valid[:, :, None], cotangent, jnp.zeros_like(cotangent)).reshape(tokens, width)
    d_ffn_set = [d_ffn] + [z_shift(d_ffn, s) for s in range(1, n_z)]

    x_own = layer_in.reshape(tokens, width)
    n_one, n_halo, b_own, u_own, b_halo, u_halo, mixed, mixed_halo, conv = mixer_in(
        own_len, x_own, x_halo, small_all, w_b, w_u
    )
    c_own, gated, middle, n_two = mixer_out(x_own, n_one, conv, small_all, w_c, w_o)

    n_two_set = [n_two] + [z_shift(n_two, s) for s in range(1, n_z)]
    order = [0, 1, 3, 2] if n_z == 4 else list(range(n_z))
    runs = {s: ffn_piece(n_two_set[s], d_ffn_set[s], w_gu_all, w_down_all) for s in order}
    d_parts = [runs[0][0]] + [z_shift(runs[s][0], n_z - s) for s in order[1:]]

    n_all = jnp.concatenate([n_two_set[s] for s in order], axis=0)
    d_all = jnp.concatenate([d_ffn_set[s] for s in order], axis=0)
    hid_all = jnp.concatenate([runs[s][2] for s in order], axis=0)
    dgu_all = jnp.concatenate([runs[s][3] for s in order], axis=0)
    away, home = ffn_grads(index, 3, 4, n_all, d_all, hid_all, dgu_all)
    other = dp_swap(away, 1)
    halves = [(home[3 - kq].astype(F32) + other[3 - kq].astype(F32)).astype(BF) for kq in range(4)]
    ffn_total = plane_reduce(halves)

    d_mix, d_b, d_u, d_c, d_b_halo, d_u_halo, grad_mid, d_x_halo, small_grads = mixer_back(
        own_len,
        d_parts,
        (middle, d_ffn, x_own, x_halo, small_all, b_own, u_own, c_own, b_halo, u_halo, mixed, mixed_halo, conv),
        (w_b, w_u, w_c, w_o),
    )
    co_away, co_home = mixer_grads(index, (n_one, d_c, d_mix, gated), n_z, block, False)
    d_bu_halo = jnp.concatenate([d_b_halo, d_u_halo], axis=1)
    bu_away, bu_home = mixer_grads(
        index, (n_one, d_b, n_one, d_u, n_halo, d_bu_halo, small_grads), n_z, block, True
    )

    def mixer_reduce(away, home):
        other = dp_swap(away, 1)
        halves = [(home[kq].astype(F32) + other[kq].astype(F32)).astype(BF) for kq in range(4)]
        plane = plane_reduce(halves).astype(BF)
        total = lax.dynamic_index_in_dim(plane, z, 0, keepdims=False).astype(F32)
        for s in range(1, n_z):
            piece = lax.dynamic_index_in_dim(plane, lax.rem(z + s, n_z), 0, keepdims=False)
            total = total + z_shift(piece, s).astype(F32)
        return total

    co_total = mixer_reduce(co_away, co_home)
    bu_total = mixer_reduce(bu_away, bu_home)

    ffn_sum = runs[0][1].astype(F32)
    for s in order[1:]:
        ffn_sum = ffn_sum + z_shift(runs[s][1], n_z - s).astype(F32)
    layer_out = (middle + ffn_sum).astype(BF).reshape(row_count, own_len, width)

    back = d_x_halo.reshape(row_count, reach * width)
    spread = mm_tn(before_mask, back).astype(BF).reshape(INNER, outer * row_count, reach * width)
    for step in (4, 2, 1):
        spread = (spread[:step].astype(F32) + dp_swap(spread[step:], step).astype(F32)).astype(BF)
    returned = spread[0]
    if outer > 1:
        returned = lax.psum_scatter(
            returned, "dp", scatter_dimension=0, tiled=True, axis_index_groups=groups
        )
    returned = z_shift(jnp.where(z == 0, returned, back), n_z - 1)
    returned = returned.astype(F32).reshape(row_count, reach, width)
    grad_in = grad_mid.reshape(row_count, own_len, width)
    grad_in = grad_in + jnp.pad(returned, ((0, 0), (own_len - reach, 0), (0, 0)))

    if outer > 1:
        narrow = functools.partial(
            lax.psum_scatter, axis_name="dp", tiled=True, axis_index_groups=groups
        )
        grad_bu = narrow(bu_total[: 2 * block].reshape(2, block, channels), scatter_dimension=1)
        grad_co = narrow(co_total.reshape(2, block, channels), scatter_dimension=1)
        grad_small = narrow(bu_total[2 * block : 2 * block + n_small, :block], scatter_dimension=1)
        ffn_total = narrow(ffn_total, scatter_dimension=0)
    else:
        grad_bu = bu_total[: 2 * block].reshape(2, block, channels)
        grad_co = co_total.reshape(2, block, channels)
        grad_small = bu_total[2 * block : 2 * block + n_small, :block]
    return (
        layer_out,
        grad_in.astype(BF),
        grad_small[0],
        jnp.stack([grad_bu[0], grad_co[0], grad_bu[1]], axis=1),
        grad_small[2:],
        grad_co[1].T,
        grad_small[1],
        jnp.stack([ffn_total[:, :units], ffn_total[:, units : 2 * units]], axis=1),
        ffn_total[:, 2 * units :].T,
    )


def solution(mesh):
    in_specs = (
        P("dp", "tensor", None),
        P("dp", "tensor", None),
        P(),
        P(),
        P(),
        P("dp"),
        P("dp", None, "tensor"),
        P(None, "dp"),
        P("tensor", "dp"),
        P("dp"),
        P("dp", None, "tensor"),
        P("tensor", "dp"),
    )
    out_specs = (
        P("dp", "tensor", None),
        P("dp", "tensor", None),
        P("dp"),
        P("dp", None, "tensor"),
        P(None, "dp"),
        P("tensor", "dp"),
        P("dp"),
        P("dp", None, "tensor"),
        P("tensor", "dp"),
    )
    return jax.shard_map(body, mesh=mesh, in_specs=in_specs, out_specs=out_specs, check_vma=False)
```

```python
import functools
import jax
import jax.numpy as jnp
from jax import lax
from jax.experimental import pallas as pl
from jax.experimental.pallas import tpu as pltpu
from jax.sharding import PartitionSpec as P

EPS = 1e-05
INNER = 8
BF = jnp.bfloat16
F32 = jnp.float32
VMEM_LIMIT = 12 << 20


def dp_swap(value, step, tag):
    size = lax.axis_size("dp")
    hop = step * (size // INNER)
    with jax.named_scope(f"{tag}_dp{step}"):
        return lax.ppermute(value, "dp", [(i, i ^ hop) for i in range(size)])


def z_shift(value, step, tag):
    size = lax.axis_size("tensor")
    with jax.named_scope(f"{tag}_z"):
        return lax.ppermute(value, "tensor", [(i, (i + step) % size) for i in range(size)])


def z_swap(value, step, tag):
    size = lax.axis_size("tensor")
    with jax.named_scope(f"{tag}_z{step}"):
        return lax.ppermute(value, "tensor", [(i, i ^ step) for i in range(size)])


def after(value, *events):
    return lax.optimization_barrier((value,) + events)[0]


def mm(a, b):
    return lax.dot_general(a, b, (((1,), (0,)), ((), ())), preferred_element_type=F32)


def mm_nt(a, b):
    return lax.dot_general(a, b, (((1,), (1,)), ((), ())), preferred_element_type=F32)


def mm_tn(a, b):
    return lax.dot_general(a, b, (((0,), (0,)), ((), ())), preferred_element_type=F32)


def shape(*dims, dtype=BF):
    return jax.ShapeDtypeStruct(dims, dtype)


def whole_call(kernel, name, outs, args, scalars=0, hbm=0, scratch=(), flops=0, extra=0, alias=None):
    specs = [pl.BlockSpec(memory_space=pltpu.SMEM)] * scalars
    specs += [pl.BlockSpec(memory_space=pltpu.HBM)] * hbm
    specs += [pl.BlockSpec(memory_space=pltpu.VMEM)] * (len(args) - scalars - hbm)
    moved = sum(a.size * a.dtype.itemsize for a in args) + sum(
        o.size * jnp.dtype(o.dtype).itemsize for o in outs
    )
    return pl.pallas_call(
        kernel,
        out_shape=outs,
        in_specs=specs,
        out_specs=[pl.BlockSpec(memory_space=pltpu.VMEM)] * len(outs),
        scratch_shapes=list(scratch),
        input_output_aliases=alias or {},
        compiler_params=pltpu.CompilerParams(vmem_limit_bytes=VMEM_LIMIT),
        cost_estimate=pl.CostEstimate(flops=1, bytes_accessed=1, transcendentals=0),
        name=name,
    )(*args)


def plane_send(local, tag, kqs, *waits):
    return [dp_swap(after(local, *waits), 2 * kq, tag) for kq in kqs]


def core_pairs(own, tag, *waits):
    other = [dp_swap(after(piece, *waits) if waits else piece, 1, tag) for piece in own]
    return [piece for pair in zip(own, other) for piece in pair]


def z_send(local, tag, steps, *waits):
    local = after(local, *waits) if waits else local
    return [z_swap(local, step, tag) for step in steps]


def z_return(parts, tag, *waits):
    total = parts[0].astype(F32)
    for step in range(1, len(parts)):
        part = after(parts[step], *waits) if waits else parts[step]
        total = total + z_swap(part, step, tag).astype(F32)
    return total


def place_mixer_kernel(with_small, idx_ref, *refs):
    pieces, outs, sems = refs[:8], refs[8:-1], refs[-1]
    me, z = idx_ref[0], idx_ref[1]
    n_z = outs[0].shape[1] // 256
    rows = outs[0].shape[0] // 8
    copies = []
    for k in range(8):
        at = pl.multiple_of(jnp.bitwise_xor(me, k) * rows, rows)
        for s in range(n_z):
            col = pl.multiple_of(jnp.bitwise_xor(z, s) * 256, 256)
            for st in range(2):
                copies.append(
                    pltpu.make_async_copy(
                        pieces[k].at[pl.ds((s * 2 + st) * rows, rows)],
                        outs[st].at[pl.ds(at, rows), pl.ds(col, 256)],
                        sems.at[k, s * 2 + st],
                    )
                )
        if with_small:
            copies.append(
                pltpu.make_async_copy(
                    pieces[k].at[pl.ds(2 * n_z * rows, 16), pl.ds(0, rows)],
                    outs[2].at[:, pl.ds(at, rows)],
                    sems.at[k, 2 * n_z],
                )
            )
    for copy in copies:
        copy.start()
    for copy in copies:
        copy.wait()


def place_mixer(index, pieces, width, n_z, with_small):
    outs = [shape(width, n_z * 256)] * 2 + ([shape(16, width)] if with_small else [])
    return whole_call(
        functools.partial(place_mixer_kernel, with_small),
        "place_small" if with_small else "place_mixer",
        outs,
        (index, *pieces),
        scalars=1,
        hbm=8,
        scratch=[pltpu.SemaphoreType.DMA((8, 2 * n_z + 1))],
    )


def place_ffn_kernel(idx_ref, *refs):
    pieces, out_ref, sems = refs[:8], refs[8], refs[9]
    me = idx_ref[0]
    rows = out_ref.shape[0] // 8
    copies = []
    for k in range(8):
        at = pl.ds(pl.multiple_of(jnp.bitwise_xor(me, k) * rows, rows), rows)
        copies.append(pltpu.make_async_copy(pieces[k], out_ref.at[at], sems.at[k]))
    for copy in copies:
        copy.start()
    for copy in copies:
        copy.wait()


def place_ffn(index, pieces):
    rows, columns = pieces[0].shape
    return whole_call(
        place_ffn_kernel,
        "place_ffn",
        [shape(8 * rows, columns)],
        (index, *pieces),
        scalars=1,
        hbm=8,
        scratch=[pltpu.SemaphoreType.DMA((8,))],
    )[0]


def ffn_kernel(step, n_ref, d_ref, w_ref, *refs):
    dn_ref, part_ref, n_all_ref, d_all_ref, hid_ref, dgu_ref = refs[-6:]
    tokens = n_ref.shape[0]
    own = slice(step * tokens, (step + 1) * tokens)
    units = w_ref.shape[1] // 3
    gu, down = slice(0, 2 * units), slice(2 * units, 3 * units)
    n_all_ref[own] = n_ref[...]
    d_all_ref[own] = d_ref[...]
    both = mm(n_ref[...], w_ref[:, gu])
    gate, up = both[:, :units], both[:, units:]
    sig = jax.nn.sigmoid(gate)
    silu = gate * sig
    hidden = (silu * up).astype(BF)
    hid_ref[own] = hidden
    d_hidden = mm(d_ref[...], w_ref[:, down])
    dgu_ref[own, :units] = (d_hidden * up * (sig * (1.0 + gate * (1.0 - sig)))).astype(BF)
    dgu_ref[own, units:] = (d_hidden * silu).astype(BF)
    dn_ref[...] = mm_nt(dgu_ref[own], w_ref[:, gu]).astype(BF)
    part_ref[...] = mm_nt(hidden, w_ref[:, down]).astype(BF)


def ffn_piece(step, steps, normed, d_out, weights, kept):
    tokens, width = normed.shape
    units = weights.shape[1] // 3
    every = steps * tokens
    return whole_call(
        functools.partial(ffn_kernel, step),
        "ffn_piece",
        [shape(tokens, width)] * 2
        + [shape(every, width), shape(every, width), shape(every, units), shape(every, 2 * units)],
        (normed, d_out, weights, *kept),
        flops=12 * tokens * width * units,
        extra=tokens * units,
        alias={3 + i: 2 + i for i in range(len(kept))},
    )


def norm_scale(value):
    return lax.rsqrt(jnp.mean(value * value, axis=-1, keepdims=True) + EPS)


def norm_back(d_normed, value, scale, gain):
    weighted = d_normed * gain
    d_value = scale * weighted - value * (scale * scale * scale) * jnp.mean(
        weighted * value, axis=-1, keepdims=True
    )
    return d_value, jnp.sum(d_normed * value * scale, axis=0, keepdims=True)


def halo_picks(tokens, own_len, halo):
    token = lax.broadcasted_iota(jnp.int32, (tokens, halo), 0)
    slot = lax.broadcasted_iota(jnp.int32, (tokens, halo), 1)
    run, pos = token // own_len, token % own_len
    one = jnp.logical_and(pos == 0, slot == 2 * run + 1)
    two = jnp.logical_and(pos < 2, slot == 2 * run + pos)
    return one.astype(BF), two.astype(BF)


def earlier(mixed, mixed_halo, own_len):
    tokens = mixed.shape[0]
    pick_one, pick_two = halo_picks(tokens, own_len, mixed_halo.shape[0])
    pos = lax.broadcasted_iota(jnp.int32, mixed.shape, 0) % own_len
    one = jnp.where(pos == 0, mm(pick_one, mixed_halo), pltpu.roll(mixed, 1, axis=0))
    two = jnp.where(pos < 2, mm(pick_two, mixed_halo), pltpu.roll(mixed, 2, axis=0))
    return one, two


def mixer_in_kernel(
    own_len, x_ref, xh_ref, small_ref, wb_ref, wu_ref, n_ref, nh_ref, b_ref, u_ref, bh_ref, uh_ref, mix_ref, mixh_ref, conv_ref
):
    gain = small_ref[0:1].astype(F32)
    x, xh = x_ref[...].astype(F32), xh_ref[...].astype(F32)
    n_ref[...] = (x * norm_scale(x) * gain).astype(BF)
    nh_ref[...] = (xh * norm_scale(xh) * gain).astype(BF)
    b_ref[...] = mm(n_ref[...], wb_ref[...])
    u_ref[...] = mm(n_ref[...], wu_ref[...])
    bh_ref[...] = mm(nh_ref[...], wb_ref[...])
    uh_ref[...] = mm(nh_ref[...], wu_ref[...])
    mix_ref[...] = (b_ref[...] * u_ref[...]).astype(BF)
    mixh_ref[...] = (bh_ref[...] * uh_ref[...]).astype(BF)
    mixed = mix_ref[...].astype(F32)
    one, two = earlier(mixed, mixh_ref[...], own_len)
    taps = [small_ref[2 + k : 3 + k].astype(F32) for k in range(3)]
    conv_ref[...] = taps[0] * two + taps[1] * one + taps[2] * mixed


def mixer_in(own_len, x, x_halo, small, w_b, w_u):
    (tokens, width), halo, ch = x.shape, x_halo.shape[0], w_b.shape[1]
    return whole_call(
        functools.partial(mixer_in_kernel, own_len),
        "mixer_in",
        [
            shape(tokens, width),
            shape(halo, width),
            shape(tokens, ch, dtype=F32),
            shape(tokens, ch, dtype=F32),
            shape(halo, ch, dtype=F32),
            shape(halo, ch, dtype=F32),
            shape(tokens, ch),
            shape(halo, ch),
            shape(tokens, ch, dtype=F32),
        ],
        (x, x_halo, small, w_b, w_u),
        flops=4 * tokens * width * ch,
    )


def mixer_out_kernel(x_ref, n_ref, conv_ref, small_ref, wc_ref, wo_ref, c_ref, gated_ref, mid_ref, n2_ref):
    c_ref[...] = mm(n_ref[...], wc_ref[...])
    gated_ref[...] = (c_ref[...] * conv_ref[...]).astype(BF)
    mid = x_ref[...].astype(F32) + mm_nt(gated_ref[...], wo_ref[...])
    mid_ref[...] = mid
    n2_ref[...] = (mid * norm_scale(mid) * small_ref[1:2].astype(F32)).astype(BF)


def mixer_out(x, n_one, conv, small, w_c, w_o):
    (tokens, width), ch = x.shape, w_c.shape[1]
    return whole_call(
        mixer_out_kernel,
        "mixer_out",
        [
            shape(tokens, ch, dtype=F32),
            shape(tokens, ch),
            shape(tokens, width, dtype=F32),
            shape(tokens, width),
        ],
        (x, n_one, conv, small, w_c, w_o),
        flops=4 * tokens * width * ch,
    )


def mixer_back_kernel(own_len, n_parts, *refs):
    parts = refs[:n_parts]
    (mid_ref, dy_ref, x_ref, xh_ref, small_ref, b_ref, u_ref, c_ref, bh_ref, uh_ref, mix_ref, mixh_ref, conv_ref) = refs[
        n_parts : n_parts + 13
    ]
    wb_ref, wu_ref, wc_ref, wo_ref = refs[n_parts + 13 : n_parts + 17]
    dmix_ref, db_ref, du_ref, dc_ref, dbh_ref, duh_ref, gin_ref, dxh_ref, sg_ref = refs[n_parts + 17 :]
    gain_one, gain_two = small_ref[0:1].astype(F32), small_ref[1:2].astype(F32)
    taps = [small_ref[2 + k : 3 + k].astype(F32) for k in range(3)]
    d_n2 = parts[0][...].astype(F32)
    for part in parts[1:]:
        d_n2 = d_n2 + part[...].astype(F32)
    mid = mid_ref[...]
    d_mid, g_two = norm_back(d_n2, mid, norm_scale(mid), gain_two)
    d_mid = d_mid + dy_ref[...].astype(F32)
    dmix_ref[...] = d_mid.astype(BF)
    d_gated = mm(dmix_ref[...], wo_ref[...])
    dc_ref[...] = (d_gated * conv_ref[...]).astype(BF)
    d_conv = d_gated * c_ref[...]
    mixed = mix_ref[...].astype(F32)
    one, two = earlier(mixed, mixh_ref[...], own_len)
    tap_rows = [jnp.sum(d_conv * view, axis=0, keepdims=True) for view in (two, one, mixed)]
    tokens = mixed.shape[0]
    pos = lax.broadcasted_iota(jnp.int32, mixed.shape, 0) % own_len
    d_mixed = taps[2] * d_conv
    d_mixed = d_mixed + taps[1] * jnp.where(pos < own_len - 1, pltpu.roll(d_conv, tokens - 1, axis=0), 0.0)
    d_mixed = d_mixed + taps[0] * jnp.where(pos < own_len - 2, pltpu.roll(d_conv, tokens - 2, axis=0), 0.0)
    db_ref[...] = (d_mixed * u_ref[...]).astype(BF)
    du_ref[...] = (d_mixed * b_ref[...]).astype(BF)
    pick_one, pick_two = halo_picks(tokens, own_len, mixh_ref.shape[0])
    low = d_conv.astype(BF)
    d_halo = taps[1] * mm_tn(pick_one, low) + taps[0] * mm_tn(pick_two, low)
    dbh_ref[...] = (d_halo * uh_ref[...]).astype(BF)
    duh_ref[...] = (d_halo * bh_ref[...]).astype(BF)
    d_n1 = mm_nt(db_ref[...], wb_ref[...]) + mm_nt(du_ref[...], wu_ref[...]) + mm_nt(dc_ref[...], wc_ref[...])
    x, xh = x_ref[...].astype(F32), xh_ref[...].astype(F32)
    d_x, g_one = norm_back(d_n1, x, norm_scale(x), gain_one)
    gin_ref[...] = d_x + d_mid
    d_nh = mm_nt(dbh_ref[...], wb_ref[...]) + mm_nt(duh_ref[...], wu_ref[...])
    d_xh, g_halo = norm_back(d_nh, xh, norm_scale(xh), gain_one)
    dxh_ref[...] = d_xh.astype(BF)
    for row, value in enumerate([g_one + g_halo, g_two] + tap_rows):
        sg_ref[row : row + 1] = value
    sg_ref[5:8] = jnp.zeros((3, sg_ref.shape[1]), F32)


def mixer_back(own_len, parts, saved, weights):
    (tokens, width), ch = parts[0].shape, weights[0].shape[1]
    halo = saved[3].shape[0]
    return whole_call(
        functools.partial(mixer_back_kernel, own_len, len(parts)),
        "mixer_back",
        [shape(tokens, width)]
        + [shape(tokens, ch)] * 3
        + [shape(halo, ch)] * 2
        + [shape(tokens, width, dtype=F32), shape(halo, width), shape(8, width, dtype=F32)],
        (*parts, *saved, *weights),
        flops=8 * tokens * width * ch,
    )


def mixer_grad_kernel(with_halo, idx_ref, *refs):
    n_in = 7 if with_halo else 4
    ins, away_ref, home_ref = refs[:n_in], refs[n_in], refs[n_in + 1]
    me, my_z = idx_ref[0], idx_ref[1]
    quad, core = me // 2, lax.rem(me, 2)
    n_z, ch = away_ref.shape[1], away_ref.shape[3]
    rows = ins[0].shape[1] // 8

    @pl.loop(0, 4)
    def _(kq):
        chip = jnp.bitwise_xor(quad, kq) * 2
        away = pl.multiple_of((chip + 1 - core) * rows, rows)
        home = pl.multiple_of((chip + core) * rows, rows)
        for st in range(2):
            left_ref, right_ref = ins[2 * st], ins[2 * st + 1]
            left = jnp.concatenate([left_ref[:, pl.ds(away, rows)], left_ref[:, pl.ds(home, rows)]], axis=1)
            grad = mm_tn(left, right_ref[...])
            if with_halo:
                nh_ref = ins[4]
                left = jnp.concatenate([nh_ref[:, pl.ds(away, rows)], nh_ref[:, pl.ds(home, rows)]], axis=1)
                grad = grad + mm_tn(left, ins[5][:, st * n_z * ch : (st + 1) * n_z * ch])
            grad = grad.astype(BF)
            for z in range(n_z):
                cols = slice(z * ch, (z + 1) * ch)
                at_z = jnp.bitwise_xor(my_z, z)
                away_ref[kq, at_z, st * rows : (st + 1) * rows] = grad[:rows, cols]
                home_ref[kq, at_z, st * rows : (st + 1) * rows] = grad[rows:, cols]
        if with_halo:
            for ref, at in ((away_ref, away), (home_ref, home)):
                values = ins[6][:, pl.ds(at, rows)]
                values = jnp.concatenate([values, jnp.zeros_like(values)], axis=0)
                values = jnp.concatenate([values] + [jnp.zeros_like(values)] * (ch // rows - 1), axis=1)
                for z in range(n_z):
                    ref[kq, z, 2 * rows :] = values.astype(BF)


def mixer_grads(index, ins, n_z, rows, with_halo):
    ch = ins[1].shape[1] // n_z
    extra = 16 if with_halo else 0
    outs = [shape(4, n_z, 2 * rows + extra, ch)] * 2
    return whole_call(
        functools.partial(mixer_grad_kernel, with_halo),
        "grads_in" if with_halo else "grads_out",
        outs,
        (index, *ins),
        scalars=1,
        flops=4 * ins[0].size * ins[1].shape[1],
    )


def ffn_grad_kernel(first, count, idx_ref, n_ref, d_ref, hid_ref, dgu_ref, away_ref, home_ref):
    me = idx_ref[0]
    quad, core = me // 2, lax.rem(me, 2)
    rows = n_ref.shape[1] // 8
    split = dgu_ref.shape[1]

    @pl.loop(0, count)
    def _(i):
        chip = jnp.bitwise_xor(quad, first + i) * 2
        away = pl.multiple_of((chip + 1 - core) * rows, rows)
        home = pl.multiple_of((chip + core) * rows, rows)
        left = jnp.concatenate([n_ref[:, pl.ds(away, rows)], n_ref[:, pl.ds(home, rows)]], axis=1)
        grad = mm_tn(left, dgu_ref[...]).astype(BF)
        away_ref[i, :, :split] = grad[:rows]
        home_ref[i, :, :split] = grad[rows:]
        left = jnp.concatenate([d_ref[:, pl.ds(away, rows)], d_ref[:, pl.ds(home, rows)]], axis=1)
        grad = mm_tn(left, hid_ref[...]).astype(BF)
        away_ref[i, :, split:] = grad[:rows]
        home_ref[i, :, split:] = grad[rows:]


def ffn_grads(index, first, count, n_all, d_all, hid_all, dgu_all):
    rows = n_all.shape[1] // 8
    columns = hid_all.shape[1] + dgu_all.shape[1]
    return whole_call(
        functools.partial(ffn_grad_kernel, first, count),
        "ffn_grads",
        [shape(count, rows, columns)] * 2,
        (index, n_all, d_all, hid_all, dgu_all),
        scalars=1,
        flops=count * 4 * rows * n_all.shape[0] * columns,
    )


def core_sum(away, home, count, tag):
    other = dp_swap(away, 1, tag)
    return [(home[kq].astype(F32) + other[kq].astype(F32)).astype(BF) for kq in range(count)]


def body(
    layer_in,
    cotangent,
    row_counts,
    tail_tokens,
    row_order,
    gain_one,
    w_in,
    kernel,
    w_out,
    gain_two,
    w_gu,
    w_down,
):
    row_count, own_len, width = layer_in.shape
    n_dp, n_z = lax.axis_size("dp"), lax.axis_size("tensor")
    outer = n_dp // INNER
    me, z = lax.axis_index("dp"), lax.axis_index("tensor")
    me_in = me // outer
    row_len = own_len * n_z
    channels = w_in.shape[2]
    reach = kernel.shape[0] - 1
    tokens = row_count * own_len
    block = width // INNER
    units = w_down.shape[0]
    index = jnp.stack([me_in, z]).astype(jnp.int32)

    given = lax.dynamic_slice_in_dim(row_order, me * row_count, row_count)
    starts = jnp.cumsum(row_counts) - row_counts
    ends = starts + row_counts - 1
    is_first = jnp.any(starts[None, :] == given[:, None], axis=1)
    at_end = ends[None, :] == given[:, None]
    row_valid = jnp.where(
        jnp.any(at_end, axis=1),
        jnp.sum(jnp.where(at_end, tail_tokens[None, :], 0), axis=1),
        row_len,
    )
    positions = z * own_len + jnp.arange(own_len, dtype=jnp.int32)
    valid = positions[None, :] < row_valid[:, None]

    small = jnp.concatenate([gain_one[None], gain_two[None], kernel], axis=0)
    w_b, w_c, w_u = (w_in[:, st] for st in range(3))
    mix_bu = jnp.stack([w_b, w_u])
    mix_co = jnp.stack([w_c, w_out.T])
    ffn_own = jnp.concatenate([w_gu[:, 0], w_gu[:, 1], w_down.T], axis=1)
    groups = [[i * outer + o for o in range(outer)] for i in range(INNER)]
    if outer > 1:
        wide = functools.partial(lax.all_gather, axis_name="dp", tiled=True, axis_index_groups=groups)
        mix_bu, mix_co, small = wide(mix_bu, axis=1), wide(mix_co, axis=1), wide(small, axis=1)
        ffn_own = wide(ffn_own, axis=0)
    n_small = small.shape[0]
    small_rows = jnp.pad(small, ((0, 16 - n_small), (0, channels - block)))
    bu_rows, co_rows = (m.reshape(2 * block, channels) for m in (mix_bu, mix_co))

    steps = tuple(range(1, n_z))
    tails = layer_in[:, own_len - reach :].reshape(row_count, reach * width)
    before = z_shift(tails, 1, "tail")
    every = before[None]
    if outer > 1:
        every = lax.all_gather(before, "dp", axis=0, axis_index_groups=groups)
    every = every[None]
    every = jnp.concatenate([every, dp_swap(every, 1, "tail")], axis=0)
    bu_set = z_send(bu_rows, "bu", steps)
    co_set = z_send(co_rows, "co", steps, *bu_set)
    ffn_near = plane_send(ffn_own, "ffn", (1, 2))
    d_ffn = jnp.where(valid[:, :, None], cotangent, jnp.zeros_like(cotangent)).reshape(tokens, width)

    gate = (*ffn_near, every)
    bu_rows = jnp.concatenate([bu_rows] + bu_set + [small_rows], axis=0)
    bu_set = plane_send(bu_rows, "bu", (1, 2, 3), *gate)
    dy_set = z_send(d_ffn, "dy", (1, 2), *gate, *co_set)
    every = jnp.concatenate([every, dp_swap(after(every, *gate), 2, "tail")], axis=0)

    gate = (*bu_set, *dy_set, every)
    co_rows = jnp.concatenate([co_rows] + co_set, axis=0)
    co_set = plane_send(co_rows, "co", (1, 2, 3), *gate)
    dy_set = dy_set + [z_swap(after(dy_set[1], *gate), 1, "dy_on")]
    every = jnp.concatenate([every, dp_swap(after(every, *gate), 4, "tail")], axis=0)
    slots = INNER * outer * row_count
    rel = jnp.bitwise_xor(me_in, jnp.arange(INNER, dtype=jnp.int32))
    slot_rows = row_order.reshape(INNER, outer * row_count)[rel].reshape(slots)
    before_mask = jnp.logical_and(
        slot_rows[None, :] == (given - 1)[:, None], jnp.logical_not(is_first)[:, None]
    )
    before_mask = jnp.logical_and(before_mask, z == 0).astype(BF)
    crossed = mm(before_mask, every.reshape(slots, reach * width))
    x_halo = jnp.where(z == 0, crossed.astype(BF), before).reshape(row_count * reach, width)
    x_own = layer_in.reshape(tokens, width)
    w_b, w_u, small_all = place_mixer(index, core_pairs([bu_rows] + bu_set, "bu"), width, n_z, True)
    n_one, n_halo, b_own, u_own, b_halo, u_halo, mixed, mixed_halo, conv = mixer_in(
        own_len, x_own, x_halo, small_all, w_b, w_u
    )

    gate = (*co_set, dy_set[2], n_one)
    ffn_far = plane_send(ffn_own, "ffn", (3,), *gate)
    w_c, w_o = place_mixer(index, core_pairs([co_rows] + co_set, "co"), width, n_z, False)
    c_own, gated, middle, n_two = mixer_out(x_own, n_one, conv, small_all, w_c, w_o)
    ffn_set = [ffn_own] + ffn_near + ffn_far
    w_ffn = place_ffn(index, core_pairs(ffn_set[:3], "ffn", *gate) + core_pairs(ffn_set[3:], "ffn"))
    d_ffn_set = [d_ffn] + dy_set
    n_two_set = [n_two] + z_send(n_two, "n2", (1, 2))
    n_two_set = n_two_set + z_send(n_two_set[2], "n2_on", (1,))
    d_parts, out_parts, kept = [], [], ()
    for s in range(n_z):
        d_part, out_part, *kept = ffn_piece(s, n_z, n_two_set[s], d_ffn_set[s], w_ffn, kept)
        d_parts.append(z_swap(d_part, s, "dn") if s else d_part)
        out_parts.append(out_part)

    away, home = ffn_grads(index, 0, 4, *kept)
    gf_set = core_sum(away, home, 4, "gf")
    gf_near = [dp_swap(after(gf_set[kq], d_parts[1]), 2 * kq, "gf") for kq in (1, 2)]
    d_mix, d_b, d_u, d_c, d_b_halo, d_u_halo, grad_mid, d_x_halo, small_grads = mixer_back(
        own_len,
        [after(d_parts[0], *gf_near)] + d_parts[1:],
        (middle, d_ffn, x_own, x_halo, small_all, b_own, u_own, c_own, b_halo, u_halo, mixed, mixed_halo, conv),
        (w_b, w_u, w_c, w_o),
    )
    co_away, co_home = mixer_grads(index, (n_one, d_c, d_mix, gated), n_z, block, False)
    d_bu_halo = jnp.concatenate([d_b_halo, d_u_halo], axis=1)
    co_halves = core_sum(co_away, co_home, 4, "gco")
    bu_away, bu_home = mixer_grads(
        index, (after(n_one, *co_halves), d_b, n_one, d_u, n_halo, d_bu_halo, small_grads), n_z, block, True
    )
    bu_halves = core_sum(bu_away, bu_home, 4, "gbu")

    gco_set = [dp_swap(co_halves[kq], 2 * kq, "gco") for kq in (1, 2, 3)]
    out_on = z_swap(after(out_parts[3], d_mix), 1, "out_on")
    out_first = z_swap(after(out_parts[1], d_mix), 1, "out")
    back = d_x_halo.reshape(row_count, reach * width)
    spread = mm_tn(before_mask, back).astype(BF).reshape(INNER, outer * row_count, reach * width)

    def fold(spread, step, *waits):
        arrived = dp_swap(after(spread[step:], *waits), step, "back").astype(F32)
        return (spread[:step].astype(F32) + arrived).astype(BF)

    spread = fold(spread, 4, *co_halves)
    gate = (*gco_set, out_on, out_first, spread)
    gbu_set = [dp_swap(after(bu_halves[kq], *gate), 2 * kq, "gbu") for kq in (1, 2, 3)]
    co_plane = co_halves[0].astype(F32) + sum(piece.astype(F32) for piece in gco_set)
    co_total = z_return(list(co_plane.astype(BF)), "gco")
    out_second = (out_parts[2].astype(F32) + out_on.astype(F32)).astype(BF)
    out_second = z_swap(after(out_second, *gate), 2, "out")
    layer_out = middle + out_parts[0].astype(F32) + out_first.astype(F32) + out_second.astype(F32)
    layer_out = layer_out.astype(BF).reshape(row_count, own_len, width)
    spread = fold(spread, 2, *gate)

    gate = (*gbu_set, co_total, out_second, spread)
    gf_far = dp_swap(after(gf_set[3], *gate), 6, "gf")
    ffn_total = gf_set[0].astype(F32) + sum(piece.astype(F32) for piece in (*gf_near, gf_far))
    bu_plane = bu_halves[0].astype(F32) + sum(piece.astype(F32) for piece in gbu_set)
    bu_total = z_return(list(bu_plane.astype(BF)), "gbu", *gate)
    returned = fold(spread, 1, *gate)[0]
    if outer > 1:
        returned = lax.psum_scatter(
            returned, "dp", scatter_dimension=0, tiled=True, axis_index_groups=groups
        )
    returned = z_shift(jnp.where(z == 0, returned, back), n_z - 1, "back")
    returned = returned.astype(F32).reshape(row_count, reach, width)
    grad_in = grad_mid.reshape(row_count, own_len, width)
    grad_in = grad_in + jnp.pad(returned, ((0, 0), (own_len - reach, 0), (0, 0)))

    if outer > 1:
        narrow = functools.partial(
            lax.psum_scatter, axis_name="dp", tiled=True, axis_index_groups=groups
        )
        grad_bu = narrow(bu_total[: 2 * block].reshape(2, block, channels), scatter_dimension=1)
        grad_co = narrow(co_total.reshape(2, block, channels), scatter_dimension=1)
        grad_small = narrow(bu_total[2 * block : 2 * block + n_small, :block], scatter_dimension=1)
        ffn_total = narrow(ffn_total, scatter_dimension=0)
    else:
        grad_bu = bu_total[: 2 * block].reshape(2, block, channels)
        grad_co = co_total.reshape(2, block, channels)
        grad_small = bu_total[2 * block : 2 * block + n_small, :block]
    return (
        layer_out,
        grad_in.astype(BF),
        grad_small[0],
        jnp.stack([grad_bu[0], grad_co[0], grad_bu[1]], axis=1),
        grad_small[2:],
        grad_co[1].T,
        grad_small[1],
        jnp.stack([ffn_total[:, :units], ffn_total[:, units : 2 * units]], axis=1),
        ffn_total[:, 2 * units :].T,
    )


def solution(mesh):
    in_specs = (
        P("dp", "tensor", None),
        P("dp", "tensor", None),
        P(),
        P(),
        P(),
        P("dp"),
        P("dp", None, "tensor"),
        P(None, "dp"),
        P("tensor", "dp"),
        P("dp"),
        P("dp", None, "tensor"),
        P("tensor", "dp"),
    )
    out_specs = (
        P("dp", "tensor", None),
        P("dp", "tensor", None),
        P("dp"),
        P("dp", None, "tensor"),
        P(None, "dp"),
        P("tensor", "dp"),
        P("dp"),
        P("dp", None, "tensor"),
        P("tensor", "dp"),
    )
    return jax.shard_map(body, mesh=mesh, in_specs=in_specs, out_specs=out_specs, check_vma=False)
```

```python
import functools
import jax
import jax.numpy as jnp
from jax import lax
from jax.experimental import pallas as pl
from jax.experimental.pallas import tpu as pltpu
from jax.sharding import PartitionSpec as P

EPS = 1e-05
INNER = 8
BF = jnp.bfloat16
F32 = jnp.float32
VMEM_LIMIT = 12 << 20


def dp_swap(value, step, tag):
    size = lax.axis_size("dp")
    hop = step * (size // INNER)
    with jax.named_scope(f"{tag}_dp{step}"):
        return lax.ppermute(value, "dp", [(i, i ^ hop) for i in range(size)])


def z_shift(value, step, tag):
    size = lax.axis_size("tensor")
    with jax.named_scope(f"{tag}_z"):
        return lax.ppermute(value, "tensor", [(i, (i + step) % size) for i in range(size)])


def z_swap(value, step, tag):
    size = lax.axis_size("tensor")
    with jax.named_scope(f"{tag}_z{step}"):
        return lax.ppermute(value, "tensor", [(i, i ^ step) for i in range(size)])


def after(value, *events):
    return lax.optimization_barrier((value,) + events)[0]


def mm(a, b):
    return lax.dot_general(a, b, (((1,), (0,)), ((), ())), preferred_element_type=F32)


def mm_nt(a, b):
    return lax.dot_general(a, b, (((1,), (1,)), ((), ())), preferred_element_type=F32)


def mm_tn(a, b):
    return lax.dot_general(a, b, (((0,), (0,)), ((), ())), preferred_element_type=F32)


def shape(*dims, dtype=BF):
    return jax.ShapeDtypeStruct(dims, dtype)


def whole_call(kernel, name, outs, args, scalars=0, hbm=0, scratch=(), flops=0, extra=0, alias=None):
    specs = [pl.BlockSpec(memory_space=pltpu.SMEM)] * scalars
    specs += [pl.BlockSpec(memory_space=pltpu.HBM)] * hbm
    specs += [pl.BlockSpec(memory_space=pltpu.VMEM)] * (len(args) - scalars - hbm)
    moved = sum(a.size * a.dtype.itemsize for a in args) + sum(
        o.size * jnp.dtype(o.dtype).itemsize for o in outs
    )
    return pl.pallas_call(
        kernel,
        out_shape=outs,
        in_specs=specs,
        out_specs=[pl.BlockSpec(memory_space=pltpu.VMEM)] * len(outs),
        scratch_shapes=list(scratch),
        input_output_aliases=alias or {},
        compiler_params=pltpu.CompilerParams(vmem_limit_bytes=VMEM_LIMIT),
        cost_estimate=pl.CostEstimate(flops=1, bytes_accessed=1, transcendentals=0),
        name=name,
    )(*args)


def corner(value, tag):
    size = lax.axis_size("dp")
    outer = size // INNER
    pairs = []
    for i in range(size):
        hop = 2 if (i // outer) % 2 else 4
        pairs.append((i, i ^ (hop * outer)))
    with jax.named_scope(f"{tag}_corner"):
        return lax.ppermute(value, "dp", pairs)


def core_zero():
    return lax.axis_index("dp") // (lax.axis_size("dp") // INNER) % 2 == 0


def plane_gather(local, tag, *waits):
    local = after(local, *waits) if waits else local
    return dp_swap(local, 2, tag), dp_swap(local, 4, tag)


def plane_corner(over_x, over_y, tag, *waits):
    value = jnp.where(core_zero(), over_x, over_y)
    return corner(after(value, *waits) if waits else value, tag)


def plane_sum(pieces, tag, *waits):
    far = after(pieces[3], *waits) if waits else pieces[3]
    far = corner(far, tag).astype(F32)
    first = core_zero()
    over_x = (pieces[1].astype(F32) + jnp.where(first, far, 0.0)).astype(BF)
    over_y = (pieces[2].astype(F32) + jnp.where(first, 0.0, far)).astype(BF)
    return pieces[0], dp_swap(over_x, 2, tag), dp_swap(over_y, 4, tag)


def z_send(local, tag, steps, *waits):
    local = after(local, *waits) if waits else local
    return [z_swap(local, step, tag) for step in steps]


def stack_mixer_kernel(idx_ref, small_ref, tail_ref, *refs):
    parts, out_ref = refs[:-1], refs[-1]
    z = idx_ref[1]
    rows, ch = parts[0].shape
    for s, part in enumerate(parts):
        col = pl.multiple_of(jnp.bitwise_xor(z, s) * ch, ch)
        out_ref[:rows, pl.ds(col, ch)] = part[...]
    n_small, block = small_ref.shape
    out_ref[rows : rows + n_small] = jnp.zeros((n_small, out_ref.shape[1]), BF)
    out_ref[rows : rows + n_small, :block] = small_ref[...]
    out_ref[rows + n_small :] = tail_ref[...]


def stack_mixer(index, small, tail, parts):
    rows, ch = parts[0].shape
    return whole_call(
        stack_mixer_kernel,
        "stack_mixer",
        [shape(rows + small.shape[0] + tail.shape[0], len(parts) * ch)],
        (index, small, tail, *parts),
        scalars=1,
    )[0]


def place_mixer_kernel(block, idx_ref, *refs):
    pieces, outs, sems = refs[:8], refs[8:-1], refs[-1]
    small_ref, tail_ref = outs[4], outs[5]
    me = idx_ref[0]
    n_small, n_tail = small_ref.shape[0], tail_ref.shape[0] // 8
    copies = []
    for k in range(8):
        at = pl.multiple_of(jnp.bitwise_xor(me, k) * block, block)
        for st in range(4):
            copies.append(
                pltpu.make_async_copy(
                    pieces[k].at[pl.ds(st * block, block)], outs[st].at[pl.ds(at, block)], sems.at[k, st]
                )
            )
        copies.append(
            pltpu.make_async_copy(
                pieces[k].at[pl.ds(4 * block, n_small), pl.ds(0, block)],
                small_ref.at[:, pl.ds(at, block)],
                sems.at[k, 4],
            )
        )
        copies.append(
            pltpu.make_async_copy(
                pieces[k].at[pl.ds(4 * block + n_small, n_tail)],
                tail_ref.at[pl.ds(k * n_tail, n_tail)],
                sems.at[k, 5],
            )
        )
    for copy in copies:
        copy.start()
    for copy in copies:
        copy.wait()


def place_mixer(index, pieces, block, n_small, n_tail):
    width = pieces[0].shape[1]
    return whole_call(
        functools.partial(place_mixer_kernel, block),
        "place_mixer",
        [shape(8 * block, width)] * 4 + [shape(n_small, 8 * block), shape(8 * n_tail, width)],
        (index, *pieces),
        scalars=1,
        hbm=8,
        scratch=[pltpu.SemaphoreType.DMA((8, 6))],
    )


def place_ffn_kernel(idx_ref, *refs):
    pieces, out_ref, sems = refs[:8], refs[8], refs[9]
    me = idx_ref[0]
    rows = out_ref.shape[0] // 8
    copies = []
    for k in range(8):
        at = pl.ds(pl.multiple_of(jnp.bitwise_xor(me, k) * rows, rows), rows)
        copies.append(pltpu.make_async_copy(pieces[k], out_ref.at[at], sems.at[k]))
    for copy in copies:
        copy.start()
    for copy in copies:
        copy.wait()


def place_ffn(index, pieces):
    rows, columns = pieces[0].shape
    return whole_call(
        place_ffn_kernel,
        "place_ffn",
        [shape(8 * rows, columns)],
        (index, *pieces),
        scalars=1,
        hbm=8,
        scratch=[pltpu.SemaphoreType.DMA((8,))],
    )[0]


def ffn_kernel(step, n_ref, d_ref, w_ref, *refs):
    dn_ref, part_ref, n_all_ref, d_all_ref, hid_ref, dgu_ref = refs[-6:]
    tokens = n_ref.shape[0]
    own = slice(step * tokens, (step + 1) * tokens)
    units = w_ref.shape[1] // 3
    gu, down = slice(0, 2 * units), slice(2 * units, 3 * units)
    n_all_ref[own] = n_ref[...]
    d_all_ref[own] = d_ref[...]
    both = mm(n_ref[...], w_ref[:, gu])
    gate, up = both[:, :units], both[:, units:]
    sig = jax.nn.sigmoid(gate)
    silu = gate * sig
    hidden = (silu * up).astype(BF)
    hid_ref[own] = hidden
    d_hidden = mm(d_ref[...], w_ref[:, down])
    dgu_ref[own, :units] = (d_hidden * up * (sig * (1.0 + gate * (1.0 - sig)))).astype(BF)
    dgu_ref[own, units:] = (d_hidden * silu).astype(BF)
    dn_ref[...] = mm_nt(dgu_ref[own], w_ref[:, gu]).astype(BF)
    part_ref[...] = mm_nt(hidden, w_ref[:, down]).astype(BF)


def ffn_piece(step, steps, normed, d_out, weights, kept):
    tokens, width = normed.shape
    units = weights.shape[1] // 3
    every = steps * tokens
    return whole_call(
        functools.partial(ffn_kernel, step),
        "ffn_piece",
        [shape(tokens, width)] * 2
        + [shape(every, width), shape(every, width), shape(every, units), shape(every, 2 * units)],
        (normed, d_out, weights, *kept),
        flops=12 * tokens * width * units,
        extra=tokens * units,
        alias={3 + i: 2 + i for i in range(len(kept))},
    )


def norm_scale(value):
    return lax.rsqrt(jnp.mean(value * value, axis=-1, keepdims=True) + EPS)


def norm_back(d_normed, value, scale, gain):
    weighted = d_normed * gain
    d_value = scale * weighted - value * (scale * scale * scale) * jnp.mean(
        weighted * value, axis=-1, keepdims=True
    )
    return d_value, jnp.sum(d_normed * value * scale, axis=0, keepdims=True)


def halo_picks(tokens, own_len, halo):
    token = lax.broadcasted_iota(jnp.int32, (tokens, halo), 0)
    slot = lax.broadcasted_iota(jnp.int32, (tokens, halo), 1)
    run, pos = token // own_len, token % own_len
    one = jnp.logical_and(pos == 0, slot == 2 * run + 1)
    two = jnp.logical_and(pos < 2, slot == 2 * run + pos)
    return one.astype(BF), two.astype(BF)


def earlier(mixed, mixed_halo, own_len):
    tokens = mixed.shape[0]
    pick_one, pick_two = halo_picks(tokens, own_len, mixed_halo.shape[0])
    pos = lax.broadcasted_iota(jnp.int32, mixed.shape, 0) % own_len
    one = jnp.where(pos == 0, mm(pick_one, mixed_halo), pltpu.roll(mixed, 1, axis=0))
    two = jnp.where(pos < 2, mm(pick_two, mixed_halo), pltpu.roll(mixed, 2, axis=0))
    return one, two


def mixer_in_kernel(
    own_len, x_ref, xh_ref, small_ref, wb_ref, wu_ref, n_ref, nh_ref, b_ref, u_ref, bh_ref, uh_ref, mix_ref, mixh_ref, conv_ref
):
    gain = small_ref[0:1].astype(F32)
    x, xh = x_ref[...].astype(F32), xh_ref[...].astype(F32)
    n_ref[...] = (x * norm_scale(x) * gain).astype(BF)
    nh_ref[...] = (xh * norm_scale(xh) * gain).astype(BF)
    b_ref[...] = mm(n_ref[...], wb_ref[...])
    u_ref[...] = mm(n_ref[...], wu_ref[...])
    bh_ref[...] = mm(nh_ref[...], wb_ref[...])
    uh_ref[...] = mm(nh_ref[...], wu_ref[...])
    mix_ref[...] = (b_ref[...] * u_ref[...]).astype(BF)
    mixh_ref[...] = (bh_ref[...] * uh_ref[...]).astype(BF)
    mixed = mix_ref[...].astype(F32)
    one, two = earlier(mixed, mixh_ref[...], own_len)
    taps = [small_ref[2 + k : 3 + k].astype(F32) for k in range(3)]
    conv_ref[...] = taps[0] * two + taps[1] * one + taps[2] * mixed


def mixer_in(own_len, x, x_halo, small, w_b, w_u):
    (tokens, width), halo, ch = x.shape, x_halo.shape[0], w_b.shape[1]
    return whole_call(
        functools.partial(mixer_in_kernel, own_len),
        "mixer_in",
        [
            shape(tokens, width),
            shape(halo, width),
            shape(tokens, ch, dtype=F32),
            shape(tokens, ch, dtype=F32),
            shape(halo, ch, dtype=F32),
            shape(halo, ch, dtype=F32),
            shape(tokens, ch),
            shape(halo, ch),
            shape(tokens, ch, dtype=F32),
        ],
        (x, x_halo, small, w_b, w_u),
        flops=4 * tokens * width * ch,
    )


def mixer_out_kernel(x_ref, n_ref, conv_ref, small_ref, wc_ref, wo_ref, c_ref, gated_ref, mid_ref, n2_ref):
    c_ref[...] = mm(n_ref[...], wc_ref[...])
    gated_ref[...] = (c_ref[...] * conv_ref[...]).astype(BF)
    mid = x_ref[...].astype(F32) + mm_nt(gated_ref[...], wo_ref[...])
    mid_ref[...] = mid
    n2_ref[...] = (mid * norm_scale(mid) * small_ref[1:2].astype(F32)).astype(BF)


def mixer_out(x, n_one, conv, small, w_c, w_o):
    (tokens, width), ch = x.shape, w_c.shape[1]
    return whole_call(
        mixer_out_kernel,
        "mixer_out",
        [
            shape(tokens, ch, dtype=F32),
            shape(tokens, ch),
            shape(tokens, width, dtype=F32),
            shape(tokens, width),
        ],
        (x, n_one, conv, small, w_c, w_o),
        flops=4 * tokens * width * ch,
    )


def mixer_back_kernel(own_len, n_parts, *refs):
    parts = refs[:n_parts]
    (mid_ref, dy_ref, x_ref, xh_ref, small_ref, b_ref, u_ref, c_ref, bh_ref, uh_ref, mix_ref, mixh_ref, conv_ref) = refs[
        n_parts : n_parts + 13
    ]
    wb_ref, wu_ref, wc_ref, wo_ref = refs[n_parts + 13 : n_parts + 17]
    dmix_ref, db_ref, du_ref, dc_ref, dbh_ref, duh_ref, gin_ref, dxh_ref, sg_ref = refs[n_parts + 17 :]
    gain_one, gain_two = small_ref[0:1].astype(F32), small_ref[1:2].astype(F32)
    taps = [small_ref[2 + k : 3 + k].astype(F32) for k in range(3)]
    d_n2 = parts[0][...].astype(F32)
    for part in parts[1:]:
        d_n2 = d_n2 + part[...].astype(F32)
    mid = mid_ref[...]
    d_mid, g_two = norm_back(d_n2, mid, norm_scale(mid), gain_two)
    d_mid = d_mid + dy_ref[...].astype(F32)
    dmix_ref[...] = d_mid.astype(BF)
    d_gated = mm(dmix_ref[...], wo_ref[...])
    dc_ref[...] = (d_gated * conv_ref[...]).astype(BF)
    d_conv = d_gated * c_ref[...]
    mixed = mix_ref[...].astype(F32)
    one, two = earlier(mixed, mixh_ref[...], own_len)
    tap_rows = [jnp.sum(d_conv * view, axis=0, keepdims=True) for view in (two, one, mixed)]
    tokens = mixed.shape[0]
    pos = lax.broadcasted_iota(jnp.int32, mixed.shape, 0) % own_len
    d_mixed = taps[2] * d_conv
    d_mixed = d_mixed + taps[1] * jnp.where(pos < own_len - 1, pltpu.roll(d_conv, tokens - 1, axis=0), 0.0)
    d_mixed = d_mixed + taps[0] * jnp.where(pos < own_len - 2, pltpu.roll(d_conv, tokens - 2, axis=0), 0.0)
    db_ref[...] = (d_mixed * u_ref[...]).astype(BF)
    du_ref[...] = (d_mixed * b_ref[...]).astype(BF)
    pick_one, pick_two = halo_picks(tokens, own_len, mixh_ref.shape[0])
    low = d_conv.astype(BF)
    d_halo = taps[1] * mm_tn(pick_one, low) + taps[0] * mm_tn(pick_two, low)
    dbh_ref[...] = (d_halo * uh_ref[...]).astype(BF)
    duh_ref[...] = (d_halo * bh_ref[...]).astype(BF)
    d_n1 = mm_nt(db_ref[...], wb_ref[...]) + mm_nt(du_ref[...], wu_ref[...]) + mm_nt(dc_ref[...], wc_ref[...])
    x, xh = x_ref[...].astype(F32), xh_ref[...].astype(F32)
    d_x, g_one = norm_back(d_n1, x, norm_scale(x), gain_one)
    gin_ref[...] = d_x + d_mid
    d_nh = mm_nt(dbh_ref[...], wb_ref[...]) + mm_nt(duh_ref[...], wu_ref[...])
    d_xh, g_halo = norm_back(d_nh, xh, norm_scale(xh), gain_one)
    dxh_ref[...] = d_xh.astype(BF)
    for row, value in enumerate([g_one + g_halo, g_two] + tap_rows):
        sg_ref[row : row + 1] = value
    sg_ref[5:8] = jnp.zeros((3, sg_ref.shape[1]), F32)


def mixer_back(own_len, parts, saved, weights):
    (tokens, width), ch = parts[0].shape, weights[0].shape[1]
    halo = saved[3].shape[0]
    return whole_call(
        functools.partial(mixer_back_kernel, own_len, len(parts)),
        "mixer_back",
        [shape(tokens, width)]
        + [shape(tokens, ch)] * 3
        + [shape(halo, ch)] * 2
        + [shape(tokens, width, dtype=F32), shape(halo, width), shape(8, width, dtype=F32)],
        (*parts, *saved, *weights),
        flops=8 * tokens * width * ch,
    )


def mixer_grad_kernel(with_halo, idx_ref, *refs):
    n_in = 8 if with_halo else 4
    ins, away_ref, home_ref = refs[:n_in], refs[n_in], refs[n_in + 1]
    me = idx_ref[0]
    quad, core = me // 2, lax.rem(me, 2)
    width = away_ref.shape[2]
    rows = ins[0].shape[1] // 8

    @pl.loop(0, 4)
    def _(kq):
        chip = jnp.bitwise_xor(quad, kq) * 2
        away = pl.multiple_of((chip + 1 - core) * rows, rows)
        home = pl.multiple_of((chip + core) * rows, rows)
        for st in range(2):
            left_ref, right_ref = ins[2 * st], ins[2 * st + 1]
            left = jnp.concatenate([left_ref[:, pl.ds(away, rows)], left_ref[:, pl.ds(home, rows)]], axis=1)
            grad = mm_tn(left, right_ref[...])
            if with_halo:
                nh_ref = ins[4]
                left = jnp.concatenate([nh_ref[:, pl.ds(away, rows)], nh_ref[:, pl.ds(home, rows)]], axis=1)
                grad = grad + mm_tn(left, ins[5][:, st * width : (st + 1) * width])
            grad = grad.astype(BF)
            away_ref[kq, st * rows : (st + 1) * rows] = grad[:rows]
            home_ref[kq, st * rows : (st + 1) * rows] = grad[rows:]
        if with_halo:
            n_tail = ins[7].shape[0] // 8
            for ref, at, k in ((away_ref, away, 2 * kq + 1), (home_ref, home, 2 * kq)):
                values = ins[6][:, pl.ds(at, rows)]
                values = jnp.concatenate([values, jnp.zeros_like(values)], axis=0)
                ref[kq, 2 * rows : 2 * rows + 16] = jnp.zeros((16, width), BF)
                ref[kq, 2 * rows : 2 * rows + 16, :rows] = values.astype(BF)
                ref[kq, 2 * rows + 16 :] = ins[7][pl.ds(pl.multiple_of(k * n_tail, n_tail), n_tail)]


def mixer_grads(index, ins, rows, with_halo):
    extra = 16 + ins[7].shape[0] // 8 if with_halo else 0
    return whole_call(
        functools.partial(mixer_grad_kernel, with_halo),
        "grads_in" if with_halo else "grads_out",
        [shape(4, 2 * rows + extra, ins[1].shape[1])] * 2,
        (index, *ins),
        scalars=1,
    )


def split_kernel(rows, idx_ref, *refs):
    terms, outs = refs[:3], refs[3:]
    z = idx_ref[1]
    n_z = len(outs)
    ch = terms[0].shape[1] // n_z
    n_tail = terms[0].shape[0] - rows - 16
    ahead = jnp.bitwise_xor(z, lax.rem(z + n_z - 1, n_z))

    def total(at, col):
        return sum(term[at, col].astype(F32) for term in terms).astype(BF)

    for s, out in enumerate(outs):
        out[:rows] = total(slice(0, rows), pl.ds(pl.multiple_of(jnp.bitwise_xor(z, s) * ch, ch), ch))
        if n_tail > 0:
            out[rows : rows + 16] = total(slice(rows, rows + 16), slice(0, ch))
            for c in range(n_z):
                value = total(slice(rows + 16, rows + 16 + n_tail), slice(c * ch, (c + 1) * ch))
                at = rows + 16 + c * n_tail
                out[at : at + n_tail] = jnp.where(ahead == s, value, jnp.zeros_like(value))


def split_z(index, terms, rows, n_z):
    every, width = terms[0].shape
    extra = 16 + (every - rows - 16) * n_z if every > rows else 0
    return whole_call(
        functools.partial(split_kernel, rows),
        "split_z",
        [shape(rows + extra, width // n_z)] * n_z,
        (index, *terms),
        scalars=1,
    )


def ffn_grad_kernel(first, count, idx_ref, n_ref, d_ref, hid_ref, dgu_ref, away_ref, home_ref):
    me = idx_ref[0]
    quad, core = me // 2, lax.rem(me, 2)
    rows = n_ref.shape[1] // 8
    split = dgu_ref.shape[1]

    @pl.loop(0, count)
    def _(i):
        chip = jnp.bitwise_xor(quad, first + i) * 2
        away = pl.multiple_of((chip + 1 - core) * rows, rows)
        home = pl.multiple_of((chip + core) * rows, rows)
        left = jnp.concatenate([n_ref[:, pl.ds(away, rows)], n_ref[:, pl.ds(home, rows)]], axis=1)
        grad = mm_tn(left, dgu_ref[...]).astype(BF)
        away_ref[i, :, :split] = grad[:rows]
        home_ref[i, :, :split] = grad[rows:]
        left = jnp.concatenate([d_ref[:, pl.ds(away, rows)], d_ref[:, pl.ds(home, rows)]], axis=1)
        grad = mm_tn(left, hid_ref[...]).astype(BF)
        away_ref[i, :, split:] = grad[:rows]
        home_ref[i, :, split:] = grad[rows:]


def ffn_grads(index, first, count, n_all, d_all, hid_all, dgu_all):
    rows = n_all.shape[1] // 8
    columns = hid_all.shape[1] + dgu_all.shape[1]
    return whole_call(
        functools.partial(ffn_grad_kernel, first, count),
        "ffn_grads",
        [shape(count, rows, columns)] * 2,
        (index, n_all, d_all, hid_all, dgu_all),
        scalars=1,
        flops=count * 4 * rows * n_all.shape[0] * columns,
    )


def core_sum(away, home, count, tag):
    other = dp_swap(away, 1, tag)
    return [(home[kq].astype(F32) + other[kq].astype(F32)).astype(BF) for kq in range(count)]


def body(
    layer_in,
    cotangent,
    row_counts,
    tail_tokens,
    row_order,
    gain_one,
    w_in,
    kernel,
    w_out,
    gain_two,
    w_gu,
    w_down,
):
    row_count, own_len, width = layer_in.shape
    n_dp, n_z = lax.axis_size("dp"), lax.axis_size("tensor")
    outer = n_dp // INNER
    me, z = lax.axis_index("dp"), lax.axis_index("tensor")
    me_in = me // outer
    row_len = own_len * n_z
    channels = w_in.shape[2]
    reach = kernel.shape[0] - 1
    tokens = row_count * own_len
    block = width // INNER
    units = w_down.shape[0]
    index = jnp.stack([me_in, z]).astype(jnp.int32)

    given = lax.dynamic_slice_in_dim(row_order, me * row_count, row_count)
    starts = jnp.cumsum(row_counts) - row_counts
    ends = starts + row_counts - 1
    is_first = jnp.any(starts[None, :] == given[:, None], axis=1)
    at_end = ends[None, :] == given[:, None]
    row_valid = jnp.where(
        jnp.any(at_end, axis=1),
        jnp.sum(jnp.where(at_end, tail_tokens[None, :], 0), axis=1),
        row_len,
    )
    positions = z * own_len + jnp.arange(own_len, dtype=jnp.int32)
    valid = positions[None, :] < row_valid[:, None]

    small = jnp.concatenate([gain_one[None], gain_two[None], kernel], axis=0)
    mix_own = jnp.stack([w_in[:, 0], w_in[:, 2], w_in[:, 1], w_out.T])
    ffn_own = jnp.concatenate([w_gu[:, 0], w_gu[:, 1], w_down.T], axis=1)
    groups = [[i * outer + o for o in range(outer)] for i in range(INNER)]
    tails = layer_in[:, own_len - reach :].reshape(row_count * reach, width)
    tails = z_shift(tails, 1, "tail")
    if outer > 1:
        wide = functools.partial(lax.all_gather, axis_name="dp", tiled=True, axis_index_groups=groups)
        mix_own, small = wide(mix_own, axis=1), wide(small, axis=1)
        ffn_own, tails = wide(ffn_own, axis=0), wide(tails, axis=0)
    n_small = small.shape[0]
    small = jnp.pad(small, ((0, 16 - n_small), (0, 0)))
    mix_own = mix_own.reshape(4 * block, channels)

    mix_far, mix_near = z_send(mix_own, "mix", (2, 1))
    ffn_x, ffn_y = plane_gather(ffn_own, "ffn")
    mix_last = z_swap(mix_far, 1, "mix_on")
    d_ffn = jnp.where(valid[:, :, None], cotangent, jnp.zeros_like(cotangent)).reshape(tokens, width)
    mix_rows = stack_mixer(index, small, tails, [mix_own, mix_near, mix_far, mix_last])

    mix_x, mix_y = plane_gather(mix_rows, "mix")
    dy_far, dy_near = z_send(d_ffn, "dy", (2, 1), mix_last)
    gate = (ffn_x, ffn_y)
    mix_pairs = [mix_rows, dp_swap(after(mix_rows, *gate), 1, "mix")]
    ffn_pairs = [ffn_own, dp_swap(after(ffn_own, mix_pairs[1]), 1, "ffn")]
    ffn_pairs += [ffn_x, dp_swap(after(ffn_x, ffn_pairs[1]), 1, "ffn")]
    ffn_pairs += [ffn_y, dp_swap(after(ffn_y, ffn_pairs[3]), 1, "ffn")]
    mix_d = plane_corner(mix_x, mix_y, "mix")
    dy_set = [dy_near, dy_far, z_swap(dy_far, 1, "dy_on")]
    mix_pairs += [mix_x, dp_swap(mix_x, 1, "mix"), mix_y, dp_swap(mix_y, 1, "mix")]
    mix_pairs += [mix_d, dp_swap(mix_d, 1, "mix")]
    w_b, w_u, w_c, w_o, small_all, every = place_mixer(index, mix_pairs, block, 16, tails.shape[0])

    slots = INNER * outer * row_count
    rel = jnp.bitwise_xor(me_in, jnp.arange(INNER, dtype=jnp.int32))
    slot_rows = row_order.reshape(INNER, outer * row_count)[rel].reshape(slots)
    wanted = jnp.where(z == 0, jnp.where(is_first, -1, given - 1), given)
    picks = jnp.repeat(wanted, reach)[:, None] == jnp.repeat(slot_rows, reach)[None, :]
    picks = jnp.logical_and(
        picks, jnp.arange(row_count * reach)[:, None] % reach == jnp.arange(slots * reach)[None, :] % reach
    ).astype(BF)
    x_halo = mm(picks, every).astype(BF)
    x_own = layer_in.reshape(tokens, width)
    n_one, n_halo, b_own, u_own, b_halo, u_halo, mixed, mixed_halo, conv = mixer_in(
        own_len, x_own, x_halo, small_all, w_b, w_u
    )
    c_own, gated, middle, n_two = mixer_out(x_own, n_one, conv, small_all, w_c, w_o)

    ffn_d = plane_corner(ffn_x, ffn_y, "ffn", mix_d)
    n_two_far, n_two_near = z_send(n_two, "n2", (2, 1), dy_set[2])
    n_two_set = [n_two, n_two_near, n_two_far, z_swap(n_two_far, 1, "n2_on")]
    ffn_pairs += [ffn_d, dp_swap(ffn_d, 1, "ffn")]
    w_ffn = place_ffn(index, ffn_pairs)
    d_ffn_set = [d_ffn] + dy_set
    d_parts, out_parts, kept = [], [], ()
    for s in range(n_z):
        d_part, out_part, *kept = ffn_piece(s, n_z, n_two_set[s], d_ffn_set[s], w_ffn, kept)
        d_parts.append(d_part)
        out_parts.append(out_part)
    d_far = [z_swap(d_parts[s], s, "dn") for s in (2, 3)]
    d_near = z_swap(after(d_parts[1], n_two_set[3]), 1, "dn")
    d_parts = [d_parts[0], d_near] + d_far

    away, home = ffn_grads(index, 0, 4, *kept)
    ffn_terms = plane_sum(core_sum(away, home, 4, "gf"), "gf")
    d_mix, d_b, d_u, d_c, d_b_halo, d_u_halo, grad_mid, d_x_halo, small_grads = mixer_back(
        own_len,
        d_parts,
        (middle, d_ffn, x_own, x_halo, small_all, b_own, u_own, c_own, b_halo, u_halo, mixed, mixed_halo, conv),
        (w_b, w_u, w_c, w_o),
    )

    co_away, co_home = mixer_grads(index, (n_one, d_c, d_mix, gated), block, False)
    d_bu_halo = jnp.concatenate([d_b_halo, d_u_halo], axis=1)
    spread = mm_tn(picks, d_x_halo).astype(BF)
    bu_away, bu_home = mixer_grads(
        index, (n_one, d_b, n_one, d_u, n_halo, d_bu_halo, small_grads, spread), block, True
    )
    out_on = z_swap(after(out_parts[3], *d_parts), 1, "out_on")
    out_first = z_swap(after(out_parts[1], *d_parts), 1, "out")
    co_terms = plane_sum(core_sum(co_away, co_home, 4, "gco"), "gco")
    bu_terms = plane_sum(core_sum(bu_away, bu_home, 4, "gbu"), "gbu")
    out_second = (out_parts[2].astype(F32) + out_on.astype(F32)).astype(BF)
    out_second = z_swap(out_second, 2, "out")
    layer_out = middle + out_parts[0].astype(F32) + out_first.astype(F32) + out_second.astype(F32)
    layer_out = layer_out.astype(BF).reshape(row_count, own_len, width)

    def z_total(terms, tag):
        parts = split_z(index, terms, 2 * block, n_z)
        return parts[0].astype(F32) + sum(z_swap(parts[s], s, tag).astype(F32) for s in range(1, n_z))

    co_total = z_total(co_terms, "gco")
    bu_total = z_total(bu_terms, "gbu")
    ffn_total = sum(term.astype(F32) for term in ffn_terms)
    grad_bu = bu_total[: 2 * block].reshape(2, block, channels)
    grad_co = co_total.reshape(2, block, channels)
    grad_small = bu_total[2 * block : 2 * block + n_small, :block]
    returned = bu_total[2 * block + 16 :].reshape(n_z, -1, channels)
    returned = jnp.moveaxis(returned, 0, 1).reshape(-1, width)
    if outer > 1:
        narrow = functools.partial(
            lax.psum_scatter, axis_name="dp", tiled=True, axis_index_groups=groups
        )
        grad_bu, grad_co = narrow(grad_bu, scatter_dimension=1), narrow(grad_co, scatter_dimension=1)
        grad_small = narrow(grad_small, scatter_dimension=1)
        ffn_total, returned = narrow(ffn_total, scatter_dimension=0), narrow(returned, scatter_dimension=0)
    grad_in = grad_mid.reshape(row_count, own_len, width)
    grad_in = grad_in + jnp.pad(
        returned.reshape(row_count, reach, width), ((0, 0), (own_len - reach, 0), (0, 0))
    )
    return (
        layer_out,
        grad_in.astype(BF),
        grad_small[0],
        jnp.stack([grad_bu[0], grad_co[0], grad_bu[1]], axis=1),
        grad_small[2:],
        grad_co[1].T,
        grad_small[1],
        jnp.stack([ffn_total[:, :units], ffn_total[:, units : 2 * units]], axis=1),
        ffn_total[:, 2 * units :].T,
    )


def solution(mesh):
    in_specs = (
        P("dp", "tensor", None),
        P("dp", "tensor", None),
        P(),
        P(),
        P(),
        P("dp"),
        P("dp", None, "tensor"),
        P(None, "dp"),
        P("tensor", "dp"),
        P("dp"),
        P("dp", None, "tensor"),
        P("tensor", "dp"),
    )
    out_specs = (
        P("dp", "tensor", None),
        P("dp", "tensor", None),
        P("dp"),
        P("dp", None, "tensor"),
        P(None, "dp"),
        P("tensor", "dp"),
        P("dp"),
        P("dp", None, "tensor"),
        P("tensor", "dp"),
    )
    return jax.shard_map(body, mesh=mesh, in_specs=in_specs, out_specs=out_specs, check_vma=False)
```

```python
import functools
import jax
import jax.numpy as jnp
from jax import lax
from jax.experimental import pallas as pl
from jax.experimental.pallas import tpu as pltpu
from jax.sharding import PartitionSpec as P

EPS = 1e-05
INNER = 8
BF = jnp.bfloat16
F32 = jnp.float32
VMEM_LIMIT = 12 << 20


def hold_kernel(*refs):
    pass


def hold(value, *events):
    anywhere = pl.BlockSpec(memory_space=pl.ANY)
    return pl.pallas_call(
        hold_kernel,
        out_shape=shape(*value.shape, dtype=value.dtype),
        in_specs=[anywhere] * (1 + len(events)),
        out_specs=anywhere,
        input_output_aliases={0: 0},
        cost_estimate=pl.CostEstimate(flops=1, bytes_accessed=1, transcendentals=0),
        name="hold",
    )(value, *events)


def dp_swap(value, step, tag):
    size = lax.axis_size("dp")
    hop = step * (size // INNER)
    with jax.named_scope(f"{tag}_dp{step}"):
        return lax.ppermute(value, "dp", [(i, i ^ hop) for i in range(size)])


def z_shift(value, step, tag):
    size = lax.axis_size("tensor")
    with jax.named_scope(f"{tag}_z"):
        return lax.ppermute(value, "tensor", [(i, (i + step) % size) for i in range(size)])


def z_swap(value, step, tag):
    size = lax.axis_size("tensor")
    with jax.named_scope(f"{tag}_z{step}"):
        return lax.ppermute(value, "tensor", [(i, i ^ step) for i in range(size)])


def after(value, *events):
    return lax.optimization_barrier((value,) + events)[0]


def mm(a, b):
    return lax.dot_general(a, b, (((1,), (0,)), ((), ())), preferred_element_type=F32)


def mm_nt(a, b):
    return lax.dot_general(a, b, (((1,), (1,)), ((), ())), preferred_element_type=F32)


def mm_tn(a, b):
    return lax.dot_general(a, b, (((0,), (0,)), ((), ())), preferred_element_type=F32)


def shape(*dims, dtype=BF):
    return jax.ShapeDtypeStruct(dims, dtype)


def whole_call(kernel, name, outs, args, scalars=0, hbm=0, scratch=(), alias=None, weight=0):
    specs = [pl.BlockSpec(memory_space=pltpu.SMEM)] * scalars
    specs += [pl.BlockSpec(memory_space=pltpu.HBM)] * hbm
    specs += [pl.BlockSpec(memory_space=pltpu.VMEM)] * (len(args) - scalars - hbm)
    return pl.pallas_call(
        kernel,
        out_shape=outs,
        in_specs=specs,
        out_specs=[pl.BlockSpec(memory_space=pltpu.VMEM)] * len(outs),
        scratch_shapes=list(scratch),
        input_output_aliases=alias or {},
        compiler_params=pltpu.CompilerParams(vmem_limit_bytes=VMEM_LIMIT),
        cost_estimate=pl.CostEstimate(flops=1 + weight, bytes_accessed=1, transcendentals=0),
        name=name,
    )(*args)


def corner(value, tag):
    size = lax.axis_size("dp")
    outer = size // INNER
    pairs = []
    for i in range(size):
        hop = 2 if (i // outer) % 2 else 4
        pairs.append((i, i ^ (hop * outer)))
    with jax.named_scope(f"{tag}_corner"):
        return lax.ppermute(value, "dp", pairs)


def core_zero():
    return lax.axis_index("dp") // (lax.axis_size("dp") // INNER) % 2 == 0


def plane_gather(local, tag, *waits):
    local = after(local, *waits) if waits else local
    return dp_swap(local, 2, tag), dp_swap(local, 4, tag)


def plane_corner(over_x, over_y, tag, *waits):
    value = jnp.where(core_zero(), over_x, over_y)
    return corner(after(value, *waits) if waits else value, tag)


def plane_far(pieces, tag, *waits):
    far = hold(pieces[3], *waits) if waits else pieces[3]
    return corner(far, tag)


def plane_near(pieces, far, tag, *waits):
    far = far.astype(F32)
    first = core_zero()
    over_x = (pieces[1].astype(F32) + jnp.where(first, far, 0.0)).astype(BF)
    over_y = (pieces[2].astype(F32) + jnp.where(first, 0.0, far)).astype(BF)
    if waits:
        over_x, over_y = after(over_x, *waits), after(over_y, *waits)
    return pieces[0], dp_swap(over_x, 2, tag), dp_swap(over_y, 4, tag)


def z_send(local, tag, steps, *waits):
    local = after(local, *waits) if waits else local
    return [z_swap(local, step, tag) for step in steps]


def stack_mixer_kernel(idx_ref, small_ref, tail_ref, *refs):
    parts, out_ref = refs[:-1], refs[-1]
    z = idx_ref[1]
    rows, ch = parts[0].shape
    for s, part in enumerate(parts):
        col = pl.multiple_of(jnp.bitwise_xor(z, s) * ch, ch)
        out_ref[:rows, pl.ds(col, ch)] = part[...]
    n_small, block = small_ref.shape
    out_ref[rows : rows + n_small] = jnp.zeros((n_small, out_ref.shape[1]), BF)
    out_ref[rows : rows + n_small, :block] = small_ref[...]
    out_ref[rows + n_small :] = tail_ref[...]


def stack_mixer(index, small, tail, parts):
    rows, ch = parts[0].shape
    return whole_call(
        stack_mixer_kernel,
        "stack_mixer",
        [shape(rows + small.shape[0] + tail.shape[0], len(parts) * ch)],
        (index, small, tail, *parts),
        scalars=1,
    )[0]


def place_mixer_kernel(block, idx_ref, *refs):
    pieces, outs, sems = refs[:8], refs[8:-1], refs[-1]
    small_ref, tail_ref = outs[4], outs[5]
    me = idx_ref[0]
    n_small, n_tail = small_ref.shape[0], tail_ref.shape[0] // 8
    copies = []
    for k in range(8):
        at = pl.multiple_of(jnp.bitwise_xor(me, k) * block, block)
        for st in range(4):
            copies.append(
                pltpu.make_async_copy(
                    pieces[k].at[pl.ds(st * block, block)], outs[st].at[pl.ds(at, block)], sems.at[k, st]
                )
            )
        copies.append(
            pltpu.make_async_copy(
                pieces[k].at[pl.ds(4 * block, n_small), pl.ds(0, block)],
                small_ref.at[:, pl.ds(at, block)],
                sems.at[k, 4],
            )
        )
        copies.append(
            pltpu.make_async_copy(
                pieces[k].at[pl.ds(4 * block + n_small, n_tail)],
                tail_ref.at[pl.ds(k * n_tail, n_tail)],
                sems.at[k, 5],
            )
        )
    for copy in copies:
        copy.start()
    for copy in copies:
        copy.wait()


def place_mixer(index, pieces, block, n_small, n_tail):
    width = pieces[0].shape[1]
    return whole_call(
        functools.partial(place_mixer_kernel, block),
        "place_mixer",
        [shape(8 * block, width)] * 4 + [shape(n_small, 8 * block), shape(8 * n_tail, width)],
        (index, *pieces),
        scalars=1,
        hbm=8,
        scratch=[pltpu.SemaphoreType.DMA((8, 6))],
    )


def place_ffn_kernel(idx_ref, *refs):
    pieces, out_ref, sems = refs[:8], refs[8], refs[9]
    me = idx_ref[0]
    rows = out_ref.shape[0] // 8
    copies = []
    for k in range(8):
        at = pl.ds(pl.multiple_of(jnp.bitwise_xor(me, k) * rows, rows), rows)
        copies.append(pltpu.make_async_copy(pieces[k], out_ref.at[at], sems.at[k]))
    for copy in copies:
        copy.start()
    for copy in copies:
        copy.wait()


def place_ffn(index, pieces):
    rows, columns = pieces[0].shape
    return whole_call(
        place_ffn_kernel,
        "place_ffn",
        [shape(8 * rows, columns)],
        (index, *pieces),
        scalars=1,
        hbm=8,
        scratch=[pltpu.SemaphoreType.DMA((8,))],
    )[0]


def ffn_kernel(step, n_ref, d_ref, w_ref, *refs):
    dn_ref, part_ref, n_all_ref, d_all_ref, hid_ref, dgu_ref = refs[-6:]
    tokens = n_ref.shape[0]
    own = slice(step * tokens, (step + 1) * tokens)
    units = w_ref.shape[1] // 3
    gu, down = slice(0, 2 * units), slice(2 * units, 3 * units)
    n_all_ref[own] = n_ref[...]
    d_all_ref[own] = d_ref[...]
    both = mm(n_ref[...], w_ref[:, gu])
    gate, up = both[:, :units], both[:, units:]
    sig = jax.nn.sigmoid(gate)
    silu = gate * sig
    hidden = (silu * up).astype(BF)
    hid_ref[own] = hidden
    d_hidden = mm(d_ref[...], w_ref[:, down])
    dgu_ref[own, :units] = (d_hidden * up * (sig * (1.0 + gate * (1.0 - sig)))).astype(BF)
    dgu_ref[own, units:] = (d_hidden * silu).astype(BF)
    dn_ref[...] = mm_nt(dgu_ref[own], w_ref[:, gu]).astype(BF)
    part_ref[...] = mm_nt(hidden, w_ref[:, down]).astype(BF)


def ffn_piece(step, steps, normed, d_out, weights, kept):
    tokens, width = normed.shape
    units = weights.shape[1] // 3
    every = steps * tokens
    return whole_call(
        functools.partial(ffn_kernel, step),
        "ffn_piece",
        [shape(tokens, width)] * 2
        + [shape(every, width), shape(every, width), shape(every, units), shape(every, 2 * units)],
        (normed, d_out, weights, *kept),
        alias={3 + i: 2 + i for i in range(len(kept))},
    )


def norm_scale(value):
    return lax.rsqrt(jnp.mean(value * value, axis=-1, keepdims=True) + EPS)


def norm_back(d_normed, value, scale, gain):
    weighted = d_normed * gain
    d_value = scale * weighted - value * (scale * scale * scale) * jnp.mean(
        weighted * value, axis=-1, keepdims=True
    )
    return d_value, jnp.sum(d_normed * value * scale, axis=0, keepdims=True)


def halo_picks(tokens, own_len, halo):
    token = lax.broadcasted_iota(jnp.int32, (tokens, halo), 0)
    slot = lax.broadcasted_iota(jnp.int32, (tokens, halo), 1)
    run, pos = token // own_len, token % own_len
    one = jnp.logical_and(pos == 0, slot == 2 * run + 1)
    two = jnp.logical_and(pos < 2, slot == 2 * run + pos)
    return one.astype(BF), two.astype(BF)


def earlier(mixed, mixed_halo, own_len):
    tokens = mixed.shape[0]
    pick_one, pick_two = halo_picks(tokens, own_len, mixed_halo.shape[0])
    pos = lax.broadcasted_iota(jnp.int32, mixed.shape, 0) % own_len
    one = jnp.where(pos == 0, mm(pick_one, mixed_halo), pltpu.roll(mixed, 1, axis=0))
    two = jnp.where(pos < 2, mm(pick_two, mixed_halo), pltpu.roll(mixed, 2, axis=0))
    return one, two


def mixer_in_kernel(
    own_len, x_ref, xh_ref, small_ref, wb_ref, wu_ref, n_ref, nh_ref, b_ref, u_ref, bh_ref, uh_ref, mix_ref, mixh_ref, conv_ref
):
    gain = small_ref[0:1].astype(F32)
    x, xh = x_ref[...].astype(F32), xh_ref[...].astype(F32)
    n_ref[...] = (x * norm_scale(x) * gain).astype(BF)
    nh_ref[...] = (xh * norm_scale(xh) * gain).astype(BF)
    b_ref[...] = mm(n_ref[...], wb_ref[...])
    u_ref[...] = mm(n_ref[...], wu_ref[...])
    bh_ref[...] = mm(nh_ref[...], wb_ref[...])
    uh_ref[...] = mm(nh_ref[...], wu_ref[...])
    mix_ref[...] = (b_ref[...] * u_ref[...]).astype(BF)
    mixh_ref[...] = (bh_ref[...] * uh_ref[...]).astype(BF)
    mixed = mix_ref[...].astype(F32)
    one, two = earlier(mixed, mixh_ref[...], own_len)
    taps = [small_ref[2 + k : 3 + k].astype(F32) for k in range(3)]
    conv_ref[...] = taps[0] * two + taps[1] * one + taps[2] * mixed


def mixer_in(own_len, x, x_halo, small, w_b, w_u):
    (tokens, width), halo, ch = x.shape, x_halo.shape[0], w_b.shape[1]
    return whole_call(
        functools.partial(mixer_in_kernel, own_len),
        "mixer_in",
        [
            shape(tokens, width),
            shape(halo, width),
            shape(tokens, ch, dtype=F32),
            shape(tokens, ch, dtype=F32),
            shape(halo, ch, dtype=F32),
            shape(halo, ch, dtype=F32),
            shape(tokens, ch),
            shape(halo, ch),
            shape(tokens, ch, dtype=F32),
        ],
        (x, x_halo, small, w_b, w_u),
    )


def mixer_out_kernel(x_ref, n_ref, conv_ref, small_ref, wc_ref, wo_ref, c_ref, gated_ref, mid_ref, n2_ref):
    c_ref[...] = mm(n_ref[...], wc_ref[...])
    gated_ref[...] = (c_ref[...] * conv_ref[...]).astype(BF)
    mid = x_ref[...].astype(F32) + mm_nt(gated_ref[...], wo_ref[...])
    mid_ref[...] = mid
    n2_ref[...] = (mid * norm_scale(mid) * small_ref[1:2].astype(F32)).astype(BF)


def mixer_out(x, n_one, conv, small, w_c, w_o):
    (tokens, width), ch = x.shape, w_c.shape[1]
    return whole_call(
        mixer_out_kernel,
        "mixer_out",
        [
            shape(tokens, ch, dtype=F32),
            shape(tokens, ch),
            shape(tokens, width, dtype=F32),
            shape(tokens, width),
        ],
        (x, n_one, conv, small, w_c, w_o),
    )


def mixer_back_kernel(own_len, n_parts, *refs):
    parts = refs[:n_parts]
    (mid_ref, dy_ref, x_ref, xh_ref, small_ref, b_ref, u_ref, c_ref, bh_ref, uh_ref, mix_ref, mixh_ref, conv_ref) = refs[
        n_parts : n_parts + 13
    ]
    wb_ref, wu_ref, wc_ref, wo_ref = refs[n_parts + 13 : n_parts + 17]
    dmix_ref, db_ref, du_ref, dc_ref, dbh_ref, duh_ref, gin_ref, dxh_ref, sg_ref = refs[n_parts + 17 :]
    gain_one, gain_two = small_ref[0:1].astype(F32), small_ref[1:2].astype(F32)
    taps = [small_ref[2 + k : 3 + k].astype(F32) for k in range(3)]
    d_n2 = parts[0][...].astype(F32)
    for part in parts[1:]:
        d_n2 = d_n2 + part[...].astype(F32)
    mid = mid_ref[...]
    d_mid, g_two = norm_back(d_n2, mid, norm_scale(mid), gain_two)
    d_mid = d_mid + dy_ref[...].astype(F32)
    dmix_ref[...] = d_mid.astype(BF)
    d_gated = mm(dmix_ref[...], wo_ref[...])
    dc_ref[...] = (d_gated * conv_ref[...]).astype(BF)
    d_conv = d_gated * c_ref[...]
    mixed = mix_ref[...].astype(F32)
    one, two = earlier(mixed, mixh_ref[...], own_len)
    tap_rows = [jnp.sum(d_conv * view, axis=0, keepdims=True) for view in (two, one, mixed)]
    tokens = mixed.shape[0]
    pos = lax.broadcasted_iota(jnp.int32, mixed.shape, 0) % own_len
    d_mixed = taps[2] * d_conv
    d_mixed = d_mixed + taps[1] * jnp.where(pos < own_len - 1, pltpu.roll(d_conv, tokens - 1, axis=0), 0.0)
    d_mixed = d_mixed + taps[0] * jnp.where(pos < own_len - 2, pltpu.roll(d_conv, tokens - 2, axis=0), 0.0)
    db_ref[...] = (d_mixed * u_ref[...]).astype(BF)
    du_ref[...] = (d_mixed * b_ref[...]).astype(BF)
    pick_one, pick_two = halo_picks(tokens, own_len, mixh_ref.shape[0])
    low = d_conv.astype(BF)
    d_halo = taps[1] * mm_tn(pick_one, low) + taps[0] * mm_tn(pick_two, low)
    dbh_ref[...] = (d_halo * uh_ref[...]).astype(BF)
    duh_ref[...] = (d_halo * bh_ref[...]).astype(BF)
    d_n1 = mm_nt(db_ref[...], wb_ref[...]) + mm_nt(du_ref[...], wu_ref[...]) + mm_nt(dc_ref[...], wc_ref[...])
    x, xh = x_ref[...].astype(F32), xh_ref[...].astype(F32)
    d_x, g_one = norm_back(d_n1, x, norm_scale(x), gain_one)
    gin_ref[...] = d_x + d_mid
    d_nh = mm_nt(dbh_ref[...], wb_ref[...]) + mm_nt(duh_ref[...], wu_ref[...])
    d_xh, g_halo = norm_back(d_nh, xh, norm_scale(xh), gain_one)
    dxh_ref[...] = d_xh.astype(BF)
    for row, value in enumerate([g_one + g_halo, g_two] + tap_rows):
        sg_ref[row : row + 1] = value
    sg_ref[5:8] = jnp.zeros((3, sg_ref.shape[1]), F32)


def mixer_back(own_len, parts, saved, weights):
    (tokens, width), ch = parts[0].shape, weights[0].shape[1]
    halo = saved[3].shape[0]
    return whole_call(
        functools.partial(mixer_back_kernel, own_len, len(parts)),
        "mixer_back",
        [shape(tokens, width)]
        + [shape(tokens, ch)] * 3
        + [shape(halo, ch)] * 2
        + [shape(tokens, width, dtype=F32), shape(halo, width), shape(8, width, dtype=F32)],
        (*parts, *saved, *weights),
        weight=60000000000,
    )


def mixer_grad_kernel(with_halo, idx_ref, *refs):
    n_in = 8 if with_halo else 4
    ins, away_ref, home_ref = refs[:n_in], refs[n_in], refs[n_in + 1]
    me = idx_ref[0]
    quad, core = me // 2, lax.rem(me, 2)
    width = away_ref.shape[2]
    rows = ins[0].shape[1] // 8

    @pl.loop(0, 4)
    def _(kq):
        chip = jnp.bitwise_xor(quad, kq) * 2
        away = pl.multiple_of((chip + 1 - core) * rows, rows)
        home = pl.multiple_of((chip + core) * rows, rows)
        for st in range(2):
            left_ref, right_ref = ins[2 * st], ins[2 * st + 1]
            left = jnp.concatenate([left_ref[:, pl.ds(away, rows)], left_ref[:, pl.ds(home, rows)]], axis=1)
            grad = mm_tn(left, right_ref[...])
            if with_halo:
                nh_ref = ins[4]
                left = jnp.concatenate([nh_ref[:, pl.ds(away, rows)], nh_ref[:, pl.ds(home, rows)]], axis=1)
                grad = grad + mm_tn(left, ins[5][:, st * width : (st + 1) * width])
            grad = grad.astype(BF)
            away_ref[kq, st * rows : (st + 1) * rows] = grad[:rows]
            home_ref[kq, st * rows : (st + 1) * rows] = grad[rows:]
        if with_halo:
            n_tail = ins[7].shape[0] // 8
            for ref, at, k in ((away_ref, away, 2 * kq + 1), (home_ref, home, 2 * kq)):
                values = ins[6][:, pl.ds(at, rows)]
                values = jnp.concatenate([values, jnp.zeros_like(values)], axis=0)
                ref[kq, 2 * rows : 2 * rows + 16] = jnp.zeros((16, width), BF)
                ref[kq, 2 * rows : 2 * rows + 16, :rows] = values.astype(BF)
                ref[kq, 2 * rows + 16 :] = ins[7][pl.ds(pl.multiple_of(k * n_tail, n_tail), n_tail)]


def mixer_grads(index, ins, rows, with_halo):
    extra = 16 + ins[7].shape[0] // 8 if with_halo else 0
    return whole_call(
        functools.partial(mixer_grad_kernel, with_halo),
        "grads_in" if with_halo else "grads_out",
        [shape(4, 2 * rows + extra, ins[1].shape[1])] * 2,
        (index, *ins),
        scalars=1,
    )


def split_kernel(rows, idx_ref, *refs):
    terms, outs = refs[:3], refs[3:]
    z = idx_ref[1]
    n_z = len(outs)
    ch = terms[0].shape[1] // n_z
    n_tail = terms[0].shape[0] - rows - 16
    ahead = jnp.bitwise_xor(z, lax.rem(z + n_z - 1, n_z))

    def total(at, col):
        return sum(term[at, col].astype(F32) for term in terms).astype(BF)

    for s, out in enumerate(outs):
        out[:rows] = total(slice(0, rows), pl.ds(pl.multiple_of(jnp.bitwise_xor(z, s) * ch, ch), ch))
        if n_tail > 0:
            out[rows : rows + 16] = total(slice(rows, rows + 16), slice(0, ch))
            for c in range(n_z):
                value = total(slice(rows + 16, rows + 16 + n_tail), slice(c * ch, (c + 1) * ch))
                at = rows + 16 + c * n_tail
                out[at : at + n_tail] = jnp.where(ahead == s, value, jnp.zeros_like(value))


def split_z(index, terms, rows, n_z):
    every, width = terms[0].shape
    extra = 16 + (every - rows - 16) * n_z if every > rows else 0
    return whole_call(
        functools.partial(split_kernel, rows),
        "split_z",
        [shape(rows + extra, width // n_z)] * n_z,
        (index, *terms),
        scalars=1,
    )


def finish_co_kernel(*refs):
    parts, (c_ref, out_ref) = refs[:-2], refs[-2:]
    block = c_ref.shape[0]
    total = sum(part[...].astype(F32) for part in parts)
    c_ref[...] = total[:block]
    out_ref[...] = total[block:].T


def finish_co(parts):
    rows, ch = parts[0].shape
    outs = [shape(rows // 2, ch, dtype=F32), shape(ch, rows // 2, dtype=F32)]
    return whole_call(finish_co_kernel, "finish_co", outs, tuple(parts))


def finish_bu_kernel(own_len, reach, *refs):
    n_z = len(refs) - 5
    parts = refs[:n_z]
    c_ref, mid_ref, w_ref, small_ref, in_ref = refs[n_z:]
    block, ch = c_ref.shape
    tokens = mid_ref.shape[0]

    def total(lo, hi):
        return sum(part[lo:hi].astype(F32) for part in parts)

    w_ref[0] = total(0, block)
    w_ref[1] = c_ref[...]
    w_ref[2] = total(block, 2 * block)
    small_ref[...] = total(2 * block, 2 * block + 16)[:8, :block]
    n_tail = tokens // own_len * reach
    token = lax.broadcasted_iota(jnp.int32, (tokens, n_tail), 0)
    slot = lax.broadcasted_iota(jnp.int32, (tokens, n_tail), 1)
    ahead = own_len - reach + slot % reach
    spread = jnp.logical_and(token // own_len == slot // reach, token % own_len == ahead).astype(BF)
    for c in range(n_z):
        lo = 2 * block + 16 + c * n_tail
        cols = slice(c * ch, (c + 1) * ch)
        back = mm(spread, total(lo, lo + n_tail).astype(BF))
        in_ref[:, cols] = (mid_ref[:, cols] + back).astype(BF)


def finish_bu(parts, grad_c, grad_mid, own_len, reach):
    block, ch = grad_c.shape
    return whole_call(
        functools.partial(finish_bu_kernel, own_len, reach),
        "finish_bu",
        [shape(3, block, ch, dtype=F32), shape(8, block, dtype=F32), shape(*grad_mid.shape)],
        (*parts, grad_c, grad_mid),
    )


def ffn_grad_kernel(first, count, idx_ref, n_ref, d_ref, hid_ref, dgu_ref, away_ref, home_ref):
    me = idx_ref[0]
    quad, core = me // 2, lax.rem(me, 2)
    rows = n_ref.shape[1] // 8
    split = dgu_ref.shape[1]

    @pl.loop(0, count)
    def _(i):
        chip = jnp.bitwise_xor(quad, first + i) * 2
        away = pl.multiple_of((chip + 1 - core) * rows, rows)
        home = pl.multiple_of((chip + core) * rows, rows)
        left = jnp.concatenate([n_ref[:, pl.ds(away, rows)], n_ref[:, pl.ds(home, rows)]], axis=1)
        grad = mm_tn(left, dgu_ref[...]).astype(BF)
        away_ref[i, :, :split] = grad[:rows]
        home_ref[i, :, :split] = grad[rows:]
        left = jnp.concatenate([d_ref[:, pl.ds(away, rows)], d_ref[:, pl.ds(home, rows)]], axis=1)
        grad = mm_tn(left, hid_ref[...]).astype(BF)
        away_ref[i, :, split:] = grad[:rows]
        home_ref[i, :, split:] = grad[rows:]


def ffn_grads(index, first, count, n_all, d_all, hid_all, dgu_all):
    rows = n_all.shape[1] // 8
    columns = hid_all.shape[1] + dgu_all.shape[1]
    return whole_call(
        functools.partial(ffn_grad_kernel, first, count),
        "ffn_grads",
        [shape(count, rows, columns)] * 2,
        (index, n_all, d_all, hid_all, dgu_all),
        scalars=1,
    )


def core_sum(away, home, count, tag):
    other = dp_swap(away, 1, tag)
    return [(home[kq].astype(F32) + other[kq].astype(F32)).astype(BF) for kq in range(count)]


def body(
    layer_in,
    cotangent,
    row_counts,
    tail_tokens,
    row_order,
    gain_one,
    w_in,
    kernel,
    w_out,
    gain_two,
    w_gu,
    w_down,
):
    row_count, own_len, width = layer_in.shape
    n_dp, n_z = lax.axis_size("dp"), lax.axis_size("tensor")
    outer = n_dp // INNER
    me, z = lax.axis_index("dp"), lax.axis_index("tensor")
    me_in = me // outer
    row_len = own_len * n_z
    channels = w_in.shape[2]
    reach = kernel.shape[0] - 1
    tokens = row_count * own_len
    block = width // INNER
    units = w_down.shape[0]
    index = jnp.stack([me_in, z]).astype(jnp.int32)

    given = lax.dynamic_slice_in_dim(row_order, me * row_count, row_count)
    starts = jnp.cumsum(row_counts) - row_counts
    ends = starts + row_counts - 1
    is_first = jnp.any(starts[None, :] == given[:, None], axis=1)
    at_end = ends[None, :] == given[:, None]
    row_valid = jnp.where(
        jnp.any(at_end, axis=1),
        jnp.sum(jnp.where(at_end, tail_tokens[None, :], 0), axis=1),
        row_len,
    )
    positions = z * own_len + jnp.arange(own_len, dtype=jnp.int32)
    valid = positions[None, :] < row_valid[:, None]

    small = jnp.concatenate([gain_one[None], gain_two[None], kernel], axis=0)
    mix_own = jnp.stack([w_in[:, 0], w_in[:, 2], w_in[:, 1], w_out.T])
    ffn_own = jnp.concatenate([w_gu[:, 0], w_gu[:, 1], w_down.T], axis=1)
    groups = [[i * outer + o for o in range(outer)] for i in range(INNER)]
    tails = layer_in[:, own_len - reach :].reshape(row_count * reach, width)
    tails = z_shift(tails, 1, "tail")
    if outer > 1:
        wide = functools.partial(lax.all_gather, axis_name="dp", tiled=True, axis_index_groups=groups)
        mix_own, small = wide(mix_own, axis=1), wide(small, axis=1)
        ffn_own, tails = wide(ffn_own, axis=0), wide(tails, axis=0)
    n_small = small.shape[0]
    small = jnp.pad(small, ((0, 16 - n_small), (0, 0)))
    mix_own = after(mix_own.reshape(4 * block, channels), ffn_own)

    mix_far, mix_near = z_send(mix_own, "mix", (2, 1))
    ffn_x, ffn_y = plane_gather(ffn_own, "ffn")
    mix_last = z_swap(mix_far, 1, "mix_on")
    d_ffn = jnp.where(valid[:, :, None], cotangent, jnp.zeros_like(cotangent)).reshape(tokens, width)
    tails = after(tails, d_ffn)
    mix_rows = stack_mixer(index, small, tails, [mix_own, mix_near, mix_far, mix_last])

    mix_rows = after(mix_rows, ffn_x, ffn_y)
    mix_x, mix_y = plane_gather(mix_rows, "mix")
    dy_far, dy_near = z_send(d_ffn, "dy", (2, 1), mix_last)
    mix_pairs = [mix_rows, dp_swap(mix_rows, 1, "mix")]
    ffn_pairs = [ffn_own, dp_swap(ffn_own, 1, "ffn")]
    ffn_pairs += [ffn_x, dp_swap(after(ffn_x, ffn_pairs[1]), 1, "ffn")]
    mix_d = plane_corner(mix_x, mix_y, "mix", dy_far, dy_near, ffn_pairs[1])
    ffn_pairs += [ffn_y, dp_swap(after(ffn_y, ffn_pairs[3]), 1, "ffn")]
    dy_set = [dy_near, dy_far, z_swap(dy_far, 1, "dy_on")]
    mix_pairs += [mix_x, dp_swap(mix_x, 1, "mix"), mix_y, dp_swap(mix_y, 1, "mix")]
    mix_pairs += [mix_d, dp_swap(after(mix_d, ffn_pairs[3], dy_set[2]), 1, "mix")]
    w_b, w_u, w_c, w_o, small_all, every = place_mixer(index, mix_pairs, block, 16, tails.shape[0])

    slots = INNER * outer * row_count
    rel = jnp.bitwise_xor(me_in, jnp.arange(INNER, dtype=jnp.int32))
    slot_rows = row_order.reshape(INNER, outer * row_count)[rel].reshape(slots)
    wanted = jnp.where(z == 0, jnp.where(is_first, -1, given - 1), given)
    picks = jnp.repeat(wanted, reach)[:, None] == jnp.repeat(slot_rows, reach)[None, :]
    picks = jnp.logical_and(
        picks, jnp.arange(row_count * reach)[:, None] % reach == jnp.arange(slots * reach)[None, :] % reach
    ).astype(BF)
    x_halo = mm(picks, every).astype(BF)
    x_own = layer_in.reshape(tokens, width)
    n_one, n_halo, b_own, u_own, b_halo, u_halo, mixed, mixed_halo, conv = mixer_in(
        own_len, x_own, x_halo, small_all, w_b, w_u
    )
    c_own, gated, middle, n_two = mixer_out(x_own, n_one, conv, small_all, w_c, w_o)

    ffn_d = plane_corner(ffn_x, ffn_y, "ffn", mix_d)
    n_two_far, n_two_near = z_send(n_two, "n2", (2, 1))
    n_two_set = [n_two, n_two_near, n_two_far]
    ffn_pairs += [ffn_d, dp_swap(after(ffn_d, n_two), 1, "ffn")]
    w_ffn = place_ffn(index, ffn_pairs)
    d_ffn_set = [d_ffn] + dy_set
    d_parts, out_parts, kept = [], [], ()
    for s in range(n_z):
        d_part, out_part, *kept = ffn_piece(s, n_z, n_two_set[s], d_ffn_set[s], w_ffn, kept)
        d_parts.append(d_part)
        out_parts.append(out_part)
        if s == 0:
            n_two_set.append(z_swap(after(n_two_far, d_part), 1, "n2_on"))
    d_on = z_swap(d_parts[3], 1, "dn_on")
    away, home = ffn_grads(index, 0, 4, *kept)
    d_on = after(d_on, away).astype(F32) + d_parts[2].astype(F32)
    d_near = z_swap(after(d_parts[1], n_two_set[3]), 1, "dn")
    d_parts = [d_parts[0], d_near, z_swap(d_on.astype(BF), 2, "dn")]

    ffn_pieces = core_sum(away, home, 4, "gf")
    ffn_across = plane_far(ffn_pieces, "gf")
    out_on = z_swap(after(out_parts[3], d_near), 1, "out_on")
    out_first = z_swap(after(out_parts[1], d_near), 1, "out")
    d_mix, d_b, d_u, d_c, d_b_halo, d_u_halo, grad_mid, d_x_halo, small_grads = mixer_back(
        own_len,
        d_parts,
        (middle, d_ffn, x_own, x_halo, small_all, b_own, u_own, c_own, b_halo, u_halo, mixed, mixed_halo, conv),
        (w_b, w_u, w_c, w_o),
    )

    co_away, co_home = mixer_grads(index, (after(n_one, ffn_pieces[3]), d_c, d_mix, gated), block, False)
    d_bu_halo = jnp.concatenate([d_b_halo, d_u_halo], axis=1)
    spread = mm_tn(picks, d_x_halo).astype(BF)
    bu_away, bu_home = mixer_grads(
        index, (after(n_one, co_away), d_b, n_one, d_u, n_halo, d_bu_halo, small_grads, spread), block, True
    )
    co_pieces = core_sum(after(co_away, out_on), co_home, 4, "gco")
    out_second = (out_parts[2].astype(F32) + out_on.astype(F32)).astype(BF)
    out_second = z_swap(out_second, 2, "out")
    co_across = plane_far(co_pieces, "gco")
    co_terms = plane_near(co_pieces, co_across, "gco")
    bu_pieces = core_sum(after(bu_away, co_pieces[0]), bu_home, 4, "gbu")
    bu_across = plane_far(bu_pieces, "gbu")
    bu_terms = plane_near(bu_pieces, bu_across, "gbu")
    ffn_terms = plane_near(ffn_pieces, ffn_across, "gf", bu_across)
    layer_out = middle + out_parts[0].astype(F32) + out_first.astype(F32) + out_second.astype(F32)
    layer_out = layer_out.astype(BF).reshape(row_count, own_len, width)

    def z_parts(terms, tag, *waits):
        first = after(terms[0], *waits) if waits else terms[0]
        parts = split_z(index, (first, *terms[1:]), 2 * block, n_z)
        return [parts[0]] + [z_swap(parts[s], s, tag) for s in range(1, n_z)]

    co_parts = z_parts(co_terms, "gco", out_first, out_second)
    ffn_total = sum(term.astype(F32) for term in ffn_terms)
    if outer > 1:
        narrow = functools.partial(
            lax.psum_scatter, axis_name="dp", tiled=True, axis_index_groups=groups
        )
        ffn_total = narrow(ffn_total, scatter_dimension=0)
    grad_w_gu = jnp.stack([ffn_total[:, :units], ffn_total[:, units : 2 * units]], axis=1)
    grad_w_down = ffn_total[:, 2 * units :].T
    bu_parts = z_parts(bu_terms, "gbu", co_parts[0])
    if outer > 1:
        bu_total = sum(part.astype(F32) for part in bu_parts)
        grad_co = sum(part.astype(F32) for part in co_parts).reshape(2, block, channels)
        grad_co = narrow(grad_co, scatter_dimension=1)
        grad_bu = narrow(bu_total[: 2 * block].reshape(2, block, channels), scatter_dimension=1)
        grad_small = narrow(bu_total[2 * block : 2 * block + n_small, :block], scatter_dimension=1)
        returned = bu_total[2 * block + 16 :].reshape(n_z, -1, channels)
        returned = narrow(jnp.moveaxis(returned, 0, 1).reshape(-1, width), scatter_dimension=0)
        grad_w_in = jnp.stack([grad_bu[0], grad_co[0], grad_bu[1]])
        grad_w_out = grad_co[1].T
        grad_in = grad_mid.reshape(row_count, own_len, width)
        grad_in = grad_in + jnp.pad(
            returned.reshape(row_count, reach, width), ((0, 0), (own_len - reach, 0), (0, 0))
        )
        grad_in = grad_in.astype(BF)
    else:
        grad_c, grad_w_out = finish_co(co_parts)
        grad_w_in, grad_small, grad_in = finish_bu(bu_parts, grad_c, grad_mid, own_len, reach)
        grad_in = grad_in.reshape(row_count, own_len, width)
    return (
        layer_out,
        grad_in,
        grad_small[0],
        jnp.swapaxes(grad_w_in, 0, 1),
        grad_small[2:n_small],
        grad_w_out,
        grad_small[1],
        grad_w_gu,
        grad_w_down,
    )


def solution(mesh):
    in_specs = (
        P("dp", "tensor", None),
        P("dp", "tensor", None),
        P(),
        P(),
        P(),
        P("dp"),
        P("dp", None, "tensor"),
        P(None, "dp"),
        P("tensor", "dp"),
        P("dp"),
        P("dp", None, "tensor"),
        P("tensor", "dp"),
    )
    out_specs = (
        P("dp", "tensor", None),
        P("dp", "tensor", None),
        P("dp"),
        P("dp", None, "tensor"),
        P(None, "dp"),
        P("tensor", "dp"),
        P("dp"),
        P("dp", None, "tensor"),
        P("tensor", "dp"),
    )
    return jax.shard_map(body, mesh=mesh, in_specs=in_specs, out_specs=out_specs, check_vma=False)
```

```python
import functools
import jax
import jax.numpy as jnp
from jax import lax
from jax.experimental import pallas as pl
from jax.experimental.pallas import tpu as pltpu
from jax.sharding import PartitionSpec as P

EPS = 1e-05
INNER = 8
BF = jnp.bfloat16
F32 = jnp.float32
VMEM_LIMIT = 12 << 20


def hold_kernel(*refs):
    pass


def hold(value, *events):
    anywhere = pl.BlockSpec(memory_space=pl.ANY)
    return pl.pallas_call(
        hold_kernel,
        out_shape=shape(*value.shape, dtype=value.dtype),
        in_specs=[anywhere] * (1 + len(events)),
        out_specs=anywhere,
        input_output_aliases={0: 0},
        cost_estimate=pl.CostEstimate(flops=1, bytes_accessed=1, transcendentals=0),
        name="hold",
    )(value, *events)


def dp_swap(value, step, tag):
    size = lax.axis_size("dp")
    hop = step * (size // INNER)
    with jax.named_scope(f"{tag}_dp{step}"):
        return lax.ppermute(value, "dp", [(i, i ^ hop) for i in range(size)])


def z_shift(value, step, tag):
    size = lax.axis_size("tensor")
    with jax.named_scope(f"{tag}_z"):
        return lax.ppermute(value, "tensor", [(i, (i + step) % size) for i in range(size)])


def z_swap(value, step, tag):
    size = lax.axis_size("tensor")
    with jax.named_scope(f"{tag}_z{step}"):
        return lax.ppermute(value, "tensor", [(i, i ^ step) for i in range(size)])


def after(value, *events):
    return lax.optimization_barrier((value,) + events)[0]


def mm(a, b):
    return lax.dot_general(a, b, (((1,), (0,)), ((), ())), preferred_element_type=F32)


def mm_nt(a, b):
    return lax.dot_general(a, b, (((1,), (1,)), ((), ())), preferred_element_type=F32)


def mm_tn(a, b):
    return lax.dot_general(a, b, (((0,), (0,)), ((), ())), preferred_element_type=F32)


def shape(*dims, dtype=BF):
    return jax.ShapeDtypeStruct(dims, dtype)


def whole_call(kernel, name, outs, args, scalars=0, hbm=0, scratch=(), alias=None, weight=0):
    specs = [pl.BlockSpec(memory_space=pltpu.SMEM)] * scalars
    specs += [pl.BlockSpec(memory_space=pltpu.HBM)] * hbm
    specs += [pl.BlockSpec(memory_space=pltpu.VMEM)] * (len(args) - scalars - hbm)
    return pl.pallas_call(
        kernel,
        out_shape=outs,
        in_specs=specs,
        out_specs=[pl.BlockSpec(memory_space=pltpu.VMEM)] * len(outs),
        scratch_shapes=list(scratch),
        input_output_aliases=alias or {},
        compiler_params=pltpu.CompilerParams(vmem_limit_bytes=VMEM_LIMIT),
        cost_estimate=pl.CostEstimate(flops=1 + weight, bytes_accessed=1, transcendentals=0),
        name=name,
    )(*args)


def corner(value, tag):
    size = lax.axis_size("dp")
    outer = size // INNER
    pairs = []
    for i in range(size):
        hop = 2 if (i // outer) % 2 else 4
        pairs.append((i, i ^ (hop * outer)))
    with jax.named_scope(f"{tag}_corner"):
        return lax.ppermute(value, "dp", pairs)


def core_zero():
    return lax.axis_index("dp") // (lax.axis_size("dp") // INNER) % 2 == 0


def plane_gather(local, tag, *waits):
    local = after(local, *waits) if waits else local
    return dp_swap(local, 2, tag), dp_swap(local, 4, tag)


def plane_corner(over_x, over_y, tag, *waits):
    value = jnp.where(core_zero(), over_x, over_y)
    return corner(after(value, *waits) if waits else value, tag)


def plane_far(pieces, tag, *waits):
    far = hold(pieces[3], *waits) if waits else pieces[3]
    return corner(far, tag)


def plane_near(pieces, far, tag, *waits):
    far = far.astype(F32)
    first = core_zero()
    over_x = (pieces[1].astype(F32) + jnp.where(first, far, 0.0)).astype(BF)
    over_y = (pieces[2].astype(F32) + jnp.where(first, 0.0, far)).astype(BF)
    if waits:
        over_x, over_y = after(over_x, *waits), after(over_y, *waits)
    return pieces[0], dp_swap(over_x, 2, tag), dp_swap(over_y, 4, tag)


def z_send(local, tag, steps, *waits):
    local = after(local, *waits) if waits else local
    return [z_swap(local, step, tag) for step in steps]


def stack_mixer_kernel(idx_ref, small_ref, tail_ref, *refs):
    parts, out_ref = refs[:-1], refs[-1]
    z = idx_ref[1]
    rows, ch = parts[0].shape
    for s, part in enumerate(parts):
        col = pl.multiple_of(jnp.bitwise_xor(z, s) * ch, ch)
        out_ref[:rows, pl.ds(col, ch)] = part[...]
    n_small, block = small_ref.shape
    out_ref[rows : rows + n_small] = jnp.zeros((n_small, out_ref.shape[1]), BF)
    out_ref[rows : rows + n_small, :block] = small_ref[...]
    out_ref[rows + n_small :] = tail_ref[...]


def stack_mixer(index, small, tail, parts):
    rows, ch = parts[0].shape
    return whole_call(
        stack_mixer_kernel,
        "stack_mixer",
        [shape(rows + small.shape[0] + tail.shape[0], len(parts) * ch)],
        (index, small, tail, *parts),
        scalars=1,
    )[0]


def place_mixer_kernel(block, idx_ref, *refs):
    pieces, outs, sems = refs[:8], refs[8:-1], refs[-1]
    small_ref, tail_ref = outs[4], outs[5]
    me = idx_ref[0]
    n_small, n_tail = small_ref.shape[0], tail_ref.shape[0] // 8
    copies = []
    for k in range(8):
        at = pl.multiple_of(jnp.bitwise_xor(me, k) * block, block)
        for st in range(4):
            copies.append(
                pltpu.make_async_copy(
                    pieces[k].at[pl.ds(st * block, block)], outs[st].at[pl.ds(at, block)], sems.at[k, st]
                )
            )
        copies.append(
            pltpu.make_async_copy(
                pieces[k].at[pl.ds(4 * block, n_small), pl.ds(0, block)],
                small_ref.at[:, pl.ds(at, block)],
                sems.at[k, 4],
            )
        )
        copies.append(
            pltpu.make_async_copy(
                pieces[k].at[pl.ds(4 * block + n_small, n_tail)],
                tail_ref.at[pl.ds(k * n_tail, n_tail)],
                sems.at[k, 5],
            )
        )
    for copy in copies:
        copy.start()
    for copy in copies:
        copy.wait()


def place_mixer(index, pieces, block, n_small, n_tail):
    width = pieces[0].shape[1]
    return whole_call(
        functools.partial(place_mixer_kernel, block),
        "place_mixer",
        [shape(8 * block, width)] * 4 + [shape(n_small, 8 * block), shape(8 * n_tail, width)],
        (index, *pieces),
        scalars=1,
        hbm=8,
        scratch=[pltpu.SemaphoreType.DMA((8, 6))],
    )


def place_ffn_kernel(idx_ref, *refs):
    pieces, out_ref, sems = refs[:8], refs[8], refs[9]
    me = idx_ref[0]
    rows = out_ref.shape[0] // 8
    copies = []
    for k in range(8):
        at = pl.ds(pl.multiple_of(jnp.bitwise_xor(me, k) * rows, rows), rows)
        copies.append(pltpu.make_async_copy(pieces[k], out_ref.at[at], sems.at[k]))
    for copy in copies:
        copy.start()
    for copy in copies:
        copy.wait()


def place_ffn(index, pieces):
    rows, columns = pieces[0].shape
    return whole_call(
        place_ffn_kernel,
        "place_ffn",
        [shape(8 * rows, columns)],
        (index, *pieces),
        scalars=1,
        hbm=8,
        scratch=[pltpu.SemaphoreType.DMA((8,))],
    )[0]


def ffn_kernel(step, n_ref, d_ref, w_ref, *refs):
    dn_ref, part_ref, n_all_ref, d_all_ref, hid_ref, dgu_ref = refs[-6:]
    tokens = n_ref.shape[0]
    own = slice(step * tokens, (step + 1) * tokens)
    units, width = w_ref.shape[1] // 3, w_ref.shape[0]
    wide, tall = units // 3, width // 4
    n_all_ref[own] = n_ref[...]
    d_all_ref[own] = d_ref[...]

    @pl.loop(0, 3)
    def _(i):
        one = pl.multiple_of(i * wide, wide)
        two, three = pl.multiple_of(one + units, wide), pl.multiple_of(one + 2 * units, wide)
        gate = mm(n_ref[...], w_ref[:, pl.ds(one, wide)])
        up = mm(n_ref[...], w_ref[:, pl.ds(two, wide)])
        sig = jax.nn.sigmoid(gate)
        silu = gate * sig
        hid_ref[own, pl.ds(one, wide)] = (silu * up).astype(BF)
        d_hidden = mm(d_ref[...], w_ref[:, pl.ds(three, wide)])
        d_gate = d_hidden * up * (sig * (1.0 + gate * (1.0 - sig)))
        dgu_ref[own, pl.ds(one, wide)] = d_gate.astype(BF)
        dgu_ref[own, pl.ds(two, wide)] = (d_hidden * silu).astype(BF)

    @pl.loop(0, 4)
    def _(i):
        rows = pl.ds(pl.multiple_of(i * tall, tall), tall)
        dn_ref[:, rows] = mm_nt(dgu_ref[own], w_ref[rows, : 2 * units]).astype(BF)
        part_ref[:, rows] = mm_nt(hid_ref[own], w_ref[rows, 2 * units :]).astype(BF)


def ffn_whole_kernel(step, n_ref, d_ref, w_ref, *refs):
    dn_ref, part_ref, n_all_ref, d_all_ref, hid_ref, dgu_ref = refs[-6:]
    tokens = n_ref.shape[0]
    own = slice(step * tokens, (step + 1) * tokens)
    units = w_ref.shape[1] // 3
    gu, down = slice(0, 2 * units), slice(2 * units, 3 * units)
    n_all_ref[own] = n_ref[...]
    d_all_ref[own] = d_ref[...]
    both = mm(n_ref[...], w_ref[:, gu])
    gate, up = both[:, :units], both[:, units:]
    sig = jax.nn.sigmoid(gate)
    silu = gate * sig
    hidden = (silu * up).astype(BF)
    hid_ref[own] = hidden
    d_hidden = mm(d_ref[...], w_ref[:, down])
    dgu_ref[own, :units] = (d_hidden * up * (sig * (1.0 + gate * (1.0 - sig)))).astype(BF)
    dgu_ref[own, units:] = (d_hidden * silu).astype(BF)
    dn_ref[...] = mm_nt(dgu_ref[own], w_ref[:, gu]).astype(BF)
    part_ref[...] = mm_nt(hidden, w_ref[:, down]).astype(BF)


def ffn_piece(step, steps, normed, d_out, weights, kept):
    tokens, width = normed.shape
    units = weights.shape[1] // 3
    every = steps * tokens
    return whole_call(
        functools.partial(ffn_kernel if step < 2 else ffn_whole_kernel, step),
        "ffn_piece",
        [shape(tokens, width)] * 2
        + [shape(every, width), shape(every, width), shape(every, units), shape(every, 2 * units)],
        (normed, d_out, weights, *kept),
        alias={3 + i: 2 + i for i in range(len(kept))},
    )


def norm_scale(value):
    return lax.rsqrt(jnp.mean(value * value, axis=-1, keepdims=True) + EPS)


def norm_back(d_normed, value, scale, gain):
    weighted = d_normed * gain
    d_value = scale * weighted - value * (scale * scale * scale) * jnp.mean(
        weighted * value, axis=-1, keepdims=True
    )
    return d_value, jnp.sum(d_normed * value * scale, axis=0, keepdims=True)


def halo_picks(tokens, own_len, halo):
    token = lax.broadcasted_iota(jnp.int32, (tokens, halo), 0)
    slot = lax.broadcasted_iota(jnp.int32, (tokens, halo), 1)
    run, pos = token // own_len, token % own_len
    one = jnp.logical_and(pos == 0, slot == 2 * run + 1)
    two = jnp.logical_and(pos < 2, slot == 2 * run + pos)
    return one.astype(BF), two.astype(BF)


def earlier(mixed, mixed_halo, own_len):
    tokens = mixed.shape[0]
    pick_one, pick_two = halo_picks(tokens, own_len, mixed_halo.shape[0])
    pos = lax.broadcasted_iota(jnp.int32, mixed.shape, 0) % own_len
    one = jnp.where(pos == 0, mm(pick_one, mixed_halo), pltpu.roll(mixed, 1, axis=0))
    two = jnp.where(pos < 2, mm(pick_two, mixed_halo), pltpu.roll(mixed, 2, axis=0))
    return one, two


def mixer_in_kernel(
    own_len, x_ref, xh_ref, small_ref, wb_ref, wu_ref, n_ref, nh_ref, b_ref, u_ref, bh_ref, uh_ref, mix_ref, mixh_ref, conv_ref
):
    gain = small_ref[0:1].astype(F32)
    x, xh = x_ref[...].astype(F32), xh_ref[...].astype(F32)
    n_ref[...] = (x * norm_scale(x) * gain).astype(BF)
    nh_ref[...] = (xh * norm_scale(xh) * gain).astype(BF)
    b_ref[...] = mm(n_ref[...], wb_ref[...])
    u_ref[...] = mm(n_ref[...], wu_ref[...])
    bh_ref[...] = mm(nh_ref[...], wb_ref[...])
    uh_ref[...] = mm(nh_ref[...], wu_ref[...])
    mix_ref[...] = (b_ref[...] * u_ref[...]).astype(BF)
    mixh_ref[...] = (bh_ref[...] * uh_ref[...]).astype(BF)
    mixed = mix_ref[...].astype(F32)
    one, two = earlier(mixed, mixh_ref[...], own_len)
    taps = [small_ref[2 + k : 3 + k].astype(F32) for k in range(3)]
    conv_ref[...] = taps[0] * two + taps[1] * one + taps[2] * mixed


def mixer_in(own_len, x, x_halo, small, w_b, w_u):
    (tokens, width), halo, ch = x.shape, x_halo.shape[0], w_b.shape[1]
    return whole_call(
        functools.partial(mixer_in_kernel, own_len),
        "mixer_in",
        [
            shape(tokens, width),
            shape(halo, width),
            shape(tokens, ch, dtype=F32),
            shape(tokens, ch, dtype=F32),
            shape(halo, ch, dtype=F32),
            shape(halo, ch, dtype=F32),
            shape(tokens, ch),
            shape(halo, ch),
            shape(tokens, ch, dtype=F32),
        ],
        (x, x_halo, small, w_b, w_u),
    )


def mixer_out_kernel(x_ref, n_ref, conv_ref, small_ref, wc_ref, wo_ref, c_ref, gated_ref, mid_ref, n2_ref):
    c_ref[...] = mm(n_ref[...], wc_ref[...])
    gated_ref[...] = (c_ref[...] * conv_ref[...]).astype(BF)
    mid = x_ref[...].astype(F32) + mm_nt(gated_ref[...], wo_ref[...])
    mid_ref[...] = mid
    n2_ref[...] = (mid * norm_scale(mid) * small_ref[1:2].astype(F32)).astype(BF)


def mixer_out(x, n_one, conv, small, w_c, w_o):
    (tokens, width), ch = x.shape, w_c.shape[1]
    return whole_call(
        mixer_out_kernel,
        "mixer_out",
        [
            shape(tokens, ch, dtype=F32),
            shape(tokens, ch),
            shape(tokens, width, dtype=F32),
            shape(tokens, width),
        ],
        (x, n_one, conv, small, w_c, w_o),
    )


def mixer_back_kernel(own_len, n_parts, *refs):
    parts = refs[:n_parts]
    (mid_ref, dy_ref, x_ref, xh_ref, small_ref, b_ref, u_ref, c_ref, bh_ref, uh_ref, mix_ref, mixh_ref, conv_ref) = refs[
        n_parts : n_parts + 13
    ]
    wb_ref, wu_ref, wc_ref, wo_ref = refs[n_parts + 13 : n_parts + 17]
    dmix_ref, db_ref, du_ref, dc_ref, dbh_ref, duh_ref, gin_ref, dxh_ref, sg_ref = refs[n_parts + 17 :]
    gain_one, gain_two = small_ref[0:1].astype(F32), small_ref[1:2].astype(F32)
    taps = [small_ref[2 + k : 3 + k].astype(F32) for k in range(3)]
    d_n2 = parts[0][...].astype(F32)
    for part in parts[1:]:
        d_n2 = d_n2 + part[...].astype(F32)
    mid = mid_ref[...]
    d_mid, g_two = norm_back(d_n2, mid, norm_scale(mid), gain_two)
    d_mid = d_mid + dy_ref[...].astype(F32)
    dmix_ref[...] = d_mid.astype(BF)
    d_gated = mm(dmix_ref[...], wo_ref[...])
    dc_ref[...] = (d_gated * conv_ref[...]).astype(BF)
    d_conv = d_gated * c_ref[...]
    mixed = mix_ref[...].astype(F32)
    one, two = earlier(mixed, mixh_ref[...], own_len)
    tap_rows = [jnp.sum(d_conv * view, axis=0, keepdims=True) for view in (two, one, mixed)]
    tokens = mixed.shape[0]
    pos = lax.broadcasted_iota(jnp.int32, mixed.shape, 0) % own_len
    d_mixed = taps[2] * d_conv
    d_mixed = d_mixed + taps[1] * jnp.where(pos < own_len - 1, pltpu.roll(d_conv, tokens - 1, axis=0), 0.0)
    d_mixed = d_mixed + taps[0] * jnp.where(pos < own_len - 2, pltpu.roll(d_conv, tokens - 2, axis=0), 0.0)
    db_ref[...] = (d_mixed * u_ref[...]).astype(BF)
    du_ref[...] = (d_mixed * b_ref[...]).astype(BF)
    pick_one, pick_two = halo_picks(tokens, own_len, mixh_ref.shape[0])
    low = d_conv.astype(BF)
    d_halo = taps[1] * mm_tn(pick_one, low) + taps[0] * mm_tn(pick_two, low)
    dbh_ref[...] = (d_halo * uh_ref[...]).astype(BF)
    duh_ref[...] = (d_halo * bh_ref[...]).astype(BF)
    d_n1 = mm_nt(db_ref[...], wb_ref[...]) + mm_nt(du_ref[...], wu_ref[...]) + mm_nt(dc_ref[...], wc_ref[...])
    x, xh = x_ref[...].astype(F32), xh_ref[...].astype(F32)
    d_x, g_one = norm_back(d_n1, x, norm_scale(x), gain_one)
    gin_ref[...] = d_x + d_mid
    d_nh = mm_nt(dbh_ref[...], wb_ref[...]) + mm_nt(duh_ref[...], wu_ref[...])
    d_xh, g_halo = norm_back(d_nh, xh, norm_scale(xh), gain_one)
    dxh_ref[...] = d_xh.astype(BF)
    for row, value in enumerate([g_one + g_halo, g_two] + tap_rows):
        sg_ref[row : row + 1] = value
    sg_ref[5:8] = jnp.zeros((3, sg_ref.shape[1]), F32)


def mixer_back(own_len, parts, saved, weights):
    (tokens, width), ch = parts[0].shape, weights[0].shape[1]
    halo = saved[3].shape[0]
    return whole_call(
        functools.partial(mixer_back_kernel, own_len, len(parts)),
        "mixer_back",
        [shape(tokens, width)]
        + [shape(tokens, ch)] * 3
        + [shape(halo, ch)] * 2
        + [shape(tokens, width, dtype=F32), shape(halo, width), shape(8, width, dtype=F32)],
        (*parts, *saved, *weights),
        weight=60000000000,
    )


def mixer_grad_kernel(with_halo, idx_ref, *refs):
    n_in = 8 if with_halo else 4
    ins, away_ref, home_ref = refs[:n_in], refs[n_in], refs[n_in + 1]
    me = idx_ref[0]
    quad, core = me // 2, lax.rem(me, 2)
    width = away_ref.shape[2]
    rows = ins[0].shape[1] // 8

    @pl.loop(0, 4)
    def _(kq):
        chip = jnp.bitwise_xor(quad, kq) * 2
        away = pl.multiple_of((chip + 1 - core) * rows, rows)
        home = pl.multiple_of((chip + core) * rows, rows)
        for st in range(2):
            left_ref, right_ref = ins[2 * st], ins[2 * st + 1]
            left = jnp.concatenate([left_ref[:, pl.ds(away, rows)], left_ref[:, pl.ds(home, rows)]], axis=1)
            grad = mm_tn(left, right_ref[...])
            if with_halo:
                nh_ref = ins[4]
                left = jnp.concatenate([nh_ref[:, pl.ds(away, rows)], nh_ref[:, pl.ds(home, rows)]], axis=1)
                grad = grad + mm_tn(left, ins[5][:, st * width : (st + 1) * width])
            grad = grad.astype(BF)
            away_ref[kq, st * rows : (st + 1) * rows] = grad[:rows]
            home_ref[kq, st * rows : (st + 1) * rows] = grad[rows:]
        if with_halo:
            n_tail = ins[7].shape[0] // 8
            for ref, at, k in ((away_ref, away, 2 * kq + 1), (home_ref, home, 2 * kq)):
                values = ins[6][:, pl.ds(at, rows)]
                values = jnp.concatenate([values, jnp.zeros_like(values)], axis=0)
                ref[kq, 2 * rows : 2 * rows + 16] = jnp.zeros((16, width), BF)
                ref[kq, 2 * rows : 2 * rows + 16, :rows] = values.astype(BF)
                ref[kq, 2 * rows + 16 :] = ins[7][pl.ds(pl.multiple_of(k * n_tail, n_tail), n_tail)]


def mixer_grads(index, ins, rows, with_halo):
    extra = 16 + ins[7].shape[0] // 8 if with_halo else 0
    return whole_call(
        functools.partial(mixer_grad_kernel, with_halo),
        "grads_in" if with_halo else "grads_out",
        [shape(4, 2 * rows + extra, ins[1].shape[1])] * 2,
        (index, *ins),
        scalars=1,
    )


def split_kernel(rows, idx_ref, *refs):
    terms, outs = refs[:3], refs[3:]
    z = idx_ref[1]
    n_z = len(outs)
    ch = terms[0].shape[1] // n_z
    n_tail = terms[0].shape[0] - rows - 16
    ahead = jnp.bitwise_xor(z, lax.rem(z + n_z - 1, n_z))

    def total(at, col):
        return sum(term[at, col].astype(F32) for term in terms).astype(BF)

    for s, out in enumerate(outs):
        out[:rows] = total(slice(0, rows), pl.ds(pl.multiple_of(jnp.bitwise_xor(z, s) * ch, ch), ch))
        if n_tail > 0:
            out[rows : rows + 16] = total(slice(rows, rows + 16), slice(0, ch))
            for c in range(n_z):
                value = total(slice(rows + 16, rows + 16 + n_tail), slice(c * ch, (c + 1) * ch))
                at = rows + 16 + c * n_tail
                out[at : at + n_tail] = jnp.where(ahead == s, value, jnp.zeros_like(value))


def split_z(index, terms, rows, n_z):
    every, width = terms[0].shape
    extra = 16 + (every - rows - 16) * n_z if every > rows else 0
    return whole_call(
        functools.partial(split_kernel, rows),
        "split_z",
        [shape(rows + extra, width // n_z)] * n_z,
        (index, *terms),
        scalars=1,
    )


def finish_co_kernel(*refs):
    parts, (c_ref, out_ref) = refs[:-2], refs[-2:]
    block = c_ref.shape[0]
    total = sum(part[...].astype(F32) for part in parts)
    c_ref[...] = total[:block]
    out_ref[...] = total[block:].T


def finish_co(parts):
    rows, ch = parts[0].shape
    outs = [shape(rows // 2, ch, dtype=F32), shape(ch, rows // 2, dtype=F32)]
    return whole_call(finish_co_kernel, "finish_co", outs, tuple(parts))


def finish_bu_kernel(own_len, reach, *refs):
    n_z = len(refs) - 5
    parts = refs[:n_z]
    c_ref, mid_ref, w_ref, small_ref, in_ref = refs[n_z:]
    block, ch = c_ref.shape
    tokens = mid_ref.shape[0]

    def total(lo, hi):
        return sum(part[lo:hi].astype(F32) for part in parts)

    w_ref[0] = total(0, block)
    w_ref[1] = c_ref[...]
    w_ref[2] = total(block, 2 * block)
    small_ref[...] = total(2 * block, 2 * block + 16)[:8, :block]
    n_tail = tokens // own_len * reach
    token = lax.broadcasted_iota(jnp.int32, (tokens, n_tail), 0)
    slot = lax.broadcasted_iota(jnp.int32, (tokens, n_tail), 1)
    ahead = own_len - reach + slot % reach
    spread = jnp.logical_and(token // own_len == slot // reach, token % own_len == ahead).astype(BF)
    for c in range(n_z):
        lo = 2 * block + 16 + c * n_tail
        cols = slice(c * ch, (c + 1) * ch)
        back = mm(spread, total(lo, lo + n_tail).astype(BF))
        in_ref[:, cols] = (mid_ref[:, cols] + back).astype(BF)


def finish_bu(parts, grad_c, grad_mid, own_len, reach):
    block, ch = grad_c.shape
    return whole_call(
        functools.partial(finish_bu_kernel, own_len, reach),
        "finish_bu",
        [shape(3, block, ch, dtype=F32), shape(8, block, dtype=F32), shape(*grad_mid.shape)],
        (*parts, grad_c, grad_mid),
    )


def ffn_grad_kernel(first, count, idx_ref, n_ref, d_ref, hid_ref, dgu_ref, away_ref, home_ref):
    me = idx_ref[0]
    quad, core = me // 2, lax.rem(me, 2)
    rows = n_ref.shape[1] // 8
    split = dgu_ref.shape[1]

    @pl.loop(0, count)
    def _(i):
        chip = jnp.bitwise_xor(quad, first + i) * 2
        away = pl.multiple_of((chip + 1 - core) * rows, rows)
        home = pl.multiple_of((chip + core) * rows, rows)
        left = jnp.concatenate([n_ref[:, pl.ds(away, rows)], n_ref[:, pl.ds(home, rows)]], axis=1)
        grad = mm_tn(left, dgu_ref[...]).astype(BF)
        away_ref[i, :, :split] = grad[:rows]
        home_ref[i, :, :split] = grad[rows:]
        left = jnp.concatenate([d_ref[:, pl.ds(away, rows)], d_ref[:, pl.ds(home, rows)]], axis=1)
        grad = mm_tn(left, hid_ref[...]).astype(BF)
        away_ref[i, :, split:] = grad[:rows]
        home_ref[i, :, split:] = grad[rows:]


def ffn_grads(index, first, count, n_all, d_all, hid_all, dgu_all):
    rows = n_all.shape[1] // 8
    columns = hid_all.shape[1] + dgu_all.shape[1]
    return whole_call(
        functools.partial(ffn_grad_kernel, first, count),
        "ffn_grads",
        [shape(count, rows, columns)] * 2,
        (index, n_all, d_all, hid_all, dgu_all),
        scalars=1,
    )


def core_sum(away, home, count, tag):
    other = dp_swap(away, 1, tag)
    return [(home[kq].astype(F32) + other[kq].astype(F32)).astype(BF) for kq in range(count)]


def body(
    layer_in,
    cotangent,
    row_counts,
    tail_tokens,
    row_order,
    gain_one,
    w_in,
    kernel,
    w_out,
    gain_two,
    w_gu,
    w_down,
):
    row_count, own_len, width = layer_in.shape
    n_dp, n_z = lax.axis_size("dp"), lax.axis_size("tensor")
    outer = n_dp // INNER
    me, z = lax.axis_index("dp"), lax.axis_index("tensor")
    me_in = me // outer
    row_len = own_len * n_z
    channels = w_in.shape[2]
    reach = kernel.shape[0] - 1
    tokens = row_count * own_len
    block = width // INNER
    units = w_down.shape[0]
    index = jnp.stack([me_in, z]).astype(jnp.int32)

    given = lax.dynamic_slice_in_dim(row_order, me * row_count, row_count)
    starts = jnp.cumsum(row_counts) - row_counts
    ends = starts + row_counts - 1
    is_first = jnp.any(starts[None, :] == given[:, None], axis=1)
    at_end = ends[None, :] == given[:, None]
    row_valid = jnp.where(
        jnp.any(at_end, axis=1),
        jnp.sum(jnp.where(at_end, tail_tokens[None, :], 0), axis=1),
        row_len,
    )
    positions = z * own_len + jnp.arange(own_len, dtype=jnp.int32)
    valid = positions[None, :] < row_valid[:, None]

    small = jnp.concatenate([gain_one[None], gain_two[None], kernel], axis=0)
    mix_own = jnp.stack([w_in[:, 0], w_in[:, 2], w_in[:, 1], w_out.T])
    ffn_own = jnp.concatenate([w_gu[:, 0], w_gu[:, 1], w_down.T], axis=1)
    groups = [[i * outer + o for o in range(outer)] for i in range(INNER)]
    tails = layer_in[:, own_len - reach :].reshape(row_count * reach, width)
    tails = z_shift(tails, 1, "tail")
    if outer > 1:
        wide = functools.partial(lax.all_gather, axis_name="dp", tiled=True, axis_index_groups=groups)
        mix_own, small = wide(mix_own, axis=1), wide(small, axis=1)
        ffn_own, tails = wide(ffn_own, axis=0), wide(tails, axis=0)
    n_small = small.shape[0]
    small = jnp.pad(small, ((0, 16 - n_small), (0, 0)))
    mix_own = after(mix_own.reshape(4 * block, channels), ffn_own)

    mix_far, mix_near = z_send(mix_own, "mix", (2, 1))
    ffn_x, ffn_y = plane_gather(ffn_own, "ffn")
    mix_last = z_swap(mix_far, 1, "mix_on")
    d_ffn = jnp.where(valid[:, :, None], cotangent, jnp.zeros_like(cotangent)).reshape(tokens, width)
    tails = after(tails, d_ffn)
    mix_rows = stack_mixer(index, small, tails, [mix_own, mix_near, mix_far, mix_last])

    mix_rows = after(mix_rows, ffn_x, ffn_y)
    mix_x, mix_y = plane_gather(mix_rows, "mix")
    dy_far, dy_near = z_send(d_ffn, "dy", (2, 1), mix_last)
    mix_pairs = [mix_rows, dp_swap(mix_rows, 1, "mix")]
    ffn_pairs = [ffn_own, dp_swap(ffn_own, 1, "ffn")]
    ffn_pairs += [ffn_x, dp_swap(after(ffn_x, ffn_pairs[1]), 1, "ffn")]
    mix_d = plane_corner(mix_x, mix_y, "mix", dy_far, dy_near, ffn_pairs[1])
    ffn_pairs += [ffn_y, dp_swap(after(ffn_y, ffn_pairs[3]), 1, "ffn")]
    dy_set = [dy_near, dy_far, z_swap(dy_far, 1, "dy_on")]
    mix_pairs += [mix_x, dp_swap(mix_x, 1, "mix"), mix_y, dp_swap(mix_y, 1, "mix")]
    mix_pairs += [mix_d, dp_swap(after(mix_d, ffn_pairs[3], dy_set[2]), 1, "mix")]
    w_b, w_u, w_c, w_o, small_all, every = place_mixer(index, mix_pairs, block, 16, tails.shape[0])

    slots = INNER * outer * row_count
    rel = jnp.bitwise_xor(me_in, jnp.arange(INNER, dtype=jnp.int32))
    slot_rows = row_order.reshape(INNER, outer * row_count)[rel].reshape(slots)
    wanted = jnp.where(z == 0, jnp.where(is_first, -1, given - 1), given)
    picks = jnp.repeat(wanted, reach)[:, None] == jnp.repeat(slot_rows, reach)[None, :]
    picks = jnp.logical_and(
        picks, jnp.arange(row_count * reach)[:, None] % reach == jnp.arange(slots * reach)[None, :] % reach
    ).astype(BF)
    x_halo = mm(picks, every).astype(BF)
    x_own = layer_in.reshape(tokens, width)
    n_one, n_halo, b_own, u_own, b_halo, u_halo, mixed, mixed_halo, conv = mixer_in(
        own_len, x_own, x_halo, small_all, w_b, w_u
    )
    c_own, gated, middle, n_two = mixer_out(x_own, n_one, conv, small_all, w_c, w_o)

    ffn_d = plane_corner(ffn_x, ffn_y, "ffn", mix_d)
    n_two_far, n_two_near = z_send(n_two, "n2", (2, 1))
    n_two_set = [n_two, n_two_near, n_two_far]
    ffn_pairs += [ffn_d, dp_swap(after(ffn_d, n_two), 1, "ffn")]
    w_ffn = place_ffn(index, ffn_pairs)
    d_ffn_set = [d_ffn] + dy_set
    d_parts, out_parts, kept = [], [], ()
    for s in range(n_z):
        d_part, out_part, *kept = ffn_piece(s, n_z, n_two_set[s], d_ffn_set[s], w_ffn, kept)
        d_parts.append(d_part)
        out_parts.append(out_part)
        if s == 0:
            n_two_set.append(z_swap(after(n_two_far, d_part), 1, "n2_on"))
    d_on = z_swap(d_parts[3], 1, "dn_on")
    away, home = ffn_grads(index, 0, 4, *kept)
    d_on = after(d_on, away).astype(F32) + d_parts[2].astype(F32)
    d_near = z_swap(after(d_parts[1], n_two_set[3]), 1, "dn")
    d_parts = [d_parts[0], d_near, z_swap(d_on.astype(BF), 2, "dn")]

    ffn_pieces = core_sum(away, home, 4, "gf")
    ffn_across = plane_far(ffn_pieces, "gf")
    out_on = z_swap(after(out_parts[3], d_near), 1, "out_on")
    out_first = z_swap(after(out_parts[1], d_near), 1, "out")
    d_mix, d_b, d_u, d_c, d_b_halo, d_u_halo, grad_mid, d_x_halo, small_grads = mixer_back(
        own_len,
        d_parts,
        (middle, d_ffn, x_own, x_halo, small_all, b_own, u_own, c_own, b_halo, u_halo, mixed, mixed_halo, conv),
        (w_b, w_u, w_c, w_o),
    )

    co_away, co_home = mixer_grads(index, (after(n_one, ffn_pieces[3]), d_c, d_mix, gated), block, False)
    d_bu_halo = jnp.concatenate([d_b_halo, d_u_halo], axis=1)
    spread = mm_tn(picks, d_x_halo).astype(BF)
    bu_away, bu_home = mixer_grads(
        index, (after(n_one, co_away), d_b, n_one, d_u, n_halo, d_bu_halo, small_grads, spread), block, True
    )
    co_pieces = core_sum(after(co_away, out_on), co_home, 4, "gco")
    out_second = (out_parts[2].astype(F32) + out_on.astype(F32)).astype(BF)
    out_second = z_swap(out_second, 2, "out")
    co_across = plane_far(co_pieces, "gco")
    co_terms = plane_near(co_pieces, co_across, "gco")
    bu_pieces = core_sum(after(bu_away, co_pieces[0]), bu_home, 4, "gbu")
    bu_across = plane_far(bu_pieces, "gbu")
    bu_terms = plane_near(bu_pieces, bu_across, "gbu")
    ffn_terms = plane_near(ffn_pieces, ffn_across, "gf", bu_across)
    layer_out = middle + out_parts[0].astype(F32) + out_first.astype(F32) + out_second.astype(F32)
    layer_out = layer_out.astype(BF).reshape(row_count, own_len, width)

    def z_parts(terms, tag, *waits):
        first = after(terms[0], *waits) if waits else terms[0]
        parts = split_z(index, (first, *terms[1:]), 2 * block, n_z)
        return [parts[0]] + [z_swap(parts[s], s, tag) for s in range(1, n_z)]

    co_parts = z_parts(co_terms, "gco", out_first, out_second)
    ffn_total = sum(term.astype(F32) for term in ffn_terms)
    if outer > 1:
        narrow = functools.partial(
            lax.psum_scatter, axis_name="dp", tiled=True, axis_index_groups=groups
        )
        ffn_total = narrow(ffn_total, scatter_dimension=0)
    grad_w_gu = jnp.stack([ffn_total[:, :units], ffn_total[:, units : 2 * units]], axis=1)
    grad_w_down = ffn_total[:, 2 * units :].T
    bu_parts = z_parts(bu_terms, "gbu", co_parts[0])
    if outer > 1:
        bu_total = sum(part.astype(F32) for part in bu_parts)
        grad_co = sum(part.astype(F32) for part in co_parts).reshape(2, block, channels)
        grad_co = narrow(grad_co, scatter_dimension=1)
        grad_bu = narrow(bu_total[: 2 * block].reshape(2, block, channels), scatter_dimension=1)
        grad_small = narrow(bu_total[2 * block : 2 * block + n_small, :block], scatter_dimension=1)
        returned = bu_total[2 * block + 16 :].reshape(n_z, -1, channels)
        returned = narrow(jnp.moveaxis(returned, 0, 1).reshape(-1, width), scatter_dimension=0)
        grad_w_in = jnp.stack([grad_bu[0], grad_co[0], grad_bu[1]])
        grad_w_out = grad_co[1].T
        grad_in = grad_mid.reshape(row_count, own_len, width)
        grad_in = grad_in + jnp.pad(
            returned.reshape(row_count, reach, width), ((0, 0), (own_len - reach, 0), (0, 0))
        )
        grad_in = grad_in.astype(BF)
    else:
        grad_c, grad_w_out = finish_co(co_parts)
        grad_w_in, grad_small, grad_in = finish_bu(bu_parts, grad_c, grad_mid, own_len, reach)
        grad_in = grad_in.reshape(row_count, own_len, width)
    return (
        layer_out,
        grad_in,
        grad_small[0],
        jnp.swapaxes(grad_w_in, 0, 1),
        grad_small[2:n_small],
        grad_w_out,
        grad_small[1],
        grad_w_gu,
        grad_w_down,
    )


def solution(mesh):
    in_specs = (
        P("dp", "tensor", None),
        P("dp", "tensor", None),
        P(),
        P(),
        P(),
        P("dp"),
        P("dp", None, "tensor"),
        P(None, "dp"),
        P("tensor", "dp"),
        P("dp"),
        P("dp", None, "tensor"),
        P("tensor", "dp"),
    )
    out_specs = (
        P("dp", "tensor", None),
        P("dp", "tensor", None),
        P("dp"),
        P("dp", None, "tensor"),
        P(None, "dp"),
        P("tensor", "dp"),
        P("dp"),
        P("dp", None, "tensor"),
        P("tensor", "dp"),
    )
    return jax.shard_map(body, mesh=mesh, in_specs=in_specs, out_specs=out_specs, check_vma=False)
```

```python
import functools
import jax
import jax.numpy as jnp
from jax import lax
from jax.experimental import pallas as pl
from jax.experimental.pallas import tpu as pltpu
from jax.sharding import PartitionSpec as P

EPS = 1e-05
INNER = 8
BF = jnp.bfloat16
F32 = jnp.float32
VMEM_LIMIT = 12 << 20


def hold_kernel(*refs):
    pass


def hold(value, *events):
    anywhere = pl.BlockSpec(memory_space=pl.ANY)
    return pl.pallas_call(
        hold_kernel,
        out_shape=shape(*value.shape, dtype=value.dtype),
        in_specs=[anywhere] * (1 + len(events)),
        out_specs=anywhere,
        input_output_aliases={0: 0},
        cost_estimate=pl.CostEstimate(flops=1, bytes_accessed=1, transcendentals=0),
        name="hold",
    )(value, *events)


def dp_swap(value, step, tag):
    size = lax.axis_size("dp")
    hop = step * (size // INNER)
    with jax.named_scope(f"{tag}_dp{step}"):
        return lax.ppermute(value, "dp", [(i, i ^ hop) for i in range(size)])


def z_shift(value, step, tag):
    size = lax.axis_size("tensor")
    with jax.named_scope(f"{tag}_z"):
        return lax.ppermute(value, "tensor", [(i, (i + step) % size) for i in range(size)])


def z_swap(value, step, tag):
    size = lax.axis_size("tensor")
    with jax.named_scope(f"{tag}_z{step}"):
        return lax.ppermute(value, "tensor", [(i, i ^ step) for i in range(size)])


def after(value, *events):
    return lax.optimization_barrier((value,) + events)[0]


def mm(a, b):
    return lax.dot_general(a, b, (((1,), (0,)), ((), ())), preferred_element_type=F32)


def mm_nt(a, b):
    return lax.dot_general(a, b, (((1,), (1,)), ((), ())), preferred_element_type=F32)


def mm_tn(a, b):
    return lax.dot_general(a, b, (((0,), (0,)), ((), ())), preferred_element_type=F32)


def shape(*dims, dtype=BF):
    return jax.ShapeDtypeStruct(dims, dtype)


def whole_call(kernel, name, outs, args, scalars=0, hbm=0, scratch=(), alias=None, weight=0):
    specs = [pl.BlockSpec(memory_space=pltpu.SMEM)] * scalars
    specs += [pl.BlockSpec(memory_space=pltpu.HBM)] * hbm
    specs += [pl.BlockSpec(memory_space=pltpu.VMEM)] * (len(args) - scalars - hbm)
    return pl.pallas_call(
        kernel,
        out_shape=outs,
        in_specs=specs,
        out_specs=[pl.BlockSpec(memory_space=pltpu.VMEM)] * len(outs),
        scratch_shapes=list(scratch),
        input_output_aliases=alias or {},
        compiler_params=pltpu.CompilerParams(vmem_limit_bytes=VMEM_LIMIT),
        cost_estimate=pl.CostEstimate(flops=1 + weight, bytes_accessed=1, transcendentals=0),
        name=name,
    )(*args)


def corner(value, tag):
    size = lax.axis_size("dp")
    outer = size // INNER
    pairs = []
    for i in range(size):
        hop = 2 if (i // outer) % 2 else 4
        pairs.append((i, i ^ (hop * outer)))
    with jax.named_scope(f"{tag}_corner"):
        return lax.ppermute(value, "dp", pairs)


def core_zero():
    return lax.axis_index("dp") // (lax.axis_size("dp") // INNER) % 2 == 0


def plane_gather(local, tag, *waits):
    local = after(local, *waits) if waits else local
    return dp_swap(local, 2, tag), dp_swap(local, 4, tag)


def plane_corner(over_x, over_y, tag, *waits):
    value = jnp.where(core_zero(), over_x, over_y)
    return corner(after(value, *waits) if waits else value, tag)


def plane_far(pieces, tag, *waits):
    far = hold(pieces[3], *waits) if waits else pieces[3]
    return corner(far, tag)


def plane_near(pieces, far, tag, *waits):
    far = far.astype(F32)
    first = core_zero()
    over_x = (pieces[1].astype(F32) + jnp.where(first, far, 0.0)).astype(BF)
    over_y = (pieces[2].astype(F32) + jnp.where(first, 0.0, far)).astype(BF)
    if waits:
        over_x, over_y = after(over_x, *waits), after(over_y, *waits)
    return pieces[0], dp_swap(over_x, 2, tag), dp_swap(over_y, 4, tag)


def z_send(local, tag, steps, *waits):
    local = after(local, *waits) if waits else local
    return [z_swap(local, step, tag) for step in steps]


def stack_mixer_kernel(idx_ref, small_ref, tail_ref, *refs):
    parts, out_ref = refs[:-1], refs[-1]
    z = idx_ref[1]
    rows, ch = parts[0].shape
    for s, part in enumerate(parts):
        col = pl.multiple_of(jnp.bitwise_xor(z, s) * ch, ch)
        out_ref[:rows, pl.ds(col, ch)] = part[...]
    n_small, block = small_ref.shape
    out_ref[rows : rows + n_small] = jnp.zeros((n_small, out_ref.shape[1]), BF)
    out_ref[rows : rows + n_small, :block] = small_ref[...]
    out_ref[rows + n_small :] = tail_ref[...]


def stack_mixer(index, small, tail, parts):
    rows, ch = parts[0].shape
    return whole_call(
        stack_mixer_kernel,
        "stack_mixer",
        [shape(rows + small.shape[0] + tail.shape[0], len(parts) * ch)],
        (index, small, tail, *parts),
        scalars=1,
    )[0]


def place_mixer_kernel(block, idx_ref, *refs):
    pieces, outs, sems = refs[:8], refs[8:-1], refs[-1]
    small_ref, tail_ref = outs[4], outs[5]
    me = idx_ref[0]
    n_small, n_tail = small_ref.shape[0], tail_ref.shape[0] // 8
    copies = []
    for k in range(8):
        at = pl.multiple_of(jnp.bitwise_xor(me, k) * block, block)
        for st in range(4):
            copies.append(
                pltpu.make_async_copy(
                    pieces[k].at[pl.ds(st * block, block)], outs[st].at[pl.ds(at, block)], sems.at[k, st]
                )
            )
        copies.append(
            pltpu.make_async_copy(
                pieces[k].at[pl.ds(4 * block, n_small), pl.ds(0, block)],
                small_ref.at[:, pl.ds(at, block)],
                sems.at[k, 4],
            )
        )
        copies.append(
            pltpu.make_async_copy(
                pieces[k].at[pl.ds(4 * block + n_small, n_tail)],
                tail_ref.at[pl.ds(k * n_tail, n_tail)],
                sems.at[k, 5],
            )
        )
    for copy in copies:
        copy.start()
    for copy in copies:
        copy.wait()


def place_mixer(index, pieces, block, n_small, n_tail):
    width = pieces[0].shape[1]
    return whole_call(
        functools.partial(place_mixer_kernel, block),
        "place_mixer",
        [shape(8 * block, width)] * 4 + [shape(n_small, 8 * block), shape(8 * n_tail, width)],
        (index, *pieces),
        scalars=1,
        hbm=8,
        scratch=[pltpu.SemaphoreType.DMA((8, 6))],
    )


def place_ffn_kernel(idx_ref, *refs):
    pieces, out_ref, sems = refs[:8], refs[8], refs[9]
    me = idx_ref[0]
    rows = out_ref.shape[0] // 8
    copies = []
    for k in range(8):
        at = pl.ds(pl.multiple_of(jnp.bitwise_xor(me, k) * rows, rows), rows)
        copies.append(pltpu.make_async_copy(pieces[k], out_ref.at[at], sems.at[k]))
    for copy in copies:
        copy.start()
    for copy in copies:
        copy.wait()


def place_ffn(index, pieces):
    rows, columns = pieces[0].shape
    return whole_call(
        place_ffn_kernel,
        "place_ffn",
        [shape(8 * rows, columns)],
        (index, *pieces),
        scalars=1,
        hbm=8,
        scratch=[pltpu.SemaphoreType.DMA((8,))],
    )[0]


def ffn_kernel(step, n_ref, d_ref, w_ref, *refs):
    dn_ref, part_ref, n_all_ref, d_all_ref, hid_ref, dgu_ref = refs[-6:]
    tokens = n_ref.shape[0]
    own = slice(step * tokens, (step + 1) * tokens)
    units, width = w_ref.shape[1] // 3, w_ref.shape[0]
    wide, tall = units // 3, width // 4
    n_all_ref[own] = n_ref[...]
    d_all_ref[own] = d_ref[...]

    @pl.loop(0, 3)
    def _(i):
        one = pl.multiple_of(i * wide, wide)
        two, three = pl.multiple_of(one + units, wide), pl.multiple_of(one + 2 * units, wide)
        gate = mm(n_ref[...], w_ref[:, pl.ds(one, wide)])
        up = mm(n_ref[...], w_ref[:, pl.ds(two, wide)])
        sig = jax.nn.sigmoid(gate)
        silu = gate * sig
        hid_ref[own, pl.ds(one, wide)] = (silu * up).astype(BF)
        d_hidden = mm(d_ref[...], w_ref[:, pl.ds(three, wide)])
        d_gate = d_hidden * up * (sig * (1.0 + gate * (1.0 - sig)))
        dgu_ref[own, pl.ds(one, wide)] = d_gate.astype(BF)
        dgu_ref[own, pl.ds(two, wide)] = (d_hidden * silu).astype(BF)

    @pl.loop(0, 4)
    def _(i):
        rows = pl.ds(pl.multiple_of(i * tall, tall), tall)
        dn_ref[:, rows] = mm_nt(dgu_ref[own], w_ref[rows, : 2 * units]).astype(BF)
        part_ref[:, rows] = mm_nt(hid_ref[own], w_ref[rows, 2 * units :]).astype(BF)


def ffn_whole_kernel(step, n_ref, d_ref, w_ref, *refs):
    dn_ref, part_ref, n_all_ref, d_all_ref, hid_ref, dgu_ref = refs[-6:]
    tokens = n_ref.shape[0]
    own = slice(step * tokens, (step + 1) * tokens)
    units = w_ref.shape[1] // 3
    gu, down = slice(0, 2 * units), slice(2 * units, 3 * units)
    n_all_ref[own] = n_ref[...]
    d_all_ref[own] = d_ref[...]
    both = mm(n_ref[...], w_ref[:, gu])
    gate, up = both[:, :units], both[:, units:]
    sig = jax.nn.sigmoid(gate)
    silu = gate * sig
    hidden = (silu * up).astype(BF)
    hid_ref[own] = hidden
    d_hidden = mm(d_ref[...], w_ref[:, down])
    dgu_ref[own, :units] = (d_hidden * up * (sig * (1.0 + gate * (1.0 - sig)))).astype(BF)
    dgu_ref[own, units:] = (d_hidden * silu).astype(BF)
    dn_ref[...] = mm_nt(dgu_ref[own], w_ref[:, gu]).astype(BF)
    part_ref[...] = mm_nt(hidden, w_ref[:, down]).astype(BF)


def ffn_piece(step, steps, normed, d_out, weights, kept):
    tokens, width = normed.shape
    units = weights.shape[1] // 3
    every = steps * tokens
    return whole_call(
        functools.partial(ffn_kernel if step < 2 else ffn_whole_kernel, step),
        "ffn_piece",
        [shape(tokens, width)] * 2
        + [shape(every, width), shape(every, width), shape(every, units), shape(every, 2 * units)],
        (normed, d_out, weights, *kept),
        alias={3 + i: 2 + i for i in range(len(kept))},
    )


def norm_scale(value):
    return lax.rsqrt(jnp.mean(value * value, axis=-1, keepdims=True) + EPS)


def norm_back(d_normed, value, scale, gain):
    weighted = d_normed * gain
    d_value = scale * weighted - value * (scale * scale * scale) * jnp.mean(
        weighted * value, axis=-1, keepdims=True
    )
    return d_value, jnp.sum(d_normed * value * scale, axis=0, keepdims=True)


def halo_picks(tokens, own_len, halo):
    token = lax.broadcasted_iota(jnp.int32, (tokens, halo), 0)
    slot = lax.broadcasted_iota(jnp.int32, (tokens, halo), 1)
    run, pos = token // own_len, token % own_len
    one = jnp.logical_and(pos == 0, slot == 2 * run + 1)
    two = jnp.logical_and(pos < 2, slot == 2 * run + pos)
    return one.astype(BF), two.astype(BF)


def earlier(mixed, mixed_halo, own_len):
    tokens = mixed.shape[0]
    pick_one, pick_two = halo_picks(tokens, own_len, mixed_halo.shape[0])
    pos = lax.broadcasted_iota(jnp.int32, mixed.shape, 0) % own_len
    one = jnp.where(pos == 0, mm(pick_one, mixed_halo), pltpu.roll(mixed, 1, axis=0))
    two = jnp.where(pos < 2, mm(pick_two, mixed_halo), pltpu.roll(mixed, 2, axis=0))
    return one, two


def mixer_in_kernel(
    own_len, x_ref, xh_ref, small_ref, wb_ref, wu_ref, n_ref, nh_ref, b_ref, u_ref, bh_ref, uh_ref, mix_ref, mixh_ref, conv_ref
):
    gain = small_ref[0:1].astype(F32)
    x, xh = x_ref[...].astype(F32), xh_ref[...].astype(F32)
    n_ref[...] = (x * norm_scale(x) * gain).astype(BF)
    nh_ref[...] = (xh * norm_scale(xh) * gain).astype(BF)
    b_ref[...] = mm(n_ref[...], wb_ref[...])
    u_ref[...] = mm(n_ref[...], wu_ref[...])
    bh_ref[...] = mm(nh_ref[...], wb_ref[...])
    uh_ref[...] = mm(nh_ref[...], wu_ref[...])
    mix_ref[...] = (b_ref[...] * u_ref[...]).astype(BF)
    mixh_ref[...] = (bh_ref[...] * uh_ref[...]).astype(BF)
    mixed = mix_ref[...].astype(F32)
    one, two = earlier(mixed, mixh_ref[...], own_len)
    taps = [small_ref[2 + k : 3 + k].astype(F32) for k in range(3)]
    conv_ref[...] = taps[0] * two + taps[1] * one + taps[2] * mixed


def mixer_in(own_len, x, x_halo, small, w_b, w_u):
    (tokens, width), halo, ch = x.shape, x_halo.shape[0], w_b.shape[1]
    return whole_call(
        functools.partial(mixer_in_kernel, own_len),
        "mixer_in",
        [
            shape(tokens, width),
            shape(halo, width),
            shape(tokens, ch, dtype=F32),
            shape(tokens, ch, dtype=F32),
            shape(halo, ch, dtype=F32),
            shape(halo, ch, dtype=F32),
            shape(tokens, ch),
            shape(halo, ch),
            shape(tokens, ch, dtype=F32),
        ],
        (x, x_halo, small, w_b, w_u),
    )


def mixer_out_kernel(x_ref, n_ref, conv_ref, small_ref, wc_ref, wo_ref, c_ref, gated_ref, mid_ref, n2_ref):
    c_ref[...] = mm(n_ref[...], wc_ref[...])
    gated_ref[...] = (c_ref[...] * conv_ref[...]).astype(BF)
    mid = x_ref[...].astype(F32) + mm_nt(gated_ref[...], wo_ref[...])
    mid_ref[...] = mid
    n2_ref[...] = (mid * norm_scale(mid) * small_ref[1:2].astype(F32)).astype(BF)


def mixer_out(x, n_one, conv, small, w_c, w_o):
    (tokens, width), ch = x.shape, w_c.shape[1]
    return whole_call(
        mixer_out_kernel,
        "mixer_out",
        [
            shape(tokens, ch, dtype=F32),
            shape(tokens, ch),
            shape(tokens, width, dtype=F32),
            shape(tokens, width),
        ],
        (x, n_one, conv, small, w_c, w_o),
    )


def mixer_back_kernel(own_len, n_parts, *refs):
    parts = refs[:n_parts]
    (mid_ref, dy_ref, x_ref, xh_ref, small_ref, b_ref, u_ref, c_ref, bh_ref, uh_ref, mix_ref, mixh_ref, conv_ref) = refs[
        n_parts : n_parts + 13
    ]
    wb_ref, wu_ref, wc_ref, wo_ref = refs[n_parts + 13 : n_parts + 17]
    dmix_ref, db_ref, du_ref, dc_ref, dbh_ref, duh_ref, gin_ref, dxh_ref, sg_ref = refs[n_parts + 17 :]
    gain_one, gain_two = small_ref[0:1].astype(F32), small_ref[1:2].astype(F32)
    taps = [small_ref[2 + k : 3 + k].astype(F32) for k in range(3)]
    d_n2 = parts[0][...].astype(F32)
    for part in parts[1:]:
        d_n2 = d_n2 + part[...].astype(F32)
    mid = mid_ref[...]
    d_mid, g_two = norm_back(d_n2, mid, norm_scale(mid), gain_two)
    d_mid = d_mid + dy_ref[...].astype(F32)
    dmix_ref[...] = d_mid.astype(BF)
    d_gated = mm(dmix_ref[...], wo_ref[...])
    dc_ref[...] = (d_gated * conv_ref[...]).astype(BF)
    d_conv = d_gated * c_ref[...]
    mixed = mix_ref[...].astype(F32)
    one, two = earlier(mixed, mixh_ref[...], own_len)
    tap_rows = [jnp.sum(d_conv * view, axis=0, keepdims=True) for view in (two, one, mixed)]
    tokens = mixed.shape[0]
    pos = lax.broadcasted_iota(jnp.int32, mixed.shape, 0) % own_len
    d_mixed = taps[2] * d_conv
    d_mixed = d_mixed + taps[1] * jnp.where(pos < own_len - 1, pltpu.roll(d_conv, tokens - 1, axis=0), 0.0)
    d_mixed = d_mixed + taps[0] * jnp.where(pos < own_len - 2, pltpu.roll(d_conv, tokens - 2, axis=0), 0.0)
    db_ref[...] = (d_mixed * u_ref[...]).astype(BF)
    du_ref[...] = (d_mixed * b_ref[...]).astype(BF)
    pick_one, pick_two = halo_picks(tokens, own_len, mixh_ref.shape[0])
    low = d_conv.astype(BF)
    d_halo = taps[1] * mm_tn(pick_one, low) + taps[0] * mm_tn(pick_two, low)
    dbh_ref[...] = (d_halo * uh_ref[...]).astype(BF)
    duh_ref[...] = (d_halo * bh_ref[...]).astype(BF)
    d_n1 = mm_nt(db_ref[...], wb_ref[...]) + mm_nt(du_ref[...], wu_ref[...]) + mm_nt(dc_ref[...], wc_ref[...])
    x, xh = x_ref[...].astype(F32), xh_ref[...].astype(F32)
    d_x, g_one = norm_back(d_n1, x, norm_scale(x), gain_one)
    gin_ref[...] = d_x + d_mid
    d_nh = mm_nt(dbh_ref[...], wb_ref[...]) + mm_nt(duh_ref[...], wu_ref[...])
    d_xh, g_halo = norm_back(d_nh, xh, norm_scale(xh), gain_one)
    dxh_ref[...] = d_xh.astype(BF)
    for row, value in enumerate([g_one + g_halo, g_two] + tap_rows):
        sg_ref[row : row + 1] = value
    sg_ref[5:8] = jnp.zeros((3, sg_ref.shape[1]), F32)


def mixer_back(own_len, parts, saved, weights):
    (tokens, width), ch = parts[0].shape, weights[0].shape[1]
    halo = saved[3].shape[0]
    return whole_call(
        functools.partial(mixer_back_kernel, own_len, len(parts)),
        "mixer_back",
        [shape(tokens, width)]
        + [shape(tokens, ch)] * 3
        + [shape(halo, ch)] * 2
        + [shape(tokens, width, dtype=F32), shape(halo, width), shape(8, width, dtype=F32)],
        (*parts, *saved, *weights),
        weight=60000000000,
    )


def mixer_grad_kernel(with_halo, idx_ref, *refs):
    n_in = 8 if with_halo else 4
    ins, away_ref, home_ref = refs[:n_in], refs[n_in], refs[n_in + 1]
    me = idx_ref[0]
    quad, core = me // 2, lax.rem(me, 2)
    width = away_ref.shape[2]
    rows = ins[0].shape[1] // 8

    @pl.loop(0, 4)
    def _(kq):
        chip = jnp.bitwise_xor(quad, kq) * 2
        away = pl.multiple_of((chip + 1 - core) * rows, rows)
        home = pl.multiple_of((chip + core) * rows, rows)
        for st in range(2):
            left_ref, right_ref = ins[2 * st], ins[2 * st + 1]
            left = jnp.concatenate([left_ref[:, pl.ds(away, rows)], left_ref[:, pl.ds(home, rows)]], axis=1)
            grad = mm_tn(left, right_ref[...])
            if with_halo:
                nh_ref = ins[4]
                left = jnp.concatenate([nh_ref[:, pl.ds(away, rows)], nh_ref[:, pl.ds(home, rows)]], axis=1)
                grad = grad + mm_tn(left, ins[5][:, st * width : (st + 1) * width])
            grad = grad.astype(BF)
            away_ref[kq, st * rows : (st + 1) * rows] = grad[:rows]
            home_ref[kq, st * rows : (st + 1) * rows] = grad[rows:]
        if with_halo:
            n_tail = ins[7].shape[0] // 8
            for ref, at, k in ((away_ref, away, 2 * kq + 1), (home_ref, home, 2 * kq)):
                values = ins[6][:, pl.ds(at, rows)]
                values = jnp.concatenate([values, jnp.zeros_like(values)], axis=0)
                ref[kq, 2 * rows : 2 * rows + 16] = jnp.zeros((16, width), BF)
                ref[kq, 2 * rows : 2 * rows + 16, :rows] = values.astype(BF)
                ref[kq, 2 * rows + 16 :] = ins[7][pl.ds(pl.multiple_of(k * n_tail, n_tail), n_tail)]


def mixer_grads(index, ins, rows, with_halo):
    extra = 16 + ins[7].shape[0] // 8 if with_halo else 0
    return whole_call(
        functools.partial(mixer_grad_kernel, with_halo),
        "grads_in" if with_halo else "grads_out",
        [shape(4, 2 * rows + extra, ins[1].shape[1])] * 2,
        (index, *ins),
        scalars=1,
    )


def split_kernel(rows, idx_ref, *refs):
    terms, outs = refs[:3], refs[3:]
    z = idx_ref[1]
    n_z = len(outs)
    ch = terms[0].shape[1] // n_z
    n_tail = terms[0].shape[0] - rows - 16
    ahead = jnp.bitwise_xor(z, lax.rem(z + n_z - 1, n_z))

    def total(at, col):
        return sum(term[at, col].astype(F32) for term in terms).astype(BF)

    for s, out in enumerate(outs):
        out[:rows] = total(slice(0, rows), pl.ds(pl.multiple_of(jnp.bitwise_xor(z, s) * ch, ch), ch))
        if n_tail > 0:
            out[rows : rows + 16] = total(slice(rows, rows + 16), slice(0, ch))
            for c in range(n_z):
                value = total(slice(rows + 16, rows + 16 + n_tail), slice(c * ch, (c + 1) * ch))
                at = rows + 16 + c * n_tail
                out[at : at + n_tail] = jnp.where(ahead == s, value, jnp.zeros_like(value))


def split_z(index, terms, rows, n_z):
    every, width = terms[0].shape
    extra = 16 + (every - rows - 16) * n_z if every > rows else 0
    return whole_call(
        functools.partial(split_kernel, rows),
        "split_z",
        [shape(rows + extra, width // n_z)] * n_z,
        (index, *terms),
        scalars=1,
    )


def finish_co_kernel(*refs):
    parts, (c_ref, out_ref) = refs[:-2], refs[-2:]
    block = c_ref.shape[0]
    total = sum(part[...].astype(F32) for part in parts)
    c_ref[...] = total[:block]
    out_ref[...] = total[block:].T


def finish_co(parts):
    rows, ch = parts[0].shape
    outs = [shape(rows // 2, ch, dtype=F32), shape(ch, rows // 2, dtype=F32)]
    return whole_call(finish_co_kernel, "finish_co", outs, tuple(parts))


def finish_bu_kernel(own_len, reach, *refs):
    n_z = len(refs) - 5
    parts = refs[:n_z]
    c_ref, mid_ref, w_ref, small_ref, in_ref = refs[n_z:]
    block, ch = c_ref.shape
    tokens = mid_ref.shape[0]

    def total(lo, hi):
        return sum(part[lo:hi].astype(F32) for part in parts)

    w_ref[0] = total(0, block)
    w_ref[1] = c_ref[...]
    w_ref[2] = total(block, 2 * block)
    small_ref[...] = total(2 * block, 2 * block + 16)[:8, :block]
    n_tail = tokens // own_len * reach
    token = lax.broadcasted_iota(jnp.int32, (tokens, n_tail), 0)
    slot = lax.broadcasted_iota(jnp.int32, (tokens, n_tail), 1)
    ahead = own_len - reach + slot % reach
    spread = jnp.logical_and(token // own_len == slot // reach, token % own_len == ahead).astype(BF)
    for c in range(n_z):
        lo = 2 * block + 16 + c * n_tail
        cols = slice(c * ch, (c + 1) * ch)
        back = mm(spread, total(lo, lo + n_tail).astype(BF))
        in_ref[:, cols] = (mid_ref[:, cols] + back).astype(BF)


def finish_bu(parts, grad_c, grad_mid, own_len, reach):
    block, ch = grad_c.shape
    return whole_call(
        functools.partial(finish_bu_kernel, own_len, reach),
        "finish_bu",
        [shape(3, block, ch, dtype=F32), shape(8, block, dtype=F32), shape(*grad_mid.shape)],
        (*parts, grad_c, grad_mid),
    )


def ffn_grad_kernel(first, count, idx_ref, n_ref, d_ref, hid_ref, dgu_ref, away_ref, home_ref):
    me = idx_ref[0]
    quad, core = me // 2, lax.rem(me, 2)
    rows = n_ref.shape[1] // 8
    split = dgu_ref.shape[1]

    @pl.loop(0, count)
    def _(i):
        chip = jnp.bitwise_xor(quad, first + i) * 2
        away = pl.multiple_of((chip + 1 - core) * rows, rows)
        home = pl.multiple_of((chip + core) * rows, rows)
        left = jnp.concatenate([n_ref[:, pl.ds(away, rows)], n_ref[:, pl.ds(home, rows)]], axis=1)
        grad = mm_tn(left, dgu_ref[...]).astype(BF)
        away_ref[i, :, :split] = grad[:rows]
        home_ref[i, :, :split] = grad[rows:]
        left = jnp.concatenate([d_ref[:, pl.ds(away, rows)], d_ref[:, pl.ds(home, rows)]], axis=1)
        grad = mm_tn(left, hid_ref[...]).astype(BF)
        away_ref[i, :, split:] = grad[:rows]
        home_ref[i, :, split:] = grad[rows:]


def ffn_grads(index, first, count, n_all, d_all, hid_all, dgu_all):
    rows = n_all.shape[1] // 8
    columns = hid_all.shape[1] + dgu_all.shape[1]
    return whole_call(
        functools.partial(ffn_grad_kernel, first, count),
        "ffn_grads",
        [shape(count, rows, columns)] * 2,
        (index, n_all, d_all, hid_all, dgu_all),
        scalars=1,
    )


def core_sum(away, home, count, tag):
    other = dp_swap(away, 1, tag)
    return [(home[kq].astype(F32) + other[kq].astype(F32)).astype(BF) for kq in range(count)]


def body(
    layer_in,
    cotangent,
    row_counts,
    tail_tokens,
    row_order,
    gain_one,
    w_in,
    kernel,
    w_out,
    gain_two,
    w_gu,
    w_down,
):
    row_count, own_len, width = layer_in.shape
    n_dp, n_z = lax.axis_size("dp"), lax.axis_size("tensor")
    outer = n_dp // INNER
    me, z = lax.axis_index("dp"), lax.axis_index("tensor")
    me_in = me // outer
    row_len = own_len * n_z
    channels = w_in.shape[2]
    reach = kernel.shape[0] - 1
    tokens = row_count * own_len
    block = width // INNER
    units = w_down.shape[0]
    index = jnp.stack([me_in, z]).astype(jnp.int32)

    given = lax.dynamic_slice_in_dim(row_order, me * row_count, row_count)
    starts = jnp.cumsum(row_counts) - row_counts
    ends = starts + row_counts - 1
    is_first = jnp.any(starts[None, :] == given[:, None], axis=1)
    at_end = ends[None, :] == given[:, None]
    row_valid = jnp.where(
        jnp.any(at_end, axis=1),
        jnp.sum(jnp.where(at_end, tail_tokens[None, :], 0), axis=1),
        row_len,
    )
    positions = z * own_len + jnp.arange(own_len, dtype=jnp.int32)
    valid = positions[None, :] < row_valid[:, None]

    small = jnp.concatenate([gain_one[None], gain_two[None], kernel], axis=0)
    mix_own = jnp.stack([w_in[:, 0], w_in[:, 2], w_in[:, 1], w_out.T])
    ffn_own = jnp.concatenate([w_gu[:, 0], w_gu[:, 1], w_down.T], axis=1)
    groups = [[i * outer + o for o in range(outer)] for i in range(INNER)]
    tails = layer_in[:, own_len - reach :].reshape(row_count * reach, width)
    tails = z_shift(tails, 1, "tail")
    if outer > 1:
        wide = functools.partial(lax.all_gather, axis_name="dp", tiled=True, axis_index_groups=groups)
        mix_own, small = wide(mix_own, axis=1), wide(small, axis=1)
        ffn_own, tails = wide(ffn_own, axis=0), wide(tails, axis=0)
    n_small = small.shape[0]
    small = jnp.pad(small, ((0, 16 - n_small), (0, 0)))
    mix_own = after(mix_own.reshape(4 * block, channels), ffn_own)

    mix_far, mix_near = z_send(mix_own, "mix", (2, 1))
    ffn_x, ffn_y = plane_gather(ffn_own, "ffn")
    mix_last = z_swap(mix_far, 1, "mix_on")
    d_ffn = jnp.where(valid[:, :, None], cotangent, jnp.zeros_like(cotangent)).reshape(tokens, width)
    tails = after(tails, d_ffn)
    mix_rows = stack_mixer(index, small, tails, [mix_own, mix_near, mix_far, mix_last])

    mix_rows = after(mix_rows, ffn_x, ffn_y)
    mix_x, mix_y = plane_gather(mix_rows, "mix")
    dy_far, dy_near = z_send(d_ffn, "dy", (2, 1), mix_last)
    mix_pairs = [mix_rows, dp_swap(mix_rows, 1, "mix")]
    ffn_pairs = [ffn_own, dp_swap(ffn_own, 1, "ffn")]
    ffn_pairs += [ffn_x, dp_swap(after(ffn_x, ffn_pairs[1]), 1, "ffn")]
    mix_d = plane_corner(mix_x, mix_y, "mix", dy_far, dy_near, ffn_pairs[1])
    ffn_pairs += [ffn_y, dp_swap(after(ffn_y, ffn_pairs[3]), 1, "ffn")]
    dy_set = [dy_near, dy_far, z_swap(dy_far, 1, "dy_on")]
    mix_pairs += [mix_x, dp_swap(mix_x, 1, "mix"), mix_y, dp_swap(mix_y, 1, "mix")]
    mix_pairs += [mix_d, dp_swap(after(mix_d, ffn_pairs[3], dy_set[2]), 1, "mix")]
    w_b, w_u, w_c, w_o, small_all, every = place_mixer(index, mix_pairs, block, 16, tails.shape[0])

    slots = INNER * outer * row_count
    rel = jnp.bitwise_xor(me_in, jnp.arange(INNER, dtype=jnp.int32))
    slot_rows = row_order.reshape(INNER, outer * row_count)[rel].reshape(slots)
    wanted = jnp.where(z == 0, jnp.where(is_first, -1, given - 1), given)
    picks = jnp.repeat(wanted, reach)[:, None] == jnp.repeat(slot_rows, reach)[None, :]
    picks = jnp.logical_and(
        picks, jnp.arange(row_count * reach)[:, None] % reach == jnp.arange(slots * reach)[None, :] % reach
    ).astype(BF)
    x_halo = mm(picks, every).astype(BF)
    x_own = layer_in.reshape(tokens, width)
    n_one, n_halo, b_own, u_own, b_halo, u_halo, mixed, mixed_halo, conv = mixer_in(
        own_len, x_own, x_halo, small_all, w_b, w_u
    )
    c_own, gated, middle, n_two = mixer_out(x_own, n_one, conv, small_all, w_c, w_o)

    ffn_d = plane_corner(ffn_x, ffn_y, "ffn", dy_far)
    n_two_far, n_two_near = z_send(n_two, "n2", (2, 1))
    n_two_set = [n_two, n_two_near, n_two_far]
    ffn_pairs += [ffn_d, dp_swap(after(ffn_d, n_two), 1, "ffn")]
    w_ffn = place_ffn(index, ffn_pairs)
    d_ffn_set = [d_ffn] + dy_set
    d_parts, out_parts, kept = [], [], ()
    for s in range(n_z):
        d_part, out_part, *kept = ffn_piece(s, n_z, n_two_set[s], d_ffn_set[s], w_ffn, kept)
        d_parts.append(d_part)
        out_parts.append(out_part)
        if s == 0:
            n_two_set.append(z_swap(after(n_two_far, d_part), 1, "n2_on"))
    d_on = z_swap(d_parts[3], 1, "dn_on")
    away, home = ffn_grads(index, 0, 4, *kept)
    d_on = after(d_on, away).astype(F32) + d_parts[2].astype(F32)
    d_near = z_swap(after(d_parts[1], n_two_set[3]), 1, "dn")
    d_parts = [d_parts[0], d_near, z_swap(d_on.astype(BF), 2, "dn")]

    ffn_pieces = core_sum(away, home, 4, "gf")
    ffn_across = plane_far(ffn_pieces, "gf")
    out_on = z_swap(after(out_parts[3], d_near), 1, "out_on")
    out_first = z_swap(after(out_parts[1], d_near), 1, "out")
    d_mix, d_b, d_u, d_c, d_b_halo, d_u_halo, grad_mid, d_x_halo, small_grads = mixer_back(
        own_len,
        d_parts,
        (middle, d_ffn, x_own, x_halo, small_all, b_own, u_own, c_own, b_halo, u_halo, mixed, mixed_halo, conv),
        (w_b, w_u, w_c, w_o),
    )

    co_away, co_home = mixer_grads(index, (after(n_one, ffn_pieces[3]), d_c, d_mix, gated), block, False)
    d_bu_halo = jnp.concatenate([d_b_halo, d_u_halo], axis=1)
    spread = mm_tn(picks, d_x_halo).astype(BF)
    bu_away, bu_home = mixer_grads(
        index, (after(n_one, co_away), d_b, n_one, d_u, n_halo, d_bu_halo, small_grads, spread), block, True
    )
    co_pieces = core_sum(after(co_away, out_on), co_home, 4, "gco")
    out_second = (out_parts[2].astype(F32) + out_on.astype(F32)).astype(BF)
    out_second = z_swap(out_second, 2, "out")
    co_across = plane_far(co_pieces, "gco")
    co_terms = plane_near(co_pieces, co_across, "gco")
    bu_pieces = core_sum(bu_away, bu_home, 4, "gbu")
    bu_across = plane_far(bu_pieces, "gbu")
    bu_terms = plane_near(bu_pieces, bu_across, "gbu")
    ffn_terms = plane_near(ffn_pieces, ffn_across, "gf", bu_across)
    layer_out = middle + out_parts[0].astype(F32) + out_first.astype(F32) + out_second.astype(F32)
    layer_out = layer_out.astype(BF).reshape(row_count, own_len, width)

    def z_parts(terms, tag, *waits):
        first = after(terms[0], *waits) if waits else terms[0]
        parts = split_z(index, (first, *terms[1:]), 2 * block, n_z)
        return [parts[0]] + [z_swap(parts[s], s, tag) for s in range(1, n_z)]

    co_parts = z_parts(co_terms, "gco", out_second)
    ffn_total = sum(term.astype(F32) for term in ffn_terms)
    if outer > 1:
        narrow = functools.partial(
            lax.psum_scatter, axis_name="dp", tiled=True, axis_index_groups=groups
        )
        ffn_total = narrow(ffn_total, scatter_dimension=0)
    grad_w_gu = jnp.stack([ffn_total[:, :units], ffn_total[:, units : 2 * units]], axis=1)
    grad_w_down = ffn_total[:, 2 * units :].T
    bu_parts = z_parts(bu_terms, "gbu", co_parts[0])
    if outer > 1:
        bu_total = sum(part.astype(F32) for part in bu_parts)
        grad_co = sum(part.astype(F32) for part in co_parts).reshape(2, block, channels)
        grad_co = narrow(grad_co, scatter_dimension=1)
        grad_bu = narrow(bu_total[: 2 * block].reshape(2, block, channels), scatter_dimension=1)
        grad_small = narrow(bu_total[2 * block : 2 * block + n_small, :block], scatter_dimension=1)
        returned = bu_total[2 * block + 16 :].reshape(n_z, -1, channels)
        returned = narrow(jnp.moveaxis(returned, 0, 1).reshape(-1, width), scatter_dimension=0)
        grad_w_in = jnp.stack([grad_bu[0], grad_co[0], grad_bu[1]])
        grad_w_out = grad_co[1].T
        grad_in = grad_mid.reshape(row_count, own_len, width)
        grad_in = grad_in + jnp.pad(
            returned.reshape(row_count, reach, width), ((0, 0), (own_len - reach, 0), (0, 0))
        )
        grad_in = grad_in.astype(BF)
    else:
        grad_c, grad_w_out = finish_co(co_parts)
        grad_w_in, grad_small, grad_in = finish_bu(bu_parts, grad_c, grad_mid, own_len, reach)
        grad_in = grad_in.reshape(row_count, own_len, width)
    return (
        layer_out,
        grad_in,
        grad_small[0],
        jnp.swapaxes(grad_w_in, 0, 1),
        grad_small[2:n_small],
        grad_w_out,
        grad_small[1],
        grad_w_gu,
        grad_w_down,
    )


def solution(mesh):
    in_specs = (
        P("dp", "tensor", None),
        P("dp", "tensor", None),
        P(),
        P(),
        P(),
        P("dp"),
        P("dp", None, "tensor"),
        P(None, "dp"),
        P("tensor", "dp"),
        P("dp"),
        P("dp", None, "tensor"),
        P("tensor", "dp"),
    )
    out_specs = (
        P("dp", "tensor", None),
        P("dp", "tensor", None),
        P("dp"),
        P("dp", None, "tensor"),
        P(None, "dp"),
        P("tensor", "dp"),
        P("dp"),
        P("dp", None, "tensor"),
        P("tensor", "dp"),
    )
    return jax.shard_map(body, mesh=mesh, in_specs=in_specs, out_specs=out_specs, check_vma=False)
```
